256 devices in a mesh: pb: 4 (over y), neg: 64 (over z, x, core).
Axes of the slice: x: 4, y: 4, z: 8, core: 2. Of those that a mesh axis runs over, the one named last changes fastest.
Arguments:
- hidden: bfloat16 [4, 256, 128, 1024], P('pb', 'neg'), may hold values from -6 to 6
- lengths: int32 [4, 256], P('pb', 'neg'), may hold values from 32 to 128
- teacher: float32 [4, 256], P('pb', 'neg'), may hold values from -8 to 8
- norm_gain: float32 [1024], replicated, may hold values from 0.1 to 1.9
- final_gain: float32 [1024], replicated, may hold values from 0.1 to 1.9
- score_vector: float32 [1024], replicated, may hold values from -0.1875 to 0.1875
- query_weight: bfloat16 [1024, 1024], P(('pb', 'neg')), may hold values from -0.1875 to 0.1875
- key_matrix: bfloat16 [1024, 512], P(('pb', 'neg')), may hold values from -0.1875 to 0.1875
- value_matrix: bfloat16 [1024, 512], P(('pb', 'neg')), may hold values from -0.1875 to 0.1875
- out_weight: bfloat16 [1024, 1024], P(None, ('pb', 'neg')), may hold values from -0.1875 to 0.1875
Outputs:
- scores: float32 [4, 256], P('pb', 'neg')
- loss: float32 [], replicated
- grad_hidden: bfloat16 [4, 256, 128, 1024], P('pb', 'neg')
- grad_query: float32 [1024, 1024], P(('pb', 'neg'))
- grad_key: float32 [1024, 512], P(('pb', 'neg'))
- grad_value: float32 [1024, 512], P(('pb', 'neg'))
- grad_out: float32 [1024, 1024], P(None, ('pb', 'neg'))
The draws below stay inside these ranges and needn't reach their ends.
Inputs may be any that keep to these rules, and one draw needn't show every extreme that they name: `lengths`: the number of real tokens of the pair; its other positions out of 128 are padding.
All inputs are finite; a program needn't handle non-finite values.
Results may differ from the reference program's by a relative error of at most 0.013.
Values may be sent and summed in bfloat16 or wider, within the bound.
No kernel may reach another device: no remote copies, remote signals or barrier semaphores. Data moves between devices by JAX's collectives and lax.ppermute only.
A program may use at most 64 MiB of HBM per device.

```python
import jax
import jax.numpy as jnp
from jax import lax

HIDDEN_WIDTH = 1024
HQ = 8
KEY_VALUE_HEADS = 4
HEAD_WIDTH = 128
SEQ = 128
PAIR_DEV = 4
QUERIES = 4
LIST = 256


def place_ends(array, key, smallest, largest):
    shape = array.shape
    index_at = [jax.random.randint(jax.random.fold_in(key, axis), (), 0, shape[axis]) for axis in range(len(shape))]
    array = array.at[tuple(index_at)].set(smallest)
    longest = shape.index(max(shape))
    index_at[longest] = (index_at[longest] + 1) % shape[longest]
    return array.at[tuple(index_at)].set(largest)


def levels(own_key, extent, cuts, least, high):
    loudness = 1.0
    for position, shards_of in cuts:
        heights = jax.random.uniform(jax.random.fold_in(jax.random.fold_in(own_key, 6), position), (shards_of,), jnp.float32, least / len(cuts), high / len(cuts))
        loudness = loudness * jnp.repeat(jnp.exp(heights), extent[position] // shards_of).reshape((-1,) + (1,) * (len(extent) - 1 - position))
    return loudness


def bell_draw(rng, dims, scale, bound, split=(), kind=jnp.bfloat16):
    array = jax.random.normal(rng, dims, jnp.float32) * scale
    if len(split) > 0:
        array = levels(rng, dims, split, -0.22, 0.18) * array
    return jnp.clip(array, min=-bound, max=bound).astype(kind)


def setup_inputs(seed: int = 0) -> dict:
    keys = jax.random.split(jax.random.key(seed), 11)
    hidden = bell_draw(keys[0], (QUERIES, LIST, SEQ, HIDDEN_WIDTH), 1.0, 6.0, ((0, 4), (1, 64)))
    lengths = place_ends(jax.random.randint(keys[1], (QUERIES, LIST), SEQ // 4, SEQ + 1), jax.random.fold_in(keys[1], 1), SEQ // 4, SEQ).astype(jnp.int32)
    teacher = bell_draw(keys[2], (QUERIES, LIST), 2.0, 8.0, ((0, 4), (1, 64)), jnp.float32)
    norm_gain = jnp.clip(1.0 + 0.18 * jax.random.normal(keys[3], (HIDDEN_WIDTH,), jnp.float32), 0.1, 1.9)
    final_gain = jnp.clip(1.0 + 0.18 * jax.random.normal(keys[4], (HIDDEN_WIDTH,), jnp.float32), 0.1, 1.9)
    score_vector = bell_draw(keys[5], (HIDDEN_WIDTH,), HIDDEN_WIDTH ** -0.5, 0.1875, (), jnp.float32)
    query_weight = bell_draw(keys[6], (HIDDEN_WIDTH, HQ * HEAD_WIDTH), HIDDEN_WIDTH ** -0.5, 0.1875, ((0, 256),))
    key_matrix = bell_draw(keys[7], (HIDDEN_WIDTH, KEY_VALUE_HEADS * HEAD_WIDTH), HIDDEN_WIDTH ** -0.5, 0.1875, ((0, 256),))
    value_matrix = bell_draw(keys[8], (HIDDEN_WIDTH, KEY_VALUE_HEADS * HEAD_WIDTH), HIDDEN_WIDTH ** -0.5, 0.1875, ((0, 256),))
    out_weight = bell_draw(keys[9], (HQ * HEAD_WIDTH, HIDDEN_WIDTH), (HQ * HEAD_WIDTH) ** -0.5, 0.1875, ((1, 256),))
    return dict(hidden=hidden, lengths=lengths, teacher=teacher, norm_gain=norm_gain, final_gain=final_gain, score_vector=score_vector, query_weight=query_weight, key_matrix=key_matrix, value_matrix=value_matrix, out_weight=out_weight)


EPSILON = 1e-06
ROPE_BASE = 1000000.0
TEACHER_TEMP = 2.0
GRAD_SCALE = 512.0

def rope_tables(seq_len, head_size):
    half = head_size // 2
    freqs = ROPE_BASE ** (-(jnp.arange(half, dtype=jnp.float32) * 2.0) / head_size)
    angles = jnp.arange(seq_len, dtype=jnp.float32)[:, None] * freqs[None, :]
    angles = jnp.concatenate([angles, angles], axis=1)
    return (jnp.cos(angles), jnp.sin(angles))

def rotate_half(vector):
    half = vector.shape[-1] // 2
    return jnp.concatenate([-vector[..., half:], vector[..., :half]], axis=-1)

def unrotate_half(vector):
    half = vector.shape[-1] // 2
    return jnp.concatenate([vector[..., half:], -vector[..., :half]], axis=-1)

def forward_pairs(tokens_in, lengths_here, norm_gain, final_gain, score_vector, query_weight, key_matrix, value_matrix, out_weight):
    pair_count, seq_len, model_width = tokens_in.shape
    head_count = query_weight.shape[1] // HEAD_WIDTH
    group_count = key_matrix.shape[1] // HEAD_WIDTH
    group_size = head_count // group_count
    inputs_wide = tokens_in.astype(jnp.float32)
    inv_rms = lax.rsqrt(lax.optimization_barrier(jnp.mean(inputs_wide * inputs_wide, axis=-1, keepdims=True)) + EPSILON)
    normed = (inputs_wide * inv_rms * norm_gain).astype(jnp.bfloat16)
    flat_rows = normed.reshape(pair_count * seq_len, model_width)
    key_proj = jnp.dot(flat_rows, key_matrix, preferred_element_type=jnp.float32).reshape(pair_count, seq_len, group_count, HEAD_WIDTH)
    value_proj = jnp.dot(flat_rows, value_matrix, preferred_element_type=jnp.float32).reshape(pair_count, seq_len, group_count, HEAD_WIDTH)
    positions = jnp.arange(seq_len, dtype=jnp.int32)
    last_index = (lengths_here - 1).astype(jnp.int32)
    onehot = (positions[None, :] == last_index[:, None]).astype(jnp.float32)
    normed_last = jnp.take_along_axis(normed, last_index[:, None, None], axis=1)[:, 0]
    query_proj = jnp.dot(normed_last, query_weight, preferred_element_type=jnp.float32).reshape(pair_count, head_count, HEAD_WIDTH)
    query_scale = lax.rsqrt(lax.optimization_barrier(jnp.mean(query_proj * query_proj, axis=-1, keepdims=True)) + EPSILON)
    query_unit = query_proj * query_scale
    key_scale = lax.rsqrt(lax.optimization_barrier(jnp.mean(key_proj * key_proj, axis=-1, keepdims=True)) + EPSILON)
    key_unit = key_proj * key_scale
    cos_table, sin_table = rope_tables(seq_len, HEAD_WIDTH)
    cos_query = jnp.dot(onehot, cos_table, precision=lax.Precision.HIGHEST)
    sin_query = jnp.dot(onehot, sin_table, precision=lax.Precision.HIGHEST)
    query_rot = (query_unit * cos_query[:, None, :] + rotate_half(query_unit) * sin_query[:, None, :]).astype(jnp.bfloat16)
    key_rot = (key_unit * cos_table[None, :, None, :] + rotate_half(key_unit) * sin_table[None, :, None, :]).astype(jnp.bfloat16)
    value_cast = value_proj.astype(jnp.bfloat16)
    grouped = query_rot.reshape(pair_count, group_count, group_size, HEAD_WIDTH)
    logits = jnp.einsum('pkgd,pskd->pkgs', grouped.astype(jnp.float32), key_rot.astype(jnp.float32)) * HEAD_WIDTH ** (-0.5)
    visible = (positions[None, :] <= last_index[:, None])[:, None, None, :]
    expos = jnp.where(visible, jnp.exp(logits), 0.0)
    attention_weights = expos / lax.optimization_barrier(jnp.sum(expos, axis=-1, keepdims=True))
    probs_cast = attention_weights.astype(jnp.bfloat16)
    context = jnp.einsum('pkgs,pskd->pkgd', probs_cast.astype(jnp.float32), value_cast.astype(jnp.float32))
    context = context.astype(jnp.bfloat16).reshape(pair_count, head_count * HEAD_WIDTH)
    attended = jnp.dot(context, out_weight, preferred_element_type=jnp.float32)
    residual = jnp.take_along_axis(inputs_wide, last_index[:, None, None], axis=1)[:, 0] + attended
    out_scale = lax.rsqrt(lax.optimization_barrier(jnp.mean(residual * residual, axis=-1, keepdims=True)) + EPSILON)
    out_unit = residual * out_scale
    scores_here = lax.optimization_barrier(jnp.sum(out_unit * final_gain * score_vector, axis=-1))
    stored = (tokens_in, onehot, inv_rms, normed, normed_last, query_unit, query_scale, key_unit, key_scale, cos_query, sin_query, cos_table, sin_table, query_rot, key_rot, value_cast, attention_weights, probs_cast, context, out_unit, out_scale)
    return (scores_here, stored)

def backward_pairs(stored, grad_score, norm_gain, final_gain, score_vector, query_weight, key_matrix, value_matrix, out_weight):
    tokens_in, onehot, inv_rms, normed, normed_last, query_unit, query_scale, key_unit, key_scale, cos_query, sin_query, cos_table, sin_table, query_rot, key_rot, value_cast, attention_weights, probs_cast, context, out_unit, out_scale = stored
    pair_count, seq_len, model_width = tokens_in.shape
    head_count = query_weight.shape[1] // HEAD_WIDTH
    group_count = key_matrix.shape[1] // HEAD_WIDTH
    group_size = head_count // group_count
    grad_unit = grad_score[:, None] * score_vector * final_gain
    grad_resid = out_scale * (grad_unit - out_unit * lax.optimization_barrier(jnp.mean(grad_unit * out_unit, axis=-1, keepdims=True)))
    grad_resid_cast = grad_resid.astype(jnp.bfloat16)
    grad_out = jnp.dot(context.T, grad_resid_cast, preferred_element_type=jnp.float32)
    grad_context = jnp.dot(grad_resid_cast, out_weight.T, preferred_element_type=jnp.float32).astype(jnp.bfloat16)
    grad_context = grad_context.reshape(pair_count, group_count, group_size, HEAD_WIDTH).astype(jnp.float32)
    grad_probs = jnp.einsum('pkgd,pskd->pkgs', grad_context, value_cast.astype(jnp.float32))
    grad_vals = jnp.einsum('pkgs,pkgd->pskd', probs_cast.astype(jnp.float32), grad_context)
    spread = lax.optimization_barrier(jnp.sum(attention_weights * grad_probs, axis=-1, keepdims=True))
    logit_gradient = (attention_weights * (grad_probs - spread)).astype(jnp.bfloat16).astype(jnp.float32)
    grouped = query_rot.reshape(pair_count, group_count, group_size, HEAD_WIDTH).astype(jnp.float32)
    rotated_query_gradient = jnp.einsum('pkgs,pskd->pkgd', logit_gradient, key_rot.astype(jnp.float32)) * HEAD_WIDTH ** (-0.5)
    rotated_query_gradient = rotated_query_gradient.reshape(pair_count, head_count, HEAD_WIDTH)
    grad_krot = jnp.einsum('pkgs,pkgd->pskd', logit_gradient, grouped) * HEAD_WIDTH ** (-0.5)
    grad_qunit = rotated_query_gradient * cos_query[:, None, :] + unrotate_half(rotated_query_gradient * sin_query[:, None, :])
    grad_kunit = grad_krot * cos_table[None, :, None, :] + unrotate_half(grad_krot * sin_table[None, :, None, :])
    grad_qproj = query_scale * (grad_qunit - query_unit * lax.optimization_barrier(jnp.mean(grad_qunit * query_unit, axis=-1, keepdims=True)))
    grad_kproj = key_scale * (grad_kunit - key_unit * lax.optimization_barrier(jnp.mean(grad_kunit * key_unit, axis=-1, keepdims=True)))
    grad_q_cast = grad_qproj.reshape(pair_count, head_count * HEAD_WIDTH).astype(jnp.bfloat16)
    grad_k_cast = grad_kproj.reshape(pair_count * seq_len, group_count * HEAD_WIDTH).astype(jnp.bfloat16)
    grad_v_cast = grad_vals.reshape(pair_count * seq_len, group_count * HEAD_WIDTH).astype(jnp.bfloat16)
    flat_rows = normed.reshape(pair_count * seq_len, model_width)
    grad_query = jnp.dot(normed_last.T, grad_q_cast, preferred_element_type=jnp.float32)
    grad_key = jnp.dot(flat_rows.T, grad_k_cast, preferred_element_type=jnp.float32)
    grad_value = jnp.dot(flat_rows.T, grad_v_cast, preferred_element_type=jnp.float32)
    grad_normed = jnp.dot(grad_k_cast, key_matrix.T, preferred_element_type=jnp.float32)
    grad_normed = grad_normed + jnp.dot(grad_v_cast, value_matrix.T, preferred_element_type=jnp.float32)
    grad_normed = grad_normed.reshape(pair_count, seq_len, model_width)
    grad_last = jnp.dot(grad_q_cast, query_weight.T, preferred_element_type=jnp.float32)
    grad_normed = grad_normed + onehot[:, :, None] * grad_last[:, None, :]
    inputs_wide = tokens_in.astype(jnp.float32)
    grad_scaled = grad_normed * norm_gain
    grad_input = inv_rms * grad_scaled - inputs_wide * inv_rms * inv_rms * inv_rms * lax.optimization_barrier(jnp.mean(grad_scaled * inputs_wide, axis=-1, keepdims=True))
    grad_input = grad_input + onehot[:, :, None] * grad_resid[:, None, :]
    return (grad_input.astype(jnp.bfloat16), (grad_query, grad_key, grad_value, grad_out))

def reference(hidden, lengths, teacher, norm_gain, final_gain, score_vector, query_weight, key_matrix, value_matrix, out_weight):
    query_count, list_len, seq_len, model_width = hidden.shape
    block_count = list_len // PAIR_DEV
    weights = (query_weight, key_matrix, value_matrix, out_weight)

    def score_block(carry, item):
        block_tokens, block_lengths = item
        block_scores, stored = forward_pairs(block_tokens, block_lengths, norm_gain, final_gain, score_vector, weights[0], weights[1], weights[2], weights[3])
        return (carry, block_scores)
    score_rows = []
    for query_pos in range(query_count):
        blocks_in = hidden[query_pos].reshape(block_count, PAIR_DEV, seq_len, model_width)
        blocks_len = lengths[query_pos].reshape(block_count, PAIR_DEV)
        carry_out, block_scores = lax.scan(score_block, jnp.zeros((), jnp.float32), (blocks_in, blocks_len))
        score_rows.append(block_scores.reshape(list_len))
    scores = jnp.stack(score_rows, axis=0)
    scaled = teacher / TEACHER_TEMP
    expo_s = jnp.exp(scores)
    expo_t = jnp.exp(scaled)
    total_s = lax.optimization_barrier(jnp.sum(expo_s, axis=-1, keepdims=True))
    total_t = lax.optimization_barrier(jnp.sum(expo_t, axis=-1, keepdims=True))
    prob_s = expo_s / total_s
    prob_t = expo_t / total_t
    loss = jnp.sum(prob_t * (scaled - jnp.log(total_t) - (scores - jnp.log(total_s))))
    grad_score = GRAD_SCALE * (prob_s - prob_t)

    def grad_block(carry, item):
        block_tokens, block_lengths, block_grad = item
        block_scores, stored = forward_pairs(block_tokens, block_lengths, norm_gain, final_gain, score_vector, weights[0], weights[1], weights[2], weights[3])
        grad_input, grads = backward_pairs(stored, block_grad, norm_gain, final_gain, score_vector, weights[0], weights[1], weights[2], weights[3])
        summed = (carry[0] + grads[0], carry[1] + grads[1], carry[2] + grads[2], carry[3] + grads[3])
        return (summed, grad_input)
    total_blocks = query_count * block_count
    start = (jnp.zeros(query_weight.shape, jnp.float32), jnp.zeros(key_matrix.shape, jnp.float32), jnp.zeros(value_matrix.shape, jnp.float32), jnp.zeros(out_weight.shape, jnp.float32))
    items = (hidden.reshape(total_blocks, PAIR_DEV, seq_len, model_width), lengths.reshape(total_blocks, PAIR_DEV), grad_score.reshape(total_blocks, PAIR_DEV))
    grads, grad_blocks = lax.scan(grad_block, start, items)
    grad_hidden = grad_blocks.reshape(query_count, list_len, seq_len, model_width)
    return (scores, loss, grad_hidden, grads[0], grads[1], grads[2], grads[3])
```

```python
import jax
import jax.numpy as jnp
import numpy as np
from jax import lax
from jax.experimental import pallas as pl
from jax.experimental.pallas import tpu as pltpu
from jax.sharding import Mesh
from jax.sharding import PartitionSpec as P

HW = 128
AXES = ("pb", "z", "x", "c")
NEG = ("z", "x", "c")
EPS = 1e-06
ROPE_BASE = 1000000.0
GRAD_SCALE = 512.0
PAIRS = 4
SEQ = 128
D = 1024
ROWS = PAIRS * SEQ
F32 = jnp.float32
BF16 = jnp.bfloat16
VM = pl.BlockSpec(memory_space=pltpu.VMEM)
SM = pl.BlockSpec(memory_space=pltpu.SMEM)
LAST = (((1,), (1,)), ((), ()))
FIRST = (((0,), (0,)), ((), ()))
SCALE = HW ** (-0.5)


def rope_consts():
    freqs = np.float32(ROPE_BASE) ** (-(np.arange(HW // 2, dtype=np.float32) * 2.0) / HW)
    angles = np.arange(SEQ, dtype=np.float32)[:, None] * freqs.astype(np.float32)[None, :]
    angles = np.concatenate([angles, angles], axis=1)
    sign = np.where(np.arange(HW) < HW // 2, -1.0, 1.0)
    return (
        np.cos(angles).astype(np.float32),
        (np.sin(angles) * sign[None, :]).astype(np.float32),
    )


def call(body, outs, in_specs, vmem=48, flops=0, nbytes=0):
    return pl.pallas_call(
        body,
        out_shape=[jax.ShapeDtypeStruct(s, d) for s, d in outs],
        in_specs=in_specs,
        out_specs=[VM] * len(outs),
        compiler_params=pltpu.CompilerParams(vmem_limit_bytes=vmem << 20),
        cost_estimate=pl.CostEstimate(flops=flops, bytes_accessed=nbytes, transcendentals=0),
    )


def dot(a, b, dims=(((1,), (0,)), ((), ()))):
    return lax.dot_general(a, b, dims, preferred_element_type=F32)


def half_turn(v):
    return pltpu.roll(v, HW // 2, 1)


def heads(v, n):
    return [v[:, i * HW : (i + 1) * HW] for i in range(n)]


def block_mask():
    row = lax.broadcasted_iota(jnp.int32, (8, 512), 0)
    lane = lax.broadcasted_iota(jnp.int32, (8, 512), 1)
    return (lane // HW) == (row // 2), (row % 2) == 0


def to_blocks(row, mask, even):
    h = heads(row, 8)
    e = jnp.broadcast_to(jnp.concatenate(h[0::2], axis=1), (8, 512))
    o = jnp.broadcast_to(jnp.concatenate(h[1::2], axis=1), (8, 512))
    return jnp.where(mask, jnp.where(even, e, o), 0.0)


def from_blocks(blocks, mask, even):
    e = jnp.sum(jnp.where(mask & even, blocks, 0.0), axis=0, keepdims=True)
    o = jnp.sum(jnp.where(mask & (~even), blocks, 0.0), axis=0, keepdims=True)
    parts = []
    for g in range(4):
        parts += [e[:, g * HW : (g + 1) * HW], o[:, g * HW : (g + 1) * HW]]
    return jnp.concatenate(parts, axis=1)


def prep_body(len_ref, h_ref, gain_ref, normed_ref, turned_ref, nlast_ref, xlast_ref):
    row = lax.broadcasted_iota(jnp.int32, (8, SEQ), 0)
    lane = lax.broadcasted_iota(jnp.int32, (8, SEQ), 1)
    nl = jnp.zeros((8, D), F32)
    xl = jnp.zeros((8, D), F32)
    for p in range(PAIRS):
        raw = h_ref[p * SEQ : (p + 1) * SEQ, :]
        x = raw.astype(F32)
        inv = lax.rsqrt(jnp.mean(x * x, axis=-1, keepdims=True) + EPS)
        n = (x * inv * gain_ref[...]).astype(BF16)
        normed_ref[p * SEQ : (p + 1) * SEQ, :] = n
        turned_ref[:, p * SEQ : (p + 1) * SEQ] = n.T
        e = len_ref[p] - 1
        hot = jnp.where((row == p) & (lane == e), 1.0, 0.0).astype(BF16)
        nl = nl + dot(hot, n)
        xl = xl + dot(hot, raw)
    nlast_ref[...] = nl.astype(BF16)
    xlast_ref[...] = xl


def attend_body(
    len_ref,
    normed_ref,
    nlast_ref,
    wa_ref,
    wb_ref,
    cos_ref,
    sin_ref,
    kproj_ref,
    krot_ref,
    vcast_ref,
    qproj_ref,
    qrot_ref,
    attn_ref,
    ctx_ref,
    qr_scr,
    ctx_scr,
):
    mask, even = block_mask()
    lane = lax.broadcasted_iota(jnp.int32, (8, SEQ), 1)
    for half, w_ref in enumerate((wa_ref, wb_ref)):
        kv = dot(normed_ref[...], w_ref[:, 0:512])
        kproj_ref[:, half * 256 : half * 256 + 256] = kv[:, 0:256]
        vcast_ref[:, half * 256 : half * 256 + 256] = kv[:, 256:512].astype(BF16)
        qproj_ref[:, half * 512 : half * 512 + 512] = dot(nlast_ref[...], w_ref[:, 512:1024])
    cos_q = jnp.concatenate(
        [cos_ref[pl.ds(len_ref[p] - 1, 1), :] for p in range(PAIRS)] * 2, axis=0
    )
    sin_q = jnp.concatenate(
        [sin_ref[pl.ds(len_ref[p] - 1, 1), :] for p in range(PAIRS)] * 2, axis=0
    )
    for h in range(8):
        q = qproj_ref[:, h * HW : (h + 1) * HW]
        u = q * lax.rsqrt(jnp.mean(q * q, axis=-1, keepdims=True) + EPS)
        r = u * cos_q + half_turn(u) * sin_q
        qr_scr[:, h * HW : (h + 1) * HW] = r
        qrot_ref[:, h * HW : (h + 1) * HW] = r.astype(BF16)
    ctx_scr[...] = jnp.zeros((8, D), F32)
    for p in range(PAIRS):
        rows = slice(p * SEQ, (p + 1) * SEQ)
        for g in range(4):
            k = kproj_ref[rows, g * HW : (g + 1) * HW]
            u = k * lax.rsqrt(jnp.mean(k * k, axis=-1, keepdims=True) + EPS)
            r = u * cos_ref[...] + half_turn(u) * sin_ref[...]
            krot_ref[rows, g * HW : (g + 1) * HW] = r.astype(BF16)
        qb = to_blocks(qr_scr[p : p + 1, :], mask, even).astype(BF16)
        logits = dot(qb, krot_ref[rows, :], LAST) * SCALE
        ex = jnp.where(lane <= len_ref[p] - 1, jnp.exp(logits), 0.0)
        w = ex / jnp.sum(ex, axis=-1, keepdims=True)
        attn_ref[p * 8 : (p + 1) * 8, :] = w
        c = dot(w.astype(BF16), vcast_ref[rows, :])
        ctx_scr[p : p + 1, :] = from_blocks(c, mask, even)
    ctx_ref[...] = ctx_scr[...].astype(BF16)


def score_body(
    teach_ref, ctx_ref, xlast_ref, oa_ref, ob_ref, fg_ref, sv_ref, unit_ref, oscale_ref, score_ref, tot_ref
):
    res = xlast_ref[...] + (
        dot(ctx_ref[:, 0:512], oa_ref[...], LAST) + dot(ctx_ref[:, 512:1024], ob_ref[...], LAST)
    )
    sc = lax.rsqrt(jnp.mean(res * res, axis=-1, keepdims=True) + EPS)
    unit = res * sc
    unit_ref[...] = unit
    oscale_ref[...] = jnp.broadcast_to(sc, (8, HW))
    s = jnp.sum(unit * fg_ref[...] * sv_ref[...], axis=-1, keepdims=True)
    s = jnp.broadcast_to(s, (8, HW))
    score_ref[...] = s
    row = lax.broadcasted_iota(jnp.int32, (8, HW), 0)
    lane = lax.broadcasted_iota(jnp.int32, (8, HW), 1)
    scaled = teach_ref[...] / 2.0
    es = jnp.exp(s)
    et = jnp.exp(scaled)
    v = jnp.where(lane == 0, es, jnp.where(lane == 1, et, et * (scaled - s)))
    v = jnp.where((row < PAIRS) & (lane < 3), v, 0.0)
    tot_ref[...] = jnp.broadcast_to(jnp.sum(v, axis=0, keepdims=True), (8, HW))


def unit_back_body(
    len_ref,
    krot_ref,
    vcast_ref,
    kproj_ref,
    qproj_ref,
    qrot_ref,
    attn_ref,
    unit_ref,
    oscale_ref,
    oa_ref,
    ob_ref,
    fg_ref,
    sv_ref,
    cos_ref,
    sin_ref,
    gkva_ref,
    gkvb_ref,
    gq_ref,
    gr_ref,
    gc_scr,
    gq_scr,
    qr_scr,
):
    mask, even = block_mask()
    unit = unit_ref[...]
    gu = sv_ref[...] * fg_ref[...]
    gr = oscale_ref[:, 0:1] * (gu - unit * jnp.mean(gu * unit, axis=-1, keepdims=True))
    gr_ref[...] = gr
    grb = gr.astype(BF16)
    gc_scr[:, 0:512] = dot(grb, oa_ref[...])
    gc_scr[:, 512:1024] = dot(grb, ob_ref[...])
    qr_scr[...] = qrot_ref[...].astype(F32)
    gq_scr[...] = jnp.zeros((8, D), F32)
    for p in range(PAIRS):
        rows = slice(p * SEQ, (p + 1) * SEQ)
        gb = to_blocks(gc_scr[p : p + 1, :], mask, even).astype(BF16)
        qb = to_blocks(qr_scr[p : p + 1, :], mask, even).astype(BF16)
        w = attn_ref[p * 8 : (p + 1) * 8, :]
        gp = dot(gb, vcast_ref[rows, :], LAST)
        gv = dot(w.astype(BF16), gb, FIRST)
        gkva_ref[rows, 256:512] = gv[:, 0:256]
        gkvb_ref[rows, 256:512] = gv[:, 256:512]
        spread = jnp.sum(w * gp, axis=-1, keepdims=True)
        dl = (w * (gp - spread)).astype(BF16)
        gq_scr[p : p + 1, :] = from_blocks(dot(dl, krot_ref[rows, :]) * SCALE, mask, even)
        gk = dot(dl, qb, FIRST) * SCALE
        for g in range(4):
            k = kproj_ref[rows, g * HW : (g + 1) * HW]
            sc = lax.rsqrt(jnp.mean(k * k, axis=-1, keepdims=True) + EPS)
            u = k * sc
            r = gk[:, g * HW : (g + 1) * HW]
            t = r * cos_ref[...] + half_turn(r * sin_ref[...])
            out = sc * (t - u * jnp.mean(t * u, axis=-1, keepdims=True))
            ref = gkva_ref if g < 2 else gkvb_ref
            ref[rows, (g % 2) * HW : (g % 2 + 1) * HW] = out
    cos_q = jnp.concatenate(
        [cos_ref[pl.ds(len_ref[p] - 1, 1), :] for p in range(PAIRS)] * 2, axis=0
    )
    sin_q = jnp.concatenate(
        [sin_ref[pl.ds(len_ref[p] - 1, 1), :] for p in range(PAIRS)] * 2, axis=0
    )
    for h in range(8):
        q = qproj_ref[:, h * HW : (h + 1) * HW]
        sc = lax.rsqrt(jnp.mean(q * q, axis=-1, keepdims=True) + EPS)
        u = q * sc
        r = gq_scr[:, h * HW : (h + 1) * HW]
        t = r * cos_q + half_turn(r * sin_q)
        gq_ref[:, h * HW : (h + 1) * HW] = sc * (
            t - u * jnp.mean(t * u, axis=-1, keepdims=True)
        )


def weight_body(
    pb_ref,
    tot_ref,
    score_ref,
    teach_ref,
    gkva_ref,
    gkvb_ref,
    gq_ref,
    gr_ref,
    turned_ref,
    nlast_ref,
    ctx_ref,
    loss_ref,
    grad_a_ref,
    grad_b_ref,
    skva_ref,
    skvb_ref,
    sq_ref,
    sr_ref,
):
    pb = pb_ref[0]
    lane = lax.broadcasted_iota(jnp.int32, (1, HW), 1)

    def pick(v, i):
        return jnp.sum(jnp.where(lane == i, v, 0.0), axis=-1, keepdims=True)

    loss = jnp.zeros((1, 1), F32)
    mine = jnp.zeros((1, HW), F32)
    for q in range(4):
        t = jnp.sum(tot_ref[q * 64 : (q + 1) * 64, :], axis=0, keepdims=True)
        ts, tt, cr = pick(t, 0), pick(t, 1), pick(t, 2)
        loss = loss + (cr / tt - jnp.log(tt) + jnp.log(ts))
        mine = mine + jnp.where(pb == q, t, 0.0)
    loss_ref[...] = jnp.broadcast_to(loss, (8, HW))
    ts, tt = pick(mine, 0), pick(mine, 1)
    row = lax.broadcasted_iota(jnp.int32, (8, HW), 0)
    g = GRAD_SCALE * (jnp.exp(score_ref[...]) / ts - jnp.exp(teach_ref[...] / 2.0) / tt)
    g = jnp.where(row < PAIRS, g, 0.0)
    gcol = g[:, 0:1]
    sr = gr_ref[...] * gcol
    sr_ref[...] = sr
    sq = (gq_ref[...] * gcol).astype(BF16)
    sq_ref[...] = sq
    srb = sr.astype(BF16)
    for gkv_ref, s_ref in ((gkva_ref, skva_ref), (gkvb_ref, skvb_ref)):
        for p in range(PAIRS):
            rows = slice(p * SEQ, (p + 1) * SEQ)
            s_ref[rows, :] = (gkv_ref[rows, :] * gcol[p : p + 1, :]).astype(BF16)
    for half, out_ref, s_ref in ((1, grad_b_ref, skvb_ref), (0, grad_a_ref, skva_ref)):
        cols = slice(half * 512, half * 512 + 512)
        out_ref[:, 0:512] = dot(turned_ref[...], s_ref[...]).astype(BF16)
        out_ref[:, 512:1024] = dot(nlast_ref[...], sq[:, cols], FIRST).astype(BF16)
        out_ref[:, 1024:1536] = dot(srb, ctx_ref[:, cols], FIRST).astype(BF16)


def hidden_body(
    len_ref, h_ref, gain_ref, wa_ref, wb_ref, skva_ref, skvb_ref, sq_ref, sr_ref, out_ref, last_scr
):
    last_scr[...] = dot(sq_ref[:, 0:512], wa_ref[:, 512:1024], LAST) + dot(
        sq_ref[:, 512:1024], wb_ref[:, 512:1024], LAST
    )
    pos = lax.broadcasted_iota(jnp.int32, (SEQ, 1), 0)
    for p in range(PAIRS):
        rows = slice(p * SEQ, (p + 1) * SEQ)
        gn = dot(skva_ref[rows, :], wa_ref[:, 0:512], LAST) + dot(
            skvb_ref[rows, :], wb_ref[:, 0:512], LAST
        )
        at = pos == len_ref[p] - 1
        gn = gn + jnp.where(at, last_scr[p : p + 1, :], 0.0)
        x = h_ref[rows, :].astype(F32)
        inv = lax.rsqrt(jnp.mean(x * x, axis=-1, keepdims=True) + EPS)
        s = gn * gain_ref[...]
        gi = inv * s - x * (inv * inv * inv * jnp.mean(s * x, axis=-1, keepdims=True))
        gi = gi + jnp.where(at, sr_ref[p : p + 1, :], 0.0)
        out_ref[rows, :] = gi.astype(BF16)


def everyone(x, axes, count):
    return lax.all_to_all(
        jnp.broadcast_to(x[None], (count, *x.shape)), axes, 0, 0, tiled=True
    )


def gather_rows(x):
    width = x.shape[1]
    got = everyone(x, ("z", "x"), 32).reshape(256, width)
    return everyone(got, "pb", 4).reshape(1024, width)


def scatter_rows(x):
    width = x.shape[1]
    got = lax.all_to_all(x.reshape(4, 256, width), "pb", 0, 0, tiled=True)
    part = jnp.sum(got.astype(F32), axis=0).astype(BF16)
    got = lax.all_to_all(part.reshape(32, 8, width), ("z", "x"), 0, 0, tiled=True)
    return jnp.sum(got.astype(F32), axis=0)


def swap(x):
    return lax.ppermute(x, "c", [(0, 1), (1, 0)])


def shards(
    hidden,
    lengths,
    teacher,
    norm_gain,
    final_gain,
    score_vector,
    query_weight,
    key_matrix,
    value_matrix,
    out_weight,
):
    c = lax.axis_index("c")
    first = c == 0
    pb = lax.axis_index("pb").astype(jnp.int32)[None]
    tokens = hidden.reshape(ROWS, D)
    lens = lengths[0]
    gain = norm_gain[None]
    fg = final_gain[None]
    sv = score_vector[None]
    cos_np, sin_np = rope_consts()
    cos, sin = jnp.asarray(cos_np), jnp.asarray(sin_np)
    teach = jnp.broadcast_to(jnp.pad(teacher[0], (0, 4))[:, None], (8, HW))

    turned_out = out_weight.T
    halves = [
        jnp.concatenate(
            [
                key_matrix[:, h * 256 : h * 256 + 256],
                value_matrix[:, h * 256 : h * 256 + 256],
                query_weight[:, h * 512 : h * 512 + 512],
                turned_out[:, h * 512 : h * 512 + 512],
            ],
            axis=1,
        )
        for h in range(2)
    ]
    mine = jnp.where(first, halves[0], halves[1])
    theirs = swap(jnp.where(first, halves[1], halves[0]))
    block = jnp.concatenate(
        [jnp.where(first, mine, theirs), jnp.where(first, theirs, mine)], axis=0
    )
    wa = gather_rows(block[:, 0:1024])
    oa = gather_rows(block[:, 1024:1536])
    wb = swap(wa)
    ob = swap(oa)

    normed, turned, nlast, xlast = call(
        prep_body,
        [((ROWS, D), BF16), ((D, ROWS), BF16), ((8, D), BF16), ((8, D), F32)],
        [SM, VM, VM],
        flops=10_000_000,
        nbytes=4 << 20,
    )(lens, tokens, gain)

    kproj, krot, vcast, qproj, qrot, attn, ctx = pl.pallas_call(
        attend_body,
        out_shape=[
            jax.ShapeDtypeStruct((ROWS, 512), F32),
            jax.ShapeDtypeStruct((ROWS, 512), BF16),
            jax.ShapeDtypeStruct((ROWS, 512), BF16),
            jax.ShapeDtypeStruct((8, D), F32),
            jax.ShapeDtypeStruct((8, D), BF16),
            jax.ShapeDtypeStruct((32, SEQ), F32),
            jax.ShapeDtypeStruct((8, D), BF16),
        ],
        in_specs=[SM] + [VM] * 6,
        out_specs=[VM] * 7,
        scratch_shapes=[pltpu.VMEM((8, D), F32), pltpu.VMEM((8, D), F32)],
        compiler_params=pltpu.CompilerParams(vmem_limit_bytes=48 << 20),
        cost_estimate=pl.CostEstimate(
            flops=1_100_000_000, bytes_accessed=8 << 20, transcendentals=0
        ),
    )(lens, normed, nlast, wa, wb, cos, sin)

    unit, oscale, score, tot = call(
        score_body,
        [((8, D), F32), ((8, HW), F32), ((8, HW), F32), ((8, HW), F32)],
        [VM] * 7,
        flops=20_000_000,
        nbytes=2 << 20,
    )(teach, ctx, xlast, oa, ob, fg, sv)

    totals = everyone(tot[0:1], AXES, 256).reshape(256, HW)

    gkva, gkvb, gq, gr = pl.pallas_call(
        unit_back_body,
        out_shape=[
            jax.ShapeDtypeStruct((ROWS, 512), F32),
            jax.ShapeDtypeStruct((ROWS, 512), F32),
            jax.ShapeDtypeStruct((8, D), F32),
            jax.ShapeDtypeStruct((8, D), F32),
        ],
        in_specs=[SM] + [VM] * 14,
        out_specs=[VM] * 4,
        scratch_shapes=[pltpu.VMEM((8, D), F32)] * 3,
        compiler_params=pltpu.CompilerParams(vmem_limit_bytes=48 << 20),
        cost_estimate=pl.CostEstimate(
            flops=200_000_000, bytes_accessed=8 << 20, transcendentals=0
        ),
    )(lens, krot, vcast, kproj, qproj, qrot, attn, unit, oscale, oa, ob, fg, sv, cos, sin)

    loss, grad_a, grad_b, skva, skvb, sq, sr = call(
        weight_body,
        [
            ((8, HW), F32),
            ((D, 1536), BF16),
            ((D, 1536), BF16),
            ((ROWS, 512), BF16),
            ((ROWS, 512), BF16),
            ((8, D), BF16),
            ((8, D), F32),
        ],
        [SM] + [VM] * 10,
        flops=1_100_000_000,
        nbytes=12 << 20,
    )(pb, totals, score, teach, gkva, gkvb, gq, gr, turned, nlast, ctx)

    other = swap(grad_b)
    chip = (grad_a.astype(F32) + other.astype(F32)).astype(BF16)
    reduced = scatter_rows(chip)

    (grad_hidden,) = pl.pallas_call(
        hidden_body,
        out_shape=[jax.ShapeDtypeStruct((ROWS, D), BF16)],
        in_specs=[SM] + [VM] * 8,
        out_specs=[VM],
        scratch_shapes=[pltpu.VMEM((8, D), F32)],
        compiler_params=pltpu.CompilerParams(vmem_limit_bytes=48 << 20),
        cost_estimate=pl.CostEstimate(
            flops=1_100_000_000, bytes_accessed=8 << 20, transcendentals=0
        ),
    )(lens, tokens, gain, wa, wb, skva, skvb, sq, sr)

    keep = jnp.where(first, reduced[0:4], reduced[4:8])
    got = swap(jnp.where(first, reduced[4:8], reduced[0:4]))
    low = jnp.where(first, keep, got)
    high = jnp.where(first, got, keep)

    def both(a, b):
        return jnp.concatenate([low[:, a:b], high[:, a:b]], axis=1)

    return (
        score[0:PAIRS, 0][None],
        loss[0, 0],
        grad_hidden.reshape(hidden.shape),
        both(512, 1024),
        both(0, 256),
        both(256, 512),
        both(1024, 1536).T,
    )


def solution(mesh):
    torus = Mesh(mesh.devices.reshape(mesh.shape["pb"], 8, 4, 2), AXES)
    placed = (
        P("pb", NEG, None, None),
        P("pb", NEG),
        P("pb", NEG),
        P(),
        P(),
        P(),
        P(AXES, None),
        P(AXES, None),
        P(AXES, None),
        P(None, AXES),
    )
    return jax.shard_map(
        shards,
        mesh=torus,
        in_specs=placed,
        out_specs=(
            P("pb", NEG),
            P(),
            P("pb", NEG, None, None),
            P(AXES, None),
            P(AXES, None),
            P(AXES, None),
            P(None, AXES),
        ),
        check_vma=False,
    )
```

```python
import jax
import jax.numpy as jnp
import numpy as np
from jax import lax
from jax.experimental import pallas as pl
from jax.experimental.pallas import tpu as pltpu
from jax.sharding import Mesh
from jax.sharding import PartitionSpec as P

HW = 128
AXES = ("pb", "z", "x", "c")
NEG = ("z", "x", "c")
EPS = 1e-06
ROPE_BASE = 1000000.0
GRAD_SCALE = 512.0
PAIRS = 4
SEQ = 128
D = 1024
ROWS = PAIRS * SEQ
F32 = jnp.float32
BF16 = jnp.bfloat16
VM = pl.BlockSpec(memory_space=pltpu.VMEM)
SM = pl.BlockSpec(memory_space=pltpu.SMEM)
LAST = (((1,), (1,)), ((), ()))
FIRST = (((0,), (0,)), ((), ()))
SCALE = HW ** (-0.5)


def rope_consts():
    freqs = np.float32(ROPE_BASE) ** (-(np.arange(HW // 2, dtype=np.float32) * 2.0) / HW)
    angles = np.arange(SEQ, dtype=np.float32)[:, None] * freqs.astype(np.float32)[None, :]
    angles = np.concatenate([angles, angles], axis=1)
    sign = np.where(np.arange(HW) < HW // 2, -1.0, 1.0)
    return (
        np.cos(angles).astype(np.float32),
        (np.sin(angles) * sign[None, :]).astype(np.float32),
    )


def call(body, outs, in_specs, vmem=24, flops=0, nbytes=0):
    return pl.pallas_call(
        body,
        out_shape=[jax.ShapeDtypeStruct(s, d) for s, d in outs],
        in_specs=in_specs,
        out_specs=[VM] * len(outs),
        compiler_params=pltpu.CompilerParams(vmem_limit_bytes=vmem << 20),
        cost_estimate=pl.CostEstimate(flops=flops, bytes_accessed=nbytes, transcendentals=0),
    )


def dot(a, b, dims=(((1,), (0,)), ((), ()))):
    return lax.dot_general(a, b, dims, preferred_element_type=F32)


def half_turn(v):
    return pltpu.roll(v, HW // 2, 1)


def heads(v, n):
    return [v[:, i * HW : (i + 1) * HW] for i in range(n)]


def block_mask():
    row = lax.broadcasted_iota(jnp.int32, (8, 512), 0)
    lane = lax.broadcasted_iota(jnp.int32, (8, 512), 1)
    return (lane // HW) == (row // 2), (row % 2) == 0


def to_blocks(row, mask, even):
    h = heads(row, 8)
    e = jnp.broadcast_to(jnp.concatenate(h[0::2], axis=1), (8, 512))
    o = jnp.broadcast_to(jnp.concatenate(h[1::2], axis=1), (8, 512))
    return jnp.where(mask, jnp.where(even, e, o), 0.0)


def from_blocks(blocks, mask, even):
    e = jnp.sum(jnp.where(mask & even, blocks, 0.0), axis=0, keepdims=True)
    o = jnp.sum(jnp.where(mask & (~even), blocks, 0.0), axis=0, keepdims=True)
    parts = []
    for g in range(4):
        parts += [e[:, g * HW : (g + 1) * HW], o[:, g * HW : (g + 1) * HW]]
    return jnp.concatenate(parts, axis=1)


def prep_body(len_ref, h_ref, gain_ref, normed_ref, turned_ref, nlast_ref, xlast_ref):
    row = lax.broadcasted_iota(jnp.int32, (8, SEQ), 0)
    lane = lax.broadcasted_iota(jnp.int32, (8, SEQ), 1)
    nl = jnp.zeros((8, D), F32)
    xl = jnp.zeros((8, D), F32)
    for p in range(PAIRS):
        raw = h_ref[p * SEQ : (p + 1) * SEQ, :]
        x = raw.astype(F32)
        inv = lax.rsqrt(jnp.mean(x * x, axis=-1, keepdims=True) + EPS)
        n = (x * inv * gain_ref[...]).astype(BF16)
        normed_ref[p * SEQ : (p + 1) * SEQ, :] = n
        turned_ref[:, p * SEQ : (p + 1) * SEQ] = n.T
        e = len_ref[p] - 1
        hot = jnp.where((row == p) & (lane == e), 1.0, 0.0).astype(BF16)
        nl = nl + dot(hot, n)
        xl = xl + dot(hot, raw)
    nlast_ref[...] = nl.astype(BF16)
    xlast_ref[...] = xl


def attend_body(
    len_ref,
    normed_ref,
    nlast_ref,
    kva_ref,
    kvb_ref,
    qa_ref,
    qb_ref,
    cos_ref,
    sin_ref,
    kproj_ref,
    krot_ref,
    vcast_ref,
    qproj_ref,
    qrot_ref,
    attn_ref,
    ctx_ref,
    qr_scr,
    ctx_scr,
):
    mask, even = block_mask()
    lane = lax.broadcasted_iota(jnp.int32, (8, SEQ), 1)
    for half, (kv_ref, q_ref) in enumerate(((kva_ref, qa_ref), (kvb_ref, qb_ref))):
        kv = dot(normed_ref[...], kv_ref[...])
        kproj_ref[:, half * 256 : half * 256 + 256] = kv[:, 0:256]
        vcast_ref[:, half * 256 : half * 256 + 256] = kv[:, 256:512].astype(BF16)
        qproj_ref[:, half * 512 : half * 512 + 512] = dot(nlast_ref[...], q_ref[...])
    cos_q = jnp.concatenate(
        [cos_ref[pl.ds(len_ref[p] - 1, 1), :] for p in range(PAIRS)] * 2, axis=0
    )
    sin_q = jnp.concatenate(
        [sin_ref[pl.ds(len_ref[p] - 1, 1), :] for p in range(PAIRS)] * 2, axis=0
    )
    for h in range(8):
        q = qproj_ref[:, h * HW : (h + 1) * HW]
        u = q * lax.rsqrt(jnp.mean(q * q, axis=-1, keepdims=True) + EPS)
        r = u * cos_q + half_turn(u) * sin_q
        qr_scr[:, h * HW : (h + 1) * HW] = r
        qrot_ref[:, h * HW : (h + 1) * HW] = r.astype(BF16)
    ctx_scr[...] = jnp.zeros((8, D), F32)
    for p in range(PAIRS):
        rows = slice(p * SEQ, (p + 1) * SEQ)
        for g in range(4):
            k = kproj_ref[rows, g * HW : (g + 1) * HW]
            u = k * lax.rsqrt(jnp.mean(k * k, axis=-1, keepdims=True) + EPS)
            r = u * cos_ref[...] + half_turn(u) * sin_ref[...]
            krot_ref[rows, g * HW : (g + 1) * HW] = r.astype(BF16)
        qb = to_blocks(qr_scr[p : p + 1, :], mask, even).astype(BF16)
        logits = dot(qb, krot_ref[rows, :], LAST) * SCALE
        ex = jnp.where(lane <= len_ref[p] - 1, jnp.exp(logits), 0.0)
        w = ex / jnp.sum(ex, axis=-1, keepdims=True)
        attn_ref[p * 8 : (p + 1) * 8, :] = w
        c = dot(w.astype(BF16), vcast_ref[rows, :])
        ctx_scr[p : p + 1, :] = from_blocks(c, mask, even)
    ctx_ref[...] = ctx_scr[...].astype(BF16)


def score_body(
    teach_ref, ctx_ref, xlast_ref, oa_ref, ob_ref, fg_ref, sv_ref, unit_ref, oscale_ref, score_ref, tot_ref
):
    res = xlast_ref[...] + (
        dot(ctx_ref[:, 0:512], oa_ref[...], LAST) + dot(ctx_ref[:, 512:1024], ob_ref[...], LAST)
    )
    sc = lax.rsqrt(jnp.mean(res * res, axis=-1, keepdims=True) + EPS)
    unit = res * sc
    unit_ref[...] = unit
    oscale_ref[...] = jnp.broadcast_to(sc, (8, HW))
    s = jnp.sum(unit * fg_ref[...] * sv_ref[...], axis=-1, keepdims=True)
    s = jnp.broadcast_to(s, (8, HW))
    score_ref[...] = s
    row = lax.broadcasted_iota(jnp.int32, (8, HW), 0)
    lane = lax.broadcasted_iota(jnp.int32, (8, HW), 1)
    scaled = teach_ref[...] / 2.0
    es = jnp.exp(s)
    et = jnp.exp(scaled)
    v = jnp.where(lane == 0, es, jnp.where(lane == 1, et, et * (scaled - s)))
    v = jnp.where((row < PAIRS) & (lane < 3), v, 0.0)
    tot_ref[...] = jnp.broadcast_to(jnp.sum(v, axis=0, keepdims=True), (8, HW))


def unit_back_body(
    len_ref,
    krot_ref,
    vcast_ref,
    kproj_ref,
    qproj_ref,
    qrot_ref,
    attn_ref,
    unit_ref,
    oscale_ref,
    oa_ref,
    ob_ref,
    fg_ref,
    sv_ref,
    cos_ref,
    sin_ref,
    gkva_ref,
    gkvb_ref,
    gq_ref,
    gr_ref,
    gc_scr,
    gq_scr,
    qr_scr,
):
    mask, even = block_mask()
    unit = unit_ref[...]
    gu = sv_ref[...] * fg_ref[...]
    gr = oscale_ref[:, 0:1] * (gu - unit * jnp.mean(gu * unit, axis=-1, keepdims=True))
    gr_ref[...] = gr
    grb = gr.astype(BF16)
    gc_scr[:, 0:512] = dot(grb, oa_ref[...])
    gc_scr[:, 512:1024] = dot(grb, ob_ref[...])
    qr_scr[...] = qrot_ref[...].astype(F32)
    gq_scr[...] = jnp.zeros((8, D), F32)
    for p in range(PAIRS):
        rows = slice(p * SEQ, (p + 1) * SEQ)
        gb = to_blocks(gc_scr[p : p + 1, :], mask, even).astype(BF16)
        qb = to_blocks(qr_scr[p : p + 1, :], mask, even).astype(BF16)
        w = attn_ref[p * 8 : (p + 1) * 8, :]
        gp = dot(gb, vcast_ref[rows, :], LAST)
        gv = dot(w.astype(BF16), gb, FIRST)
        gkva_ref[rows, 256:512] = gv[:, 0:256]
        gkvb_ref[rows, 256:512] = gv[:, 256:512]
        spread = jnp.sum(w * gp, axis=-1, keepdims=True)
        dl = (w * (gp - spread)).astype(BF16)
        gq_scr[p : p + 1, :] = from_blocks(dot(dl, krot_ref[rows, :]) * SCALE, mask, even)
        gk = dot(dl, qb, FIRST) * SCALE
        for g in range(4):
            k = kproj_ref[rows, g * HW : (g + 1) * HW]
            sc = lax.rsqrt(jnp.mean(k * k, axis=-1, keepdims=True) + EPS)
            u = k * sc
            r = gk[:, g * HW : (g + 1) * HW]
            t = r * cos_ref[...] + half_turn(r * sin_ref[...])
            out = sc * (t - u * jnp.mean(t * u, axis=-1, keepdims=True))
            ref = gkva_ref if g < 2 else gkvb_ref
            ref[rows, (g % 2) * HW : (g % 2 + 1) * HW] = out
    cos_q = jnp.concatenate(
        [cos_ref[pl.ds(len_ref[p] - 1, 1), :] for p in range(PAIRS)] * 2, axis=0
    )
    sin_q = jnp.concatenate(
        [sin_ref[pl.ds(len_ref[p] - 1, 1), :] for p in range(PAIRS)] * 2, axis=0
    )
    for h in range(8):
        q = qproj_ref[:, h * HW : (h + 1) * HW]
        sc = lax.rsqrt(jnp.mean(q * q, axis=-1, keepdims=True) + EPS)
        u = q * sc
        r = gq_scr[:, h * HW : (h + 1) * HW]
        t = r * cos_q + half_turn(r * sin_q)
        gq_ref[:, h * HW : (h + 1) * HW] = sc * (
            t - u * jnp.mean(t * u, axis=-1, keepdims=True)
        )


def weight_body(
    pb_ref,
    tot_ref,
    score_ref,
    teach_ref,
    gkva_ref,
    gkvb_ref,
    gq_ref,
    gr_ref,
    turned_ref,
    nlast_ref,
    ctx_ref,
    loss_ref,
    grad_kvb_ref,
    grad_qb_ref,
    grad_ob_ref,
    skva_ref,
    skvb_ref,
    sq_ref,
    sr_ref,
):
    pb = pb_ref[0]
    lane = lax.broadcasted_iota(jnp.int32, (1, HW), 1)

    def pick(v, i):
        return jnp.sum(jnp.where(lane == i, v, 0.0), axis=-1, keepdims=True)

    loss = jnp.zeros((1, 1), F32)
    mine = jnp.zeros((1, HW), F32)
    for q in range(4):
        t = jnp.sum(tot_ref[q * 64 : (q + 1) * 64, :], axis=0, keepdims=True)
        ts, tt, cr = pick(t, 0), pick(t, 1), pick(t, 2)
        loss = loss + (cr / tt - jnp.log(tt) + jnp.log(ts))
        mine = mine + jnp.where(pb == q, t, 0.0)
    loss_ref[...] = jnp.broadcast_to(loss, (8, HW))
    ts, tt = pick(mine, 0), pick(mine, 1)
    row = lax.broadcasted_iota(jnp.int32, (8, HW), 0)
    g = GRAD_SCALE * (jnp.exp(score_ref[...]) / ts - jnp.exp(teach_ref[...] / 2.0) / tt)
    g = jnp.where(row < PAIRS, g, 0.0)
    gcol = g[:, 0:1]
    sr = gr_ref[...] * gcol
    sr_ref[...] = sr
    sq = (gq_ref[...] * gcol).astype(BF16)
    sq_ref[...] = sq
    for gkv_ref, s_ref in ((gkvb_ref, skvb_ref), (gkva_ref, skva_ref)):
        for p in range(PAIRS):
            rows = slice(p * SEQ, (p + 1) * SEQ)
            s_ref[rows, :] = (gkv_ref[rows, :] * gcol[p : p + 1, :]).astype(BF16)
    grad_kvb_ref[...] = dot(turned_ref[...], skvb_ref[...]).astype(BF16)
    grad_qb_ref[...] = dot(nlast_ref[...], sq[:, 512:1024], FIRST).astype(BF16)
    grad_ob_ref[...] = dot(sr.astype(BF16), ctx_ref[:, 512:1024], FIRST).astype(BF16)


def own_weight_body(
    skva_ref, sq_ref, sr_ref, turned_ref, nlast_ref, ctx_ref, grad_kva_ref, grad_qa_ref, grad_oa_ref
):
    grad_kva_ref[...] = dot(turned_ref[...], skva_ref[...]).astype(BF16)
    grad_qa_ref[...] = dot(nlast_ref[...], sq_ref[:, 0:512], FIRST).astype(BF16)
    grad_oa_ref[...] = dot(sr_ref[...].astype(BF16), ctx_ref[:, 0:512], FIRST).astype(BF16)


def hidden_body(
    len_ref,
    h_ref,
    gain_ref,
    kva_ref,
    kvb_ref,
    qa_ref,
    qb_ref,
    skva_ref,
    skvb_ref,
    sq_ref,
    sr_ref,
    out_ref,
    last_scr,
):
    last_scr[...] = dot(sq_ref[:, 0:512], qa_ref[...], LAST) + dot(
        sq_ref[:, 512:1024], qb_ref[...], LAST
    )
    pos = lax.broadcasted_iota(jnp.int32, (SEQ, 1), 0)
    for p in range(PAIRS):
        rows = slice(p * SEQ, (p + 1) * SEQ)
        gn = dot(skva_ref[rows, :], kva_ref[...], LAST) + dot(
            skvb_ref[rows, :], kvb_ref[...], LAST
        )
        at = pos == len_ref[p] - 1
        gn = gn + jnp.where(at, last_scr[p : p + 1, :], 0.0)
        x = h_ref[rows, :].astype(F32)
        inv = lax.rsqrt(jnp.mean(x * x, axis=-1, keepdims=True) + EPS)
        s = gn * gain_ref[...]
        gi = inv * s - x * (inv * inv * inv * jnp.mean(s * x, axis=-1, keepdims=True))
        gi = gi + jnp.where(at, sr_ref[p : p + 1, :], 0.0)
        out_ref[rows, :] = gi.astype(BF16)


def everyone(x, axes, count):
    return lax.all_to_all(
        jnp.broadcast_to(x[None], (count, *x.shape)), axes, 0, 0, tiled=True
    )


def by_chip(planes):
    got = planes.reshape(4, 4, 8, 8, -1)
    return jnp.transpose(got, (0, 2, 1, 3, 4)).reshape(1024, -1)


def scatter_planes(x):
    width = x.shape[1]
    turned = jnp.transpose(x.reshape(4, 8, 4, 8, width), (0, 2, 1, 3, 4)).reshape(16, 64, width)
    got = lax.all_to_all(turned, ("pb", "x"), 0, 0, tiled=True)
    return jnp.sum(got.astype(F32), axis=0).astype(BF16)


def scatter_z(part):
    got = lax.all_to_all(part.reshape(8, 8, -1), "z", 0, 0, tiled=True)
    return jnp.sum(got.astype(F32), axis=0)


def swap(x):
    return lax.ppermute(x, "c", [(0, 1), (1, 0)])


def shards(
    hidden,
    lengths,
    teacher,
    norm_gain,
    final_gain,
    score_vector,
    query_weight,
    key_matrix,
    value_matrix,
    out_weight,
):
    c = lax.axis_index("c")
    first = c == 0
    pb = lax.axis_index("pb").astype(jnp.int32)[None]
    tokens = hidden.reshape(ROWS, D)
    lens = lengths[0]
    gain = norm_gain[None]
    fg = final_gain[None]
    sv = score_vector[None]
    cos_np, sin_np = rope_consts()
    cos, sin = jnp.asarray(cos_np), jnp.asarray(sin_np)
    teach = jnp.broadcast_to(jnp.pad(teacher[0], (0, 4))[:, None], (8, HW))

    turned_out = out_weight.T
    halves = [
        jnp.concatenate(
            [
                key_matrix[:, h * 256 : h * 256 + 256],
                value_matrix[:, h * 256 : h * 256 + 256],
                query_weight[:, h * 512 : h * 512 + 512],
                turned_out[:, h * 512 : h * 512 + 512],
            ],
            axis=1,
        )
        for h in range(2)
    ]
    mine = jnp.where(first, halves[0], halves[1])
    theirs = swap(jnp.where(first, halves[1], halves[0]))
    block = jnp.concatenate(
        [jnp.where(first, mine, theirs), jnp.where(first, theirs, mine)], axis=0
    )
    column = everyone(block, "z", 8).reshape(64, 1536)
    normed, turned, nlast, xlast = call(
        prep_body,
        [((ROWS, D), BF16), ((D, ROWS), BF16), ((8, D), BF16), ((8, D), F32)],
        [SM, VM, VM],
        flops=10_000_000,
        nbytes=4 << 20,
    )(lens, tokens, gain)

    column, normed, turned, nlast, xlast = lax.optimization_barrier(
        (column, normed, turned, nlast, xlast)
    )
    kvqa = by_chip(everyone(column[:, 0:1024], ("pb", "x"), 16))
    kva, qa = kvqa[:, 0:512], kvqa[:, 512:1024]
    planes_o = everyone(column[:, 1024:1536], ("pb", "x"), 16)
    kvb = swap(kva)
    qb = swap(qa)

    kproj, krot, vcast, qproj, qrot, attn, ctx = pl.pallas_call(
        attend_body,
        out_shape=[
            jax.ShapeDtypeStruct((ROWS, 512), F32),
            jax.ShapeDtypeStruct((ROWS, 512), BF16),
            jax.ShapeDtypeStruct((ROWS, 512), BF16),
            jax.ShapeDtypeStruct((8, D), F32),
            jax.ShapeDtypeStruct((8, D), BF16),
            jax.ShapeDtypeStruct((32, SEQ), F32),
            jax.ShapeDtypeStruct((8, D), BF16),
        ],
        in_specs=[SM] + [VM] * 8,
        out_specs=[VM] * 7,
        scratch_shapes=[pltpu.VMEM((8, D), F32), pltpu.VMEM((8, D), F32)],
        compiler_params=pltpu.CompilerParams(vmem_limit_bytes=24 << 20),
        cost_estimate=pl.CostEstimate(
            flops=1_100_000_000, bytes_accessed=8 << 20, transcendentals=0
        ),
    )(lens, normed, nlast, kva, kvb, qa, qb, cos, sin)

    ctx, planes_o = lax.optimization_barrier((ctx, planes_o))
    oa = by_chip(planes_o)
    ob = swap(oa)

    unit, oscale, score, tot = call(
        score_body,
        [((8, D), F32), ((8, HW), F32), ((8, HW), F32), ((8, HW), F32)],
        [VM] * 7,
        flops=20_000_000,
        nbytes=2 << 20,
    )(teach, ctx, xlast, oa, ob, fg, sv)

    totals = everyone(tot[0:1], AXES, 256).reshape(256, HW)

    gkva, gkvb, gq, gr = pl.pallas_call(
        unit_back_body,
        out_shape=[
            jax.ShapeDtypeStruct((ROWS, 512), F32),
            jax.ShapeDtypeStruct((ROWS, 512), F32),
            jax.ShapeDtypeStruct((8, D), F32),
            jax.ShapeDtypeStruct((8, D), F32),
        ],
        in_specs=[SM] + [VM] * 14,
        out_specs=[VM] * 4,
        scratch_shapes=[pltpu.VMEM((8, D), F32)] * 3,
        compiler_params=pltpu.CompilerParams(vmem_limit_bytes=24 << 20),
        cost_estimate=pl.CostEstimate(
            flops=200_000_000, bytes_accessed=8 << 20, transcendentals=0
        ),
    )(lens, krot, vcast, kproj, qproj, qrot, attn, unit, oscale, oa, ob, fg, sv, cos, sin)

    half_grad = ((D, 512), BF16)
    loss, grad_kvb, grad_qb, grad_ob, skva, skvb, sq, sr = call(
        weight_body,
        [
            ((8, HW), F32),
            half_grad,
            half_grad,
            half_grad,
            ((ROWS, 512), BF16),
            ((ROWS, 512), BF16),
            ((8, D), BF16),
            ((8, D), F32),
        ],
        [SM] + [VM] * 10,
        flops=600_000_000,
        nbytes=8 << 20,
    )(pb, totals, score, teach, gkva, gkvb, gq, gr, turned, nlast, ctx)
    grad_kva, grad_qa, grad_oa = call(
        own_weight_body,
        [half_grad, half_grad, half_grad],
        [VM] * 6,
        flops=600_000_000,
        nbytes=6 << 20,
    )(skva, sq, sr, turned, nlast, ctx)

    def chip(own, other):
        return (own.astype(F32) + swap(other).astype(F32)).astype(BF16)

    part = scatter_planes(
        jnp.concatenate(
            [chip(grad_kva, grad_kvb), chip(grad_qa, grad_qb), chip(grad_oa, grad_ob)], axis=1
        )
    )

    (grad_hidden,) = pl.pallas_call(
        hidden_body,
        out_shape=[jax.ShapeDtypeStruct((ROWS, D), BF16)],
        in_specs=[SM] + [VM] * 10,
        out_specs=[VM],
        scratch_shapes=[pltpu.VMEM((8, D), F32)],
        compiler_params=pltpu.CompilerParams(vmem_limit_bytes=24 << 20),
        cost_estimate=pl.CostEstimate(
            flops=1_100_000_000, bytes_accessed=8 << 20, transcendentals=0
        ),
    )(lens, tokens, gain, kva, kvb, qa, qb, skva, skvb, sq, sr)

    part, grad_hidden = lax.optimization_barrier((part, grad_hidden))
    reduced = scatter_z(part)
    keep = jnp.where(first, reduced[0:4], reduced[4:8])
    got = swap(jnp.where(first, reduced[4:8], reduced[0:4]))
    low = jnp.where(first, keep, got)
    high = jnp.where(first, got, keep)

    def both(a, b):
        return jnp.concatenate([low[:, a:b], high[:, a:b]], axis=1)

    return (
        score[0:PAIRS, 0][None],
        loss[0, 0],
        grad_hidden.reshape(hidden.shape),
        both(512, 1024),
        both(0, 256),
        both(256, 512),
        both(1024, 1536).T,
    )


def solution(mesh):
    torus = Mesh(mesh.devices.reshape(mesh.shape["pb"], 8, 4, 2), AXES)
    placed = (
        P("pb", NEG, None, None),
        P("pb", NEG),
        P("pb", NEG),
        P(),
        P(),
        P(),
        P(AXES, None),
        P(AXES, None),
        P(AXES, None),
        P(None, AXES),
    )
    return jax.shard_map(
        shards,
        mesh=torus,
        in_specs=placed,
        out_specs=(
            P("pb", NEG),
            P(),
            P("pb", NEG, None, None),
            P(AXES, None),
            P(AXES, None),
            P(AXES, None),
            P(None, AXES),
        ),
        check_vma=False,
    )
```

```python
import jax
import jax.numpy as jnp
import numpy as np
from jax import lax
from jax.experimental import pallas as pl
from jax.experimental.pallas import tpu as pltpu
from jax.sharding import Mesh
from jax.sharding import PartitionSpec as P

HW = 128
AXES = ("pb", "z", "x", "c")
NEG = ("z", "x", "c")
EPS = 1e-06
ROPE_BASE = 1000000.0
GRAD_SCALE = 512.0
PAIRS = 4
SEQ = 128
D = 1024
ROWS = PAIRS * SEQ
F32 = jnp.float32
BF16 = jnp.bfloat16
SM = pl.BlockSpec(memory_space=pltpu.SMEM)
LAST = (((1,), (1,)), ((), ()))
FIRST = (((0,), (0,)), ((), ()))
SCALE = HW ** (-0.5)


def rope_consts():
    freqs = np.float32(ROPE_BASE) ** (-(np.arange(HW // 2, dtype=np.float32) * 2.0) / HW)
    angles = np.arange(SEQ, dtype=np.float32)[:, None] * freqs.astype(np.float32)[None, :]
    angles = np.concatenate([angles, angles], axis=1)
    sign = np.where(np.arange(HW) < HW // 2, -1.0, 1.0)
    return (
        np.cos(angles).astype(np.float32),
        (np.sin(angles) * sign[None, :]).astype(np.float32),
    )


def whole(shape):
    return pl.BlockSpec(shape, lambda i: (0,) * len(shape), pipeline_mode=pl.Buffered(1))


def call(body, scalars, arrays, outs, scratch=(), flops=0):
    moved = sum(a.size * a.dtype.itemsize for a in arrays)
    moved += sum(int(np.prod(o)) * np.dtype(d).itemsize for o, d in outs)
    return pl.pallas_call(
        body,
        grid=(1,),
        out_shape=[jax.ShapeDtypeStruct(o, d) for o, d in outs],
        in_specs=[SM] * len(scalars) + [whole(a.shape) for a in arrays],
        out_specs=[whole(o) for o, _ in outs],
        scratch_shapes=[pltpu.VMEM(o, d) for o, d in scratch],
        compiler_params=pltpu.CompilerParams(vmem_limit_bytes=30 << 20),
        cost_estimate=pl.CostEstimate(flops=flops, bytes_accessed=moved, transcendentals=0),
    )(*scalars, *arrays)


def block_at(me, step, width):
    return pl.ds(pl.multiple_of(lax.rem(me + step + 4, 4) * width, width), width)


def dot(a, b, dims=(((1,), (0,)), ((), ()))):
    return lax.dot_general(a, b, dims, preferred_element_type=F32)


def half_turn(v):
    return pltpu.roll(v, HW // 2, 1)


def heads(v, n):
    return [v[:, i * HW : (i + 1) * HW] for i in range(n)]


def block_mask():
    row = lax.broadcasted_iota(jnp.int32, (8, 512), 0)
    lane = lax.broadcasted_iota(jnp.int32, (8, 512), 1)
    return (lane // HW) == (row // 2), (row % 2) == 0


def to_blocks(row, mask, even):
    h = heads(row, 8)
    e = jnp.broadcast_to(jnp.concatenate(h[0::2], axis=1), (8, 512))
    o = jnp.broadcast_to(jnp.concatenate(h[1::2], axis=1), (8, 512))
    return jnp.where(mask, jnp.where(even, e, o), 0.0)


def from_blocks(blocks, mask, even):
    e = jnp.sum(jnp.where(mask & even, blocks, 0.0), axis=0, keepdims=True)
    o = jnp.sum(jnp.where(mask & (~even), blocks, 0.0), axis=0, keepdims=True)
    parts = []
    for g in range(4):
        parts += [e[:, g * HW : (g + 1) * HW], o[:, g * HW : (g + 1) * HW]]
    return jnp.concatenate(parts, axis=1)


def prep_body(len_ref, h_ref, gain_ref, normed_ref, turned_ref, nlast_ref, xlast_ref):
    row = lax.broadcasted_iota(jnp.int32, (8, SEQ), 0)
    lane = lax.broadcasted_iota(jnp.int32, (8, SEQ), 1)
    nl = jnp.zeros((8, D), F32)
    xl = jnp.zeros((8, D), F32)
    for p in range(PAIRS):
        raw = h_ref[p * SEQ : (p + 1) * SEQ, :]
        x = raw.astype(F32)
        inv = lax.rsqrt(jnp.mean(x * x, axis=-1, keepdims=True) + EPS)
        n = (x * inv * gain_ref[...]).astype(BF16)
        normed_ref[p * SEQ : (p + 1) * SEQ, :] = n
        turned_ref[:, p * SEQ : (p + 1) * SEQ] = n.T
        e = len_ref[p] - 1
        hot = jnp.where((row == p) & (lane == e), 1.0, 0.0).astype(BF16)
        nl = nl + dot(hot, n)
        xl = xl + dot(hot, raw)
    nlast_ref[...] = nl.astype(BF16)
    xlast_ref[...] = xl


def arrange_body(at_ref, *refs):
    a_refs, b_refs, out_a_ref, out_b_ref = refs[0:4], refs[4:8], refs[8], refs[9]
    y, x = at_ref[0], at_ref[1]
    for d in range(4):
        out_a_ref[:, pl.ds(lax.rem(x - d + 4, 4), 1)] = a_refs[d][...].reshape(8, 1, 8, 1024)
        out_b_ref[pl.ds(lax.rem(y - d + 4, 4), 1)] = b_refs[d][...].reshape(1, 64, 512)


def attend_body(at_ref, len_ref, normed_ref, nlast_ref, cos_ref, sin_ref, *refs):
    kv_refs, q_refs = (refs[0:4], refs[4:8]), (refs[8:12], refs[12:16])
    kproj_ref, krot_ref, vcast_ref, qproj_ref, qrot_ref, attn_ref, ctx_ref, qr_scr, ctx_scr = refs[16:]
    y, x = at_ref[0], at_ref[1]
    mask, even = block_mask()
    lane = lax.broadcasted_iota(jnp.int32, (8, SEQ), 1)
    for half in range(2):
        kv = jnp.zeros((ROWS, 512), F32)
        q = jnp.zeros((8, 512), F32)
        for d in range(4):
            kv = kv + dot(normed_ref[:, block_at(y, -d, 256)], kv_refs[half][d][...])
            q = q + dot(nlast_ref[:, block_at(x, -d, 256)], q_refs[half][d][...])
        kproj_ref[:, half * 256 : half * 256 + 256] = kv[:, 0:256]
        vcast_ref[:, half * 256 : half * 256 + 256] = kv[:, 256:512].astype(BF16)
        qproj_ref[:, half * 512 : half * 512 + 512] = q
    cos_q = jnp.concatenate(
        [cos_ref[pl.ds(len_ref[p] - 1, 1), :] for p in range(PAIRS)] * 2, axis=0
    )
    sin_q = jnp.concatenate(
        [sin_ref[pl.ds(len_ref[p] - 1, 1), :] for p in range(PAIRS)] * 2, axis=0
    )
    for h in range(8):
        q = qproj_ref[:, h * HW : (h + 1) * HW]
        u = q * lax.rsqrt(jnp.mean(q * q, axis=-1, keepdims=True) + EPS)
        r = u * cos_q + half_turn(u) * sin_q
        qr_scr[:, h * HW : (h + 1) * HW] = r
        qrot_ref[:, h * HW : (h + 1) * HW] = r.astype(BF16)
    ctx_scr[...] = jnp.zeros((8, D), F32)
    for p in range(PAIRS):
        rows = slice(p * SEQ, (p + 1) * SEQ)
        for g in range(4):
            k = kproj_ref[rows, g * HW : (g + 1) * HW]
            u = k * lax.rsqrt(jnp.mean(k * k, axis=-1, keepdims=True) + EPS)
            r = u * cos_ref[...] + half_turn(u) * sin_ref[...]
            krot_ref[rows, g * HW : (g + 1) * HW] = r.astype(BF16)
        qb = to_blocks(qr_scr[p : p + 1, :], mask, even).astype(BF16)
        logits = dot(qb, krot_ref[rows, :], LAST) * SCALE
        ex = jnp.where(lane <= len_ref[p] - 1, jnp.exp(logits), 0.0)
        w = ex / jnp.sum(ex, axis=-1, keepdims=True)
        attn_ref[p * 8 : (p + 1) * 8, :] = w
        c = dot(w.astype(BF16), vcast_ref[rows, :])
        ctx_scr[p : p + 1, :] = from_blocks(c, mask, even)
    ctx_ref[...] = ctx_scr[...].astype(BF16)


def score_body(at_ref, teach_ref, ctx_ref, xlast_ref, fg_ref, sv_ref, *refs):
    oa_refs, ob_refs = refs[0:4], refs[4:8]
    unit_ref, oscale_ref, score_ref, tot_ref, att_scr = refs[8:]
    y = at_ref[0]
    for d in range(4):
        att_scr[:, block_at(y, -d, 256)] = dot(ctx_ref[:, 0:512], oa_refs[d][...], LAST) + dot(
            ctx_ref[:, 512:1024], ob_refs[d][...], LAST
        )
    res = xlast_ref[...] + att_scr[...]
    sc = lax.rsqrt(jnp.mean(res * res, axis=-1, keepdims=True) + EPS)
    unit = res * sc
    unit_ref[...] = unit
    oscale_ref[...] = jnp.broadcast_to(sc, (8, HW))
    s = jnp.sum(unit * fg_ref[...] * sv_ref[...], axis=-1, keepdims=True)
    s = jnp.broadcast_to(s, (8, HW))
    score_ref[...] = s
    row = lax.broadcasted_iota(jnp.int32, (8, HW), 0)
    lane = lax.broadcasted_iota(jnp.int32, (8, HW), 1)
    scaled = teach_ref[...] / 2.0
    es = jnp.exp(s)
    et = jnp.exp(scaled)
    v = jnp.where(lane == 0, es, jnp.where(lane == 1, et, et * (scaled - s)))
    v = jnp.where((row < PAIRS) & (lane < 3), v, 0.0)
    tot_ref[...] = jnp.broadcast_to(jnp.sum(v, axis=0, keepdims=True), (8, HW))


def unit_back_body(
    at_ref,
    len_ref,
    krot_ref,
    vcast_ref,
    kproj_ref,
    qproj_ref,
    qrot_ref,
    attn_ref,
    unit_ref,
    oscale_ref,
    fg_ref,
    sv_ref,
    cos_ref,
    sin_ref,
    *refs,
):
    oa_refs, ob_refs = refs[0:4], refs[4:8]
    gkva_ref, gkvb_ref, gq_ref, gr_ref, gc_scr, gq_scr, qr_scr, gr_scr = refs[8:]
    y = at_ref[0]
    mask, even = block_mask()
    unit = unit_ref[...]
    gu = sv_ref[...] * fg_ref[...]
    gr = oscale_ref[:, 0:1] * (gu - unit * jnp.mean(gu * unit, axis=-1, keepdims=True))
    gr_ref[...] = gr
    gr_scr[...] = gr.astype(BF16)
    for half, o_refs in enumerate((oa_refs, ob_refs)):
        gc = jnp.zeros((8, 512), F32)
        for d in range(4):
            gc = gc + dot(gr_scr[:, block_at(y, -d, 256)], o_refs[d][...])
        gc_scr[:, half * 512 : half * 512 + 512] = gc
    qr_scr[...] = qrot_ref[...].astype(F32)
    gq_scr[...] = jnp.zeros((8, D), F32)
    for p in range(PAIRS):
        rows = slice(p * SEQ, (p + 1) * SEQ)
        gb = to_blocks(gc_scr[p : p + 1, :], mask, even).astype(BF16)
        qb = to_blocks(qr_scr[p : p + 1, :], mask, even).astype(BF16)
        w = attn_ref[p * 8 : (p + 1) * 8, :]
        gp = dot(gb, vcast_ref[rows, :], LAST)
        gv = dot(w.astype(BF16), gb, FIRST)
        gkva_ref[rows, 256:512] = gv[:, 0:256]
        gkvb_ref[rows, 256:512] = gv[:, 256:512]
        spread = jnp.sum(w * gp, axis=-1, keepdims=True)
        dl = (w * (gp - spread)).astype(BF16)
        gq_scr[p : p + 1, :] = from_blocks(dot(dl, krot_ref[rows, :]) * SCALE, mask, even)
        gk = dot(dl, qb, FIRST) * SCALE
        for g in range(4):
            k = kproj_ref[rows, g * HW : (g + 1) * HW]
            sc = lax.rsqrt(jnp.mean(k * k, axis=-1, keepdims=True) + EPS)
            u = k * sc
            r = gk[:, g * HW : (g + 1) * HW]
            t = r * cos_ref[...] + half_turn(r * sin_ref[...])
            out = sc * (t - u * jnp.mean(t * u, axis=-1, keepdims=True))
            ref = gkva_ref if g < 2 else gkvb_ref
            ref[rows, (g % 2) * HW : (g % 2 + 1) * HW] = out
    cos_q = jnp.concatenate(
        [cos_ref[pl.ds(len_ref[p] - 1, 1), :] for p in range(PAIRS)] * 2, axis=0
    )
    sin_q = jnp.concatenate(
        [sin_ref[pl.ds(len_ref[p] - 1, 1), :] for p in range(PAIRS)] * 2, axis=0
    )
    for h in range(8):
        q = qproj_ref[:, h * HW : (h + 1) * HW]
        sc = lax.rsqrt(jnp.mean(q * q, axis=-1, keepdims=True) + EPS)
        u = q * sc
        r = gq_scr[:, h * HW : (h + 1) * HW]
        t = r * cos_q + half_turn(r * sin_q)
        gq_ref[:, h * HW : (h + 1) * HW] = sc * (
            t - u * jnp.mean(t * u, axis=-1, keepdims=True)
        )


def weight_pieces(y, x, turned_ref, nlast_ref, skv, sq, srow, sturn, ctx_ref, half, last_refs):
    (row_scr, turn_scr), outs, adds = last_refs
    low = slice(half * 512, half * 512 + 256)
    high = slice(half * 512 + 256, half * 512 + 512)
    for d in range(4):
        out_a, out_b = outs[d], outs[4 + d]
        rows_y, rows_x = block_at(y, d, 256), block_at(x, d, 256)
        kv = dot(turned_ref[rows_y, :], skv)
        o_low = dot(row_scr[:, rows_y], ctx_ref[:, low], FIRST)
        q = dot(nlast_ref[:, rows_x], sq, FIRST)
        o_high = dot(turn_scr[:, rows_x], ctx_ref[:, high], FIRST)
        if adds is None:
            out_a[:, 0:512] = kv.astype(BF16)
            out_a[:, 512:768] = o_low.astype(BF16)
            out_b[:, 0:512] = q.astype(BF16)
            out_b[:, 512:768] = o_high.astype(BF16)
        else:
            add_a, add_b = adds[d], adds[4 + d]
            out_a[:, 0:512] = (kv + add_a[:, 0:512].astype(F32)).astype(BF16)
            out_a[:, 512:768] = (o_low + add_a[:, 512:768].astype(F32)).astype(BF16)
            out_b[:, 0:512] = (q + add_b[:, 0:512].astype(F32)).astype(BF16)
            out_b[:, 512:768] = (o_high + add_b[:, 512:768].astype(F32)).astype(BF16)


def weight_body(
    at_ref,
    tot_ref,
    score_ref,
    teach_ref,
    gkva_ref,
    gkvb_ref,
    gq_ref,
    gr_ref,
    grturn_ref,
    turned_ref,
    nlast_ref,
    ctx_ref,
    *refs,
):
    outs = refs[0:8]
    loss_ref, skva_ref, skvb_ref, sq_ref, sr_ref, srow_ref, sturn_ref = refs[8:]
    y, x = at_ref[0], at_ref[1]
    pb = y
    lane = lax.broadcasted_iota(jnp.int32, (1, HW), 1)

    def pick(v, i):
        return jnp.sum(jnp.where(lane == i, v, 0.0), axis=-1, keepdims=True)

    loss = jnp.zeros((1, 1), F32)
    mine = jnp.zeros((1, HW), F32)
    for q in range(4):
        t = jnp.sum(tot_ref[q * 64 : (q + 1) * 64, :], axis=0, keepdims=True)
        ts, tt, cr = pick(t, 0), pick(t, 1), pick(t, 2)
        loss = loss + (cr / tt - jnp.log(tt) + jnp.log(ts))
        mine = mine + jnp.where(pb == q, t, 0.0)
    loss_ref[...] = jnp.broadcast_to(loss, (8, HW))
    ts, tt = pick(mine, 0), pick(mine, 1)
    row = lax.broadcasted_iota(jnp.int32, (8, HW), 0)
    g = GRAD_SCALE * (jnp.exp(score_ref[...]) / ts - jnp.exp(teach_ref[...] / 2.0) / tt)
    g = jnp.where(row < PAIRS, g, 0.0)
    gcol = g[:, 0:1]
    sr = gr_ref[...] * gcol
    sr_ref[...] = sr
    sq = (gq_ref[...] * gcol).astype(BF16)
    sq_ref[...] = sq
    for gkv_ref, s_ref in ((gkvb_ref, skvb_ref), (gkva_ref, skva_ref)):
        for p in range(PAIRS):
            rows = slice(p * SEQ, (p + 1) * SEQ)
            s_ref[rows, :] = (gkv_ref[rows, :] * gcol[p : p + 1, :]).astype(BF16)
    srow_ref[...] = sr.astype(BF16)
    sturn_ref[...] = (grturn_ref[...] * gcol).astype(BF16)
    weight_pieces(
        y, x, turned_ref, nlast_ref, skvb_ref[...], sq[:, 512:1024], None, None, ctx_ref, 1,
        ((srow_ref, sturn_ref), outs, None),
    )


def own_weight_body(
    at_ref, skva_ref, sq_ref, srow_ref, sturn_ref, turned_ref, nlast_ref, ctx_ref, *refs
):
    weight_pieces(
        at_ref[0], at_ref[1], turned_ref, nlast_ref, skva_ref[...], sq_ref[:, 0:512], None, None,
        ctx_ref, 0, ((srow_ref, sturn_ref), refs[8:16], refs[0:8]),
    )


def middle_body(at_ref, *refs):
    a_refs, b_refs, out_a, out_b, a_scr, b_scr = (
        refs[0:4],
        refs[4:8],
        refs[8:12],
        refs[12:16],
        refs[16],
        refs[17],
    )
    y, x = at_ref[0], at_ref[1]

    def summed(parts):
        total = parts[0][...].astype(F32)
        for part in parts[1:]:
            total = total + part[...].astype(F32)
        return total

    a_scr[...] = summed(a_refs).reshape(8, 4, 8, 768)
    b_scr[...] = summed(b_refs).reshape(4, 64, 768)
    for d in range(4):
        out_a[d][...] = a_scr[:, pl.ds(lax.rem(x + d, 4), 1)].reshape(64, 768).astype(BF16)
        out_b[d][...] = b_scr[pl.ds(lax.rem(y + d, 4), 1)].reshape(64, 768).astype(BF16)


def last_body(at_ref, sq_ref, *refs):
    q_refs, out_ref = (refs[0:4], refs[4:8]), refs[8]
    x = at_ref[1]
    for d in range(4):
        out_ref[:, block_at(x, -d, 256)] = dot(sq_ref[:, 0:512], q_refs[0][d][...], LAST) + dot(
            sq_ref[:, 512:1024], q_refs[1][d][...], LAST
        )


def hidden_body(at_ref, len_ref, h_ref, gain_ref, skva_ref, skvb_ref, last_ref, sr_ref, *refs):
    kva_refs, kvb_refs, out_ref, gn_scr = refs[0:4], refs[4:8], refs[8], refs[9]
    y = at_ref[0]
    for d in range(4):
        gn_scr[:, block_at(y, -d, 256)] = dot(skva_ref[...], kva_refs[d][...], LAST) + dot(
            skvb_ref[...], kvb_refs[d][...], LAST
        )
    pos = lax.broadcasted_iota(jnp.int32, (SEQ, 1), 0)
    for p in range(PAIRS):
        rows = slice(p * SEQ, (p + 1) * SEQ)
        gn = gn_scr[rows, :]
        at = pos == len_ref[p] - 1
        gn = gn + jnp.where(at, last_ref[p : p + 1, :], 0.0)
        x = h_ref[rows, :].astype(F32)
        inv = lax.rsqrt(jnp.mean(x * x, axis=-1, keepdims=True) + EPS)
        s = gn * gain_ref[...]
        gi = inv * s - x * (inv * inv * inv * jnp.mean(s * x, axis=-1, keepdims=True))
        gi = gi + jnp.where(at, sr_ref[p : p + 1, :], 0.0)
        out_ref[rows, :] = gi.astype(BF16)


def everyone(x, axes, count):
    return lax.all_to_all(
        jnp.broadcast_to(x[None], (count, *x.shape)), axes, 0, 0, tiled=True
    )


def from_ring(x, axis):
    return [x] + [
        lax.ppermute(x, axis, [(i, (i + d) % 4) for i in range(4)]) for d in range(1, 4)
    ]


def along_ring(pieces, axis):
    return [pieces[0]] + [
        lax.ppermute(pieces[d], axis, [(i, (i + d) % 4) for i in range(4)]) for d in range(1, 4)
    ]


def chunk_turn(v):
    return jnp.transpose(v.reshape(8, 32, 4, 8), (0, 2, 1, 3)).reshape(8, D)


def chunk_back(v):
    return jnp.transpose(v.reshape(8, 4, 32, 8), (0, 2, 1, 3)).reshape(8, D)


def swap(x):
    return lax.ppermute(x, "c", [(0, 1), (1, 0)])


def shards(
    hidden,
    lengths,
    teacher,
    norm_gain,
    final_gain,
    score_vector,
    query_weight,
    key_matrix,
    value_matrix,
    out_weight,
):
    c = lax.axis_index("c")
    first = c == 0
    at = jnp.stack([lax.axis_index("pb"), lax.axis_index("x")]).astype(jnp.int32)
    tokens = hidden.reshape(ROWS, D)
    lens = lengths[0]
    gain = norm_gain[None]
    fg = final_gain[None]
    sv = score_vector[None]
    cos_np, sin_np = rope_consts()
    cos, sin = jnp.asarray(cos_np), jnp.asarray(sin_np)
    teach = jnp.broadcast_to(jnp.pad(teacher[0], (0, 4))[:, None], (8, HW))

    turned_out = out_weight.T
    halves = [
        jnp.concatenate(
            [
                key_matrix[:, h * 256 : h * 256 + 256],
                value_matrix[:, h * 256 : h * 256 + 256],
                query_weight[:, h * 512 : h * 512 + 512],
                turned_out[:, h * 512 : h * 512 + 512],
            ],
            axis=1,
        )
        for h in range(2)
    ]
    mine = jnp.where(first, halves[0], halves[1])
    theirs = swap(jnp.where(first, halves[1], halves[0]))
    block = jnp.concatenate(
        [jnp.where(first, mine, theirs), jnp.where(first, theirs, mine)], axis=0
    )
    wide = jnp.concatenate([block[:, 0:512], block[:, 1024:1536], block[:, 512:1024]], axis=1)
    column = everyone(wide, "z", 8).reshape(64, 1536)

    normed, turned, nlast, xlast = call(
        prep_body,
        [lens],
        [tokens, gain],
        [((ROWS, D), BF16), ((D, ROWS), BF16), ((8, D), BF16), ((8, D), F32)],
        flops=10_000_000,
    )
    nlast = chunk_turn(nlast)
    column, normed, turned, nlast, xlast = lax.optimization_barrier(
        (column, normed, turned, nlast, xlast)
    )
    slab_a, slab_b = call(
        arrange_body,
        [at],
        [*from_ring(column[:, 0:1024], "x"), *from_ring(column[:, 1024:1536], "pb")],
        [((8, 4, 8, 1024), BF16), ((4, 64, 512), BF16)],
    )
    slab_a = slab_a.reshape(256, 1024)
    kva = from_ring(slab_a[:, 0:512], "pb")
    qa = from_ring(slab_b.reshape(256, 512), "x")
    oa = from_ring(slab_a[:, 512:1024], "pb")
    kvb = [swap(v) for v in kva]
    qb = [swap(v) for v in qa]
    ob = [swap(v) for v in oa]

    kproj, krot, vcast, qproj, qrot, attn, ctx = call(
        attend_body,
        [at, lens],
        [normed, nlast, cos, sin, *kva, *kvb, *qa, *qb],
        [
            ((ROWS, 512), F32),
            ((ROWS, 512), BF16),
            ((ROWS, 512), BF16),
            ((8, D), F32),
            ((8, D), BF16),
            ((32, SEQ), F32),
            ((8, D), BF16),
        ],
        [((8, D), F32), ((8, D), F32)],
        flops=1_100_000_000,
    )
    unit, oscale, score, tot = call(
        score_body,
        [at],
        [teach, ctx, xlast, fg, sv, *oa, *ob],
        [((8, D), F32), ((8, HW), F32), ((8, HW), F32), ((8, HW), F32)],
        [((8, D), F32)],
        flops=20_000_000,
    )

    totals = everyone(tot[0:1], AXES, 256).reshape(256, HW)

    gkva, gkvb, gq, gr = call(
        unit_back_body,
        [at, lens],
        [krot, vcast, kproj, qproj, qrot, attn, unit, oscale, fg, sv, cos, sin, *oa, *ob],
        [((ROWS, 512), F32), ((ROWS, 512), F32), ((8, D), F32), ((8, D), F32)],
        [((8, D), F32), ((8, D), F32), ((8, D), F32), ((8, D), BF16)],
        flops=200_000_000,
    )
    grturn = chunk_turn(gr)

    piece = ((256, 768), BF16)
    res = call(
        weight_body,
        [at],
        [totals, score, teach, gkva, gkvb, gq, gr, grturn, turned, nlast, ctx],
        [piece] * 8
        + [
            ((8, HW), F32),
            ((ROWS, 512), BF16),
            ((ROWS, 512), BF16),
            ((8, D), BF16),
            ((8, D), F32),
            ((8, D), BF16),
            ((8, D), BF16),
        ],
        flops=600_000_000,
    )
    loss, skva, skvb, sq, sr, srow, sturn = res[8:]
    chip = call(
        own_weight_body,
        [at],
        [skva, sq, srow, sturn, turned, nlast, ctx, *[swap(v) for v in res[0:8]]],
        [piece] * 8,
        flops=600_000_000,
    )
    got_a = along_ring(chip[0:4], "pb")
    got_b = along_ring(chip[4:8], "x")
    (last,) = call(last_body, [at], [sq, *qa, *qb], [((8, D), F32)], flops=20_000_000)
    (grad_hidden,) = call(
        hidden_body,
        [at, lens],
        [tokens, gain, skva, skvb, chunk_back(last), sr, *kva, *kvb],
        [((ROWS, D), BF16)],
        [((ROWS, D), F32)],
        flops=1_100_000_000,
    )
    got_a, got_b, grad_hidden = lax.optimization_barrier((got_a, got_b, grad_hidden))
    mid = call(middle_body, [at], [*got_a, *got_b], [((64, 768), BF16)] * 8, [((8, 4, 8, 768), F32), ((4, 64, 768), F32)])
    done_a = along_ring(mid[0:4], "x")
    done_b = along_ring(mid[4:8], "pb")

    def added(parts):
        total = parts[0].astype(F32)
        for part in parts[1:]:
            total = total + part.astype(F32)
        return total.astype(BF16)

    part = jnp.concatenate([added(done_a), added(done_b)], axis=1)
    rec = lax.all_to_all(part.reshape(8, 8, 1536), "z", 0, 0, tiled=True)
    rec = jnp.sum(rec.astype(F32), axis=0)
    reduced = jnp.concatenate(
        [rec[:, 0:512], rec[:, 768:1280], rec[:, 512:768], rec[:, 1280:1536]], axis=1
    )

    keep = jnp.where(first, reduced[0:4], reduced[4:8])
    got = swap(jnp.where(first, reduced[4:8], reduced[0:4]))
    low = jnp.where(first, keep, got)
    high = jnp.where(first, got, keep)

    def both(a, b):
        return jnp.concatenate([low[:, a:b], high[:, a:b]], axis=1)

    return (
        score[0:PAIRS, 0][None],
        loss[0, 0],
        grad_hidden.reshape(hidden.shape),
        both(512, 1024),
        both(0, 256),
        both(256, 512),
        both(1024, 1536).T,
    )


def solution(mesh):
    torus = Mesh(mesh.devices.reshape(mesh.shape["pb"], 8, 4, 2), AXES)
    placed = (
        P("pb", NEG, None, None),
        P("pb", NEG),
        P("pb", NEG),
        P(),
        P(),
        P(),
        P(AXES, None),
        P(AXES, None),
        P(AXES, None),
        P(None, AXES),
    )
    return jax.shard_map(
        shards,
        mesh=torus,
        in_specs=placed,
        out_specs=(
            P("pb", NEG),
            P(),
            P("pb", NEG, None, None),
            P(AXES, None),
            P(AXES, None),
            P(AXES, None),
            P(None, AXES),
        ),
        check_vma=False,
    )
```

```python
import jax
import jax.numpy as jnp
import numpy as np
from jax import lax
from jax.experimental import pallas as pl
from jax.experimental.pallas import tpu as pltpu
from jax.sharding import Mesh
from jax.sharding import PartitionSpec as P

HW = 128
AXES = ("pb", "z", "x", "c")
NEG = ("z", "x", "c")
EPS = 1e-06
ROPE_BASE = 1000000.0
GRAD_SCALE = 512.0
PAIRS = 4
SEQ = 128
D = 1024
ROWS = PAIRS * SEQ
F32 = jnp.float32
BF16 = jnp.bfloat16
SM = pl.BlockSpec(memory_space=pltpu.SMEM)
LAST = (((1,), (1,)), ((), ()))
FIRST = (((0,), (0,)), ((), ()))
SCALE = HW ** (-0.5)


def rope_consts():
    freqs = np.float32(ROPE_BASE) ** (-(np.arange(HW // 2, dtype=np.float32) * 2.0) / HW)
    angles = np.arange(SEQ, dtype=np.float32)[:, None] * freqs.astype(np.float32)[None, :]
    angles = np.concatenate([angles, angles], axis=1)
    sign = np.where(np.arange(HW) < HW // 2, -1.0, 1.0)
    return (
        np.cos(angles).astype(np.float32),
        (np.sin(angles) * sign[None, :]).astype(np.float32),
    )


def whole(shape):
    return pl.BlockSpec(shape, lambda i: (0,) * len(shape), pipeline_mode=pl.Buffered(1))


def call(body, scalars, arrays, outs, scratch=(), flops=0, grant=52):
    moved = sum(a.size * a.dtype.itemsize for a in arrays)
    moved += sum(int(np.prod(o)) * np.dtype(d).itemsize for o, d in outs)
    return pl.pallas_call(
        body,
        grid=(1,),
        out_shape=[jax.ShapeDtypeStruct(o, d) for o, d in outs],
        in_specs=[SM] * len(scalars) + [whole(a.shape) for a in arrays],
        out_specs=[whole(o) for o, _ in outs],
        scratch_shapes=[pltpu.VMEM(o, d) for o, d in scratch],
        compiler_params=pltpu.CompilerParams(vmem_limit_bytes=grant << 20),
        cost_estimate=pl.CostEstimate(flops=flops, bytes_accessed=moved, transcendentals=0),
    )(*scalars, *arrays)


def block_at(me, step, width):
    return pl.ds(pl.multiple_of(lax.rem(me + step + 4, 4) * width, width), width)


def dot(a, b, dims=(((1,), (0,)), ((), ()))):
    return lax.dot_general(a, b, dims, preferred_element_type=F32)


def half_turn(v):
    return pltpu.roll(v, HW // 2, 1)


def heads(v, n):
    return [v[:, i * HW : (i + 1) * HW] for i in range(n)]


def block_mask():
    row = lax.broadcasted_iota(jnp.int32, (8, 512), 0)
    lane = lax.broadcasted_iota(jnp.int32, (8, 512), 1)
    return (lane // HW) == (row // 2), (row % 2) == 0


def to_blocks(row, mask, even):
    h = heads(row, 8)
    e = jnp.broadcast_to(jnp.concatenate(h[0::2], axis=1), (8, 512))
    o = jnp.broadcast_to(jnp.concatenate(h[1::2], axis=1), (8, 512))
    return jnp.where(mask, jnp.where(even, e, o), 0.0)


def from_blocks(blocks, mask, even):
    e = jnp.sum(jnp.where(mask & even, blocks, 0.0), axis=0, keepdims=True)
    o = jnp.sum(jnp.where(mask & (~even), blocks, 0.0), axis=0, keepdims=True)
    parts = []
    for g in range(4):
        parts += [e[:, g * HW : (g + 1) * HW], o[:, g * HW : (g + 1) * HW]]
    return jnp.concatenate(parts, axis=1)


def prep_body(len_ref, h_ref, gain_ref, normed_ref, turned_ref, nlast_ref, xlast_ref):
    row = lax.broadcasted_iota(jnp.int32, (8, SEQ), 0)
    lane = lax.broadcasted_iota(jnp.int32, (8, SEQ), 1)
    nl = jnp.zeros((8, D), F32)
    xl = jnp.zeros((8, D), F32)
    for p in range(PAIRS):
        raw = h_ref[p * SEQ : (p + 1) * SEQ, :]
        x = raw.astype(F32)
        inv = lax.rsqrt(jnp.mean(x * x, axis=-1, keepdims=True) + EPS)
        n = (x * inv * gain_ref[...]).astype(BF16)
        normed_ref[p * SEQ : (p + 1) * SEQ, :] = n
        turned_ref[:, p * SEQ : (p + 1) * SEQ] = n.T
        e = len_ref[p] - 1
        hot = jnp.where((row == p) & (lane == e), 1.0, 0.0).astype(BF16)
        nl = nl + dot(hot, n)
        xl = xl + dot(hot, raw)
    nlast_ref[...] = nl.astype(BF16)
    xlast_ref[...] = xl


def arrange_body(at_ref, *refs):
    a_refs, out_ref = refs[0:4], refs[4]
    x = at_ref[1]
    for d in range(4):
        out_ref[:, pl.ds(lax.rem(x - d + 4, 4), 1)] = a_refs[d][...].reshape(8, 1, 8, 1024)


def attend_body(at_ref, len_ref, normed_ref, nlast_ref, cos_ref, sin_ref, *refs):
    kv_refs, q_refs = refs[0:2], (refs[2:6], refs[6:10])
    kproj_ref, krot_ref, vcast_ref, qproj_ref, qrot_ref, attn_ref, ctx_ref, qr_scr, ctx_scr = refs[10:]
    x = at_ref[1]
    mask, even = block_mask()
    lane = lax.broadcasted_iota(jnp.int32, (8, SEQ), 1)
    for half in range(2):
        kv_ref = kv_refs[half]

        @pl.loop(0, PAIRS)
        def _(p):
            rows = pl.ds(pl.multiple_of(p * SEQ, SEQ), SEQ)
            kv = dot(normed_ref[rows, :], kv_ref[...])
            kproj_ref[rows, half * 256 : half * 256 + 256] = kv[:, 0:256]
            vcast_ref[rows, half * 256 : half * 256 + 256] = kv[:, 256:512].astype(BF16)

        q = jnp.zeros((8, 512), F32)
        for d in range(4):
            q = q + dot(nlast_ref[:, block_at(x, -d, 256)], q_refs[half][d][...])
        qproj_ref[:, half * 512 : half * 512 + 512] = q
    cos_q = jnp.concatenate(
        [cos_ref[pl.ds(len_ref[p] - 1, 1), :] for p in range(PAIRS)] * 2, axis=0
    )
    sin_q = jnp.concatenate(
        [sin_ref[pl.ds(len_ref[p] - 1, 1), :] for p in range(PAIRS)] * 2, axis=0
    )
    for h in range(8):
        q = qproj_ref[:, h * HW : (h + 1) * HW]
        u = q * lax.rsqrt(jnp.mean(q * q, axis=-1, keepdims=True) + EPS)
        r = u * cos_q + half_turn(u) * sin_q
        qr_scr[:, h * HW : (h + 1) * HW] = r
        qrot_ref[:, h * HW : (h + 1) * HW] = r.astype(BF16)
    ctx_scr[...] = jnp.zeros((8, D), F32)
    for p in range(PAIRS):
        rows = slice(p * SEQ, (p + 1) * SEQ)
        for g in range(4):
            k = kproj_ref[rows, g * HW : (g + 1) * HW]
            u = k * lax.rsqrt(jnp.mean(k * k, axis=-1, keepdims=True) + EPS)
            r = u * cos_ref[...] + half_turn(u) * sin_ref[...]
            krot_ref[rows, g * HW : (g + 1) * HW] = r.astype(BF16)
        qb = to_blocks(qr_scr[p : p + 1, :], mask, even).astype(BF16)
        logits = dot(qb, krot_ref[rows, :], LAST) * SCALE
        ex = jnp.where(lane <= len_ref[p] - 1, jnp.exp(logits), 0.0)
        w = ex / jnp.sum(ex, axis=-1, keepdims=True)
        attn_ref[p * 8 : (p + 1) * 8, :] = w
        c = dot(w.astype(BF16), vcast_ref[rows, :])
        ctx_scr[p : p + 1, :] = from_blocks(c, mask, even)
    ctx_ref[...] = ctx_scr[...].astype(BF16)


def score_body(teach_ref, ctx_ref, xlast_ref, fg_ref, sv_ref, oa_ref, ob_ref, *refs):
    unit_ref, oscale_ref, score_ref, tot_ref, line_ref = refs
    res = xlast_ref[...] + (
        dot(ctx_ref[:, 0:512], oa_ref[...], LAST) + dot(ctx_ref[:, 512:1024], ob_ref[...], LAST)
    )
    sc = lax.rsqrt(jnp.mean(res * res, axis=-1, keepdims=True) + EPS)
    unit = res * sc
    unit_ref[...] = unit
    oscale_ref[...] = jnp.broadcast_to(sc, (8, HW))
    s = jnp.sum(unit * fg_ref[...] * sv_ref[...], axis=-1, keepdims=True)
    s = jnp.broadcast_to(s, (8, HW))
    score_ref[...] = s
    row = lax.broadcasted_iota(jnp.int32, (8, HW), 0)
    lane = lax.broadcasted_iota(jnp.int32, (8, HW), 1)
    line_ref[...] = jnp.sum(jnp.where(row == lane, s, 0.0), axis=0, keepdims=True)[:, 0:PAIRS]
    scaled = teach_ref[...] / 2.0
    es = jnp.exp(s)
    et = jnp.exp(scaled)
    v = jnp.where(lane == 0, es, jnp.where(lane == 1, et, et * (scaled - s)))
    v = jnp.where((row < PAIRS) & (lane < 3), v, 0.0)
    tot_ref[...] = jnp.broadcast_to(jnp.sum(v, axis=0, keepdims=True), (8, HW))


def unit_back_body(
    len_ref,
    krot_ref,
    vcast_ref,
    kproj_ref,
    qproj_ref,
    qrot_ref,
    attn_ref,
    unit_ref,
    oscale_ref,
    fg_ref,
    sv_ref,
    cos_ref,
    sin_ref,
    *refs,
):
    oa_ref, ob_ref, gkva_ref, gkvb_ref, gq_ref, gr_ref, gc_scr, gq_scr, qr_scr = refs
    mask, even = block_mask()
    unit = unit_ref[...]
    gu = sv_ref[...] * fg_ref[...]
    gr = oscale_ref[:, 0:1] * (gu - unit * jnp.mean(gu * unit, axis=-1, keepdims=True))
    gr_ref[...] = gr
    grb = gr.astype(BF16)
    gc_scr[:, 0:512] = dot(grb, oa_ref[...])
    gc_scr[:, 512:1024] = dot(grb, ob_ref[...])
    qr_scr[...] = qrot_ref[...].astype(F32)
    gq_scr[...] = jnp.zeros((8, D), F32)
    for p in range(PAIRS):
        rows = slice(p * SEQ, (p + 1) * SEQ)
        gb = to_blocks(gc_scr[p : p + 1, :], mask, even).astype(BF16)
        qb = to_blocks(qr_scr[p : p + 1, :], mask, even).astype(BF16)
        w = attn_ref[p * 8 : (p + 1) * 8, :]
        gp = dot(gb, vcast_ref[rows, :], LAST)
        gv = dot(w.astype(BF16), gb, FIRST)
        gkva_ref[rows, 256:512] = gv[:, 0:256]
        gkvb_ref[rows, 256:512] = gv[:, 256:512]
        spread = jnp.sum(w * gp, axis=-1, keepdims=True)
        dl = (w * (gp - spread)).astype(BF16)
        gq_scr[p : p + 1, :] = from_blocks(dot(dl, krot_ref[rows, :]) * SCALE, mask, even)
        gk = dot(dl, qb, FIRST) * SCALE
        for g in range(4):
            k = kproj_ref[rows, g * HW : (g + 1) * HW]
            sc = lax.rsqrt(jnp.mean(k * k, axis=-1, keepdims=True) + EPS)
            u = k * sc
            r = gk[:, g * HW : (g + 1) * HW]
            t = r * cos_ref[...] + half_turn(r * sin_ref[...])
            out = sc * (t - u * jnp.mean(t * u, axis=-1, keepdims=True))
            ref = gkva_ref if g < 2 else gkvb_ref
            ref[rows, (g % 2) * HW : (g % 2 + 1) * HW] = out
    cos_q = jnp.concatenate(
        [cos_ref[pl.ds(len_ref[p] - 1, 1), :] for p in range(PAIRS)] * 2, axis=0
    )
    sin_q = jnp.concatenate(
        [sin_ref[pl.ds(len_ref[p] - 1, 1), :] for p in range(PAIRS)] * 2, axis=0
    )
    for h in range(8):
        q = qproj_ref[:, h * HW : (h + 1) * HW]
        sc = lax.rsqrt(jnp.mean(q * q, axis=-1, keepdims=True) + EPS)
        u = q * sc
        r = gq_scr[:, h * HW : (h + 1) * HW]
        t = r * cos_q + half_turn(r * sin_q)
        gq_ref[:, h * HW : (h + 1) * HW] = sc * (
            t - u * jnp.mean(t * u, axis=-1, keepdims=True)
        )


def weight_pieces(x, half, turned_ref, nlast_ref, skv_ref, sq_ref, srow_ref, sturn_ref, ctx_ref, store):
    low = slice(half * 512, half * 512 + 256)
    high = slice(half * 512 + 256, half * 512 + 512)

    @pl.loop(0, 4)
    def _(i):
        rows = pl.ds(pl.multiple_of(i * 256, 256), 256)
        kv = dot(turned_ref[rows, :], skv_ref[...])
        o_low = dot(srow_ref[:, rows], ctx_ref[:, low], FIRST)
        rows_x = block_at(x, i, 256)
        q = dot(nlast_ref[:, rows_x], sq_ref[:, half * 512 : half * 512 + 512], FIRST)
        o_high = dot(sturn_ref[:, rows_x], ctx_ref[:, high], FIRST)
        store(pl.ds(i, 1), kv, o_low, q, o_high)


def weight_body(
    at_ref,
    tot_ref,
    score_ref,
    teach_ref,
    gkva_ref,
    gkvb_ref,
    gq_ref,
    gr_ref,
    grturn_ref,
    turned_ref,
    nlast_ref,
    ctx_ref,
    *refs,
):
    out_a, out_b, loss_ref, skva_ref, skvb_ref, sq_ref, sr_ref, srow_ref, sturn_ref = refs
    pb, x = at_ref[0], at_ref[1]
    lane = lax.broadcasted_iota(jnp.int32, (1, HW), 1)

    def pick(v, i):
        return jnp.sum(jnp.where(lane == i, v, 0.0), axis=-1, keepdims=True)

    loss = jnp.zeros((1, 1), F32)
    mine = jnp.zeros((1, HW), F32)
    for q in range(4):
        t = jnp.sum(tot_ref[q * 64 : (q + 1) * 64, :], axis=0, keepdims=True)
        ts, tt, cr = pick(t, 0), pick(t, 1), pick(t, 2)
        loss = loss + (cr / tt - jnp.log(tt) + jnp.log(ts))
        mine = mine + jnp.where(pb == q, t, 0.0)
    loss_ref[...] = loss
    ts, tt = pick(mine, 0), pick(mine, 1)
    row = lax.broadcasted_iota(jnp.int32, (8, HW), 0)
    g = GRAD_SCALE * (jnp.exp(score_ref[...]) / ts - jnp.exp(teach_ref[...] / 2.0) / tt)
    g = jnp.where(row < PAIRS, g, 0.0)
    gcol = g[:, 0:1]
    sr = gr_ref[...] * gcol
    sr_ref[...] = sr
    sq = (gq_ref[...] * gcol).astype(BF16)
    sq_ref[...] = sq
    for gkv_ref, s_ref in ((gkvb_ref, skvb_ref), (gkva_ref, skva_ref)):
        for p in range(PAIRS):
            rows = slice(p * SEQ, (p + 1) * SEQ)
            s_ref[rows, :] = (gkv_ref[rows, :] * gcol[p : p + 1, :]).astype(BF16)
    srow_ref[...] = sr.astype(BF16)
    sturn_ref[...] = (grturn_ref[...] * gcol).astype(BF16)

    def store(at, kv, o_low, q, o_high):
        out_a[at, :, 0:512] = kv.astype(BF16)[None]
        out_a[at, :, 512:768] = o_low.astype(BF16)[None]
        out_b[at, :, 0:512] = q.astype(BF16)[None]
        out_b[at, :, 512:768] = o_high.astype(BF16)[None]

    weight_pieces(
        x, 1, turned_ref, nlast_ref, skvb_ref, sq_ref, srow_ref, sturn_ref, ctx_ref, store
    )


def own_weight_body(
    at_ref,
    skva_ref,
    sq_ref,
    srow_ref,
    sturn_ref,
    turned_ref,
    nlast_ref,
    ctx_ref,
    add_a,
    add_b,
    out_a,
    *refs,
):
    outs_b, b_scr = refs[0:4], refs[4]

    def store(at, kv, o_low, q, o_high):
        out_a[at, :, 0:512] = (kv[None] + add_a[at, :, 0:512].astype(F32)).astype(BF16)
        out_a[at, :, 512:768] = (o_low[None] + add_a[at, :, 512:768].astype(F32)).astype(BF16)
        b_scr[at, :, 0:512] = (q[None] + add_b[at, :, 0:512].astype(F32)).astype(BF16)
        b_scr[at, :, 512:768] = (o_high[None] + add_b[at, :, 512:768].astype(F32)).astype(BF16)

    weight_pieces(
        at_ref[1], 0, turned_ref, nlast_ref, skva_ref, sq_ref, srow_ref, sturn_ref, ctx_ref, store
    )
    for d in range(4):
        outs_b[d][...] = b_scr[d]


def middle_body(at_ref, got_a_ref, *refs):
    b_refs, out_a, out_b, a_scr = refs[0:4], refs[4:8], refs[8], refs[9]
    x = at_ref[1]
    total_a = got_a_ref[0].astype(F32)
    total_b = b_refs[0][...].astype(F32)
    for d in range(1, 4):
        total_a = total_a + got_a_ref[d].astype(F32)
        total_b = total_b + b_refs[d][...].astype(F32)
    out_b[...] = total_b.astype(BF16)
    a_scr[...] = total_a.reshape(8, 4, 8, 768)
    for d in range(4):
        out_a[d][...] = a_scr[:, pl.ds(lax.rem(x + d, 4), 1)].reshape(64, 768).astype(BF16)


def last_body(at_ref, sq_ref, *refs):
    q_refs, out_ref = (refs[0:4], refs[4:8]), refs[8]
    x = at_ref[1]
    for d in range(4):
        out_ref[:, block_at(x, -d, 256)] = dot(sq_ref[:, 0:512], q_refs[0][d][...], LAST) + dot(
            sq_ref[:, 512:1024], q_refs[1][d][...], LAST
        )


def hidden_body(
    len_ref, h_ref, gain_ref, skva_ref, skvb_ref, last_ref, sr_ref, kva_ref, kvb_ref, out_ref
):
    pos = lax.broadcasted_iota(jnp.int32, (SEQ, 1), 0)

    @pl.loop(0, PAIRS)
    def _(p):
        rows = pl.ds(pl.multiple_of(p * SEQ, SEQ), SEQ)
        gn = dot(skva_ref[rows, :], kva_ref[...], LAST) + dot(
            skvb_ref[rows, :], kvb_ref[...], LAST
        )
        at = pos == len_ref[p] - 1
        gn = gn + jnp.where(at, last_ref[pl.ds(p, 1), :], 0.0)
        x = h_ref[rows, :].astype(F32)
        inv = lax.rsqrt(jnp.mean(x * x, axis=-1, keepdims=True) + EPS)
        s = gn * gain_ref[...]
        gi = inv * s - x * (inv * inv * inv * jnp.mean(s * x, axis=-1, keepdims=True))
        gi = gi + jnp.where(at, sr_ref[pl.ds(p, 1), :], 0.0)
        out_ref[rows, :] = gi.astype(BF16)


def everyone(x, axes, count):
    return lax.all_to_all(
        jnp.broadcast_to(x[None], (count, *x.shape)), axes, 0, 0, tiled=True
    )


def from_ring(x, axis):
    return [x] + [
        lax.ppermute(x, axis, [(i, (i + d) % 4) for i in range(4)]) for d in range(1, 4)
    ]


def along_ring(pieces, axis):
    return [pieces[0]] + [
        lax.ppermute(pieces[d], axis, [(i, (i + d) % 4) for i in range(4)]) for d in range(1, 4)
    ]


def chunk_turn(v):
    return jnp.transpose(v.reshape(8, 32, 4, 8), (0, 2, 1, 3)).reshape(8, D)


def chunk_back(v):
    return jnp.transpose(v.reshape(8, 4, 32, 8), (0, 2, 1, 3)).reshape(8, D)


def swap(x):
    return lax.ppermute(x, "c", [(0, 1), (1, 0)])


def shards(
    hidden,
    lengths,
    teacher,
    norm_gain,
    final_gain,
    score_vector,
    query_weight,
    key_matrix,
    value_matrix,
    out_weight,
):
    c = lax.axis_index("c")
    first = c == 0
    at = jnp.stack([lax.axis_index("pb"), lax.axis_index("x")]).astype(jnp.int32)
    tokens = hidden.reshape(ROWS, D)
    lens = lengths[0]
    gain = norm_gain[None]
    fg = final_gain[None]
    sv = score_vector[None]
    cos_np, sin_np = rope_consts()
    cos, sin = jnp.asarray(cos_np), jnp.asarray(sin_np)
    teach = jnp.broadcast_to(jnp.pad(teacher[0], (0, 4))[:, None], (8, HW))

    turned_out = out_weight.T
    halves = [
        jnp.concatenate(
            [
                key_matrix[:, h * 256 : h * 256 + 256],
                value_matrix[:, h * 256 : h * 256 + 256],
                query_weight[:, h * 512 : h * 512 + 512],
                turned_out[:, h * 512 : h * 512 + 512],
            ],
            axis=1,
        )
        for h in range(2)
    ]
    mine = jnp.where(first, halves[0], halves[1])
    theirs = swap(jnp.where(first, halves[1], halves[0]))
    block = jnp.concatenate(
        [jnp.where(first, mine, theirs), jnp.where(first, theirs, mine)], axis=0
    )
    wide = jnp.concatenate([block[:, 0:512], block[:, 1024:1536], block[:, 512:1024]], axis=1)
    column = everyone(wide, "z", 8).reshape(64, 1536)

    normed, turned, nlast, xlast = call(
        prep_body,
        [lens],
        [tokens, gain],
        [((ROWS, D), BF16), ((D, ROWS), BF16), ((8, D), BF16), ((8, D), F32)],
        flops=10_000_000,
    )
    nlast = chunk_turn(nlast)
    column, normed, turned, nlast, xlast = lax.optimization_barrier(
        (column, normed, turned, nlast, xlast)
    )
    (slab_a,) = call(
        arrange_body,
        [at],
        from_ring(column[:, 0:1024], "x"),
        [((8, 4, 8, 1024), BF16)],
    )
    slab_a = slab_a.reshape(256, 1024)
    slab_b = everyone(column[:, 1024:1536], "pb", 4).reshape(256, 512)
    slab_a, slab_b = lax.optimization_barrier((slab_a, slab_b))
    qa = from_ring(slab_b, "x")
    kva = everyone(slab_a[:, 0:512], "pb", 4).reshape(1024, 512)
    kva, qa, slab_o = lax.optimization_barrier((kva, qa, slab_a[:, 512:1024]))
    planes_o = everyone(slab_o, "pb", 4)
    kvb = swap(kva)
    qb = [swap(v) for v in qa]

    kproj, krot, vcast, qproj, qrot, attn, ctx = call(
        attend_body,
        [at, lens],
        [normed, nlast, cos, sin, kva, kvb, *qa, *qb],
        [
            ((ROWS, 512), F32),
            ((ROWS, 512), BF16),
            ((ROWS, 512), BF16),
            ((8, D), F32),
            ((8, D), BF16),
            ((32, SEQ), F32),
            ((8, D), BF16),
        ],
        [((8, D), F32), ((8, D), F32)],
        flops=1_100_000_000,
    )
    ctx, planes_o = lax.optimization_barrier((ctx, planes_o))
    oa = planes_o.reshape(1024, 512)
    ob = swap(oa)
    unit, oscale, score, tot, line = call(
        score_body,
        [],
        [teach, ctx, xlast, fg, sv, oa, ob],
        [((8, D), F32), ((8, HW), F32), ((8, HW), F32), ((8, HW), F32), ((1, PAIRS), F32)],
        flops=20_000_000,
    )

    totals = everyone(tot[0:1], AXES, 256).reshape(256, HW)

    gkva, gkvb, gq, gr = call(
        unit_back_body,
        [lens],
        [krot, vcast, kproj, qproj, qrot, attn, unit, oscale, fg, sv, cos, sin, oa, ob],
        [((ROWS, 512), F32), ((ROWS, 512), F32), ((8, D), F32), ((8, D), F32)],
        [((8, D), F32), ((8, D), F32), ((8, D), F32)],
        flops=200_000_000,
    )
    grturn = chunk_turn(gr)

    pieces = ((4, 256, 768), BF16)
    back_a, back_b, loss, skva, skvb, sq, sr, srow, sturn = call(
        weight_body,
        [at],
        [totals, score, teach, gkva, gkvb, gq, gr, grturn, turned, nlast, ctx],
        [
            pieces,
            pieces,
            ((1, 1), F32),
            ((ROWS, 512), BF16),
            ((ROWS, 512), BF16),
            ((8, D), BF16),
            ((8, D), F32),
            ((8, D), BF16),
            ((8, D), BF16),
        ],
        flops=600_000_000,
    )
    chip_a, *chip_b = call(
        own_weight_body,
        [at],
        [skva, sq, srow, sturn, turned, nlast, ctx, swap(back_a), swap(back_b)],
        [pieces] + [((256, 768), BF16)] * 4,
        [pieces],
        flops=600_000_000,
    )
    got_a = lax.all_to_all(chip_a, "pb", 0, 0, tiled=True)
    got_b = along_ring(chip_b, "x")
    (last,) = call(last_body, [at], [sq, *qa, *qb], [((8, D), F32)], flops=20_000_000)
    (grad_hidden,) = call(
        hidden_body,
        [lens],
        [tokens, gain, skva, skvb, chunk_back(last), sr, kva, kvb],
        [((ROWS, D), BF16)],
        flops=1_100_000_000,
    )
    got_a, got_b, grad_hidden = lax.optimization_barrier((got_a, got_b, grad_hidden))
    *mid_a, mid_b = call(
        middle_body,
        [at],
        [got_a, *got_b],
        [((64, 768), BF16)] * 4 + [((256, 768), BF16)],
        [((8, 4, 8, 768), F32)],
    )
    done_a = along_ring(mid_a, "x")
    done_b = lax.all_to_all(mid_b.reshape(4, 64, 768), "pb", 0, 0, tiled=True)

    def added(parts):
        total = parts[0].astype(F32)
        for part in parts[1:]:
            total = total + part.astype(F32)
        return total.astype(BF16)

    part = jnp.concatenate([added(done_a), added(done_b)], axis=1)
    rec = lax.all_to_all(part.reshape(8, 8, 1536), "z", 0, 0, tiled=True)
    rec = jnp.sum(rec.astype(F32), axis=0)
    reduced = jnp.concatenate(
        [rec[:, 0:512], rec[:, 768:1280], rec[:, 512:768], rec[:, 1280:1536]], axis=1
    )

    keep = jnp.where(first, reduced[0:4], reduced[4:8])
    got = swap(jnp.where(first, reduced[4:8], reduced[0:4]))
    low = jnp.where(first, keep, got)
    high = jnp.where(first, got, keep)

    def both(a, b):
        return jnp.concatenate([low[:, a:b], high[:, a:b]], axis=1)

    return (
        line,
        loss.reshape(()),
        grad_hidden.reshape(hidden.shape),
        both(512, 1024),
        both(0, 256),
        both(256, 512),
        both(1024, 1536).T,
    )


def solution(mesh):
    torus = Mesh(mesh.devices.reshape(mesh.shape["pb"], 8, 4, 2), AXES)
    placed = (
        P("pb", NEG, None, None),
        P("pb", NEG),
        P("pb", NEG),
        P(),
        P(),
        P(),
        P(AXES, None),
        P(AXES, None),
        P(AXES, None),
        P(None, AXES),
    )
    return jax.shard_map(
        shards,
        mesh=torus,
        in_specs=placed,
        out_specs=(
            P("pb", NEG),
            P(),
            P("pb", NEG, None, None),
            P(AXES, None),
            P(AXES, None),
            P(AXES, None),
            P(None, AXES),
        ),
        check_vma=False,
    )
```

```python
import jax
import jax.numpy as jnp
import numpy as np
from jax import lax
from jax.experimental import pallas as pl
from jax.experimental.pallas import tpu as pltpu
from jax.sharding import Mesh
from jax.sharding import PartitionSpec as P

HW = 128
AXES = ("pb", "z", "x", "c")
NEG = ("z", "x", "c")
EPS = 1e-06
ROPE_BASE = 1000000.0
GRAD_SCALE = 512.0
PAIRS = 4
SEQ = 128
D = 1024
ROWS = PAIRS * SEQ
BOTH = 2 * PAIRS
F32 = jnp.float32
BF16 = jnp.bfloat16
SM = pl.BlockSpec(memory_space=pltpu.SMEM)
LAST = (((1,), (1,)), ((), ()))
FIRST = (((0,), (0,)), ((), ()))
SCALE = HW ** (-0.5)


def rope_consts():
    freqs = np.float32(ROPE_BASE) ** (-(np.arange(HW // 2, dtype=np.float32) * 2.0) / HW)
    angles = np.arange(SEQ, dtype=np.float32)[:, None] * freqs.astype(np.float32)[None, :]
    angles = np.concatenate([angles, angles], axis=1)
    sign = np.where(np.arange(HW) < HW // 2, -1.0, 1.0)
    return (
        np.cos(angles).astype(np.float32),
        (np.sin(angles) * sign[None, :]).astype(np.float32),
    )


def whole(shape):
    return pl.BlockSpec(shape, lambda i: (0,) * len(shape), pipeline_mode=pl.Buffered(1))


def call(body, scalars, arrays, outs, scratch=(), flops=0, grant=52, light=False):
    moved = sum(a.size * a.dtype.itemsize for a in arrays)
    moved += sum(int(np.prod(o)) * np.dtype(d).itemsize for o, d in outs)
    if light:
        moved = flops = 1024
    return pl.pallas_call(
        body,
        grid=(1,),
        out_shape=[jax.ShapeDtypeStruct(o, d) for o, d in outs],
        in_specs=[SM] * len(scalars) + [whole(a.shape) for a in arrays],
        out_specs=[whole(o) for o, _ in outs],
        scratch_shapes=[pltpu.VMEM(o, d) for o, d in scratch],
        compiler_params=pltpu.CompilerParams(vmem_limit_bytes=grant << 20),
        cost_estimate=pl.CostEstimate(flops=flops, bytes_accessed=moved, transcendentals=0),
    )(*scalars, *arrays)


def block_at(me, step, width):
    return pl.ds(pl.multiple_of(lax.rem(me + step + 4, 4) * width, width), width)


def dot(a, b, dims=(((1,), (0,)), ((), ()))):
    return lax.dot_general(a, b, dims, preferred_element_type=F32)


def half_turn(v):
    return pltpu.roll(v, HW // 2, 1)


def heads(v, n):
    return [v[:, i * HW : (i + 1) * HW] for i in range(n)]


def block_mask():
    row = lax.broadcasted_iota(jnp.int32, (8, 256), 0)
    lane = lax.broadcasted_iota(jnp.int32, (8, 256), 1)
    return (lane // HW) == (row // 2), (row % 2) == 0


def to_blocks(row, mask, even):
    h = heads(row, 4)
    e = jnp.broadcast_to(jnp.concatenate(h[0::2], axis=1), (8, 256))
    o = jnp.broadcast_to(jnp.concatenate(h[1::2], axis=1), (8, 256))
    return jnp.where(mask, jnp.where(even, e, o), 0.0)


def from_blocks(blocks, mask, even):
    e = jnp.sum(jnp.where(mask & even, blocks, 0.0), axis=0, keepdims=True)
    o = jnp.sum(jnp.where(mask & (~even), blocks, 0.0), axis=0, keepdims=True)
    return jnp.concatenate([e[:, 0:HW], o[:, 0:HW], e[:, HW:], o[:, HW:]], axis=1)


def query_tables(len_ref, cos_ref, sin_ref):
    return [
        jnp.concatenate([t[pl.ds(len_ref[p] - 1, 1), :] for p in range(BOTH)], axis=0)
        for t in (cos_ref, sin_ref)
    ]


def prep_body(len_ref, h_ref, gain_ref, normed_ref, turned_ref, nlast_ref, xlast_ref):
    row = lax.broadcasted_iota(jnp.int32, (8, SEQ), 0)
    lane = lax.broadcasted_iota(jnp.int32, (8, SEQ), 1)
    nl = jnp.zeros((8, D), F32)
    xl = jnp.zeros((8, D), F32)
    for p in range(PAIRS):
        raw = h_ref[p * SEQ : (p + 1) * SEQ, :]
        x = raw.astype(F32)
        inv = lax.rsqrt(jnp.mean(x * x, axis=-1, keepdims=True) + EPS)
        n = (x * inv * gain_ref[...]).astype(BF16)
        normed_ref[p * SEQ : (p + 1) * SEQ, :] = n
        turned_ref[:, p * SEQ : (p + 1) * SEQ] = n.T
        e = len_ref[p] - 1
        hot = jnp.where((row == p) & (lane == e), 1.0, 0.0).astype(BF16)
        nl = nl + dot(hot, n)
        xl = xl + dot(hot, raw)
    nlast_ref[...] = nl.astype(BF16)
    xlast_ref[...] = xl


def arrange_body(at_ref, *refs):
    a_refs, out_ref = refs[0:4], refs[4]
    x = at_ref[1]
    for d in range(4):
        out_ref[:, pl.ds(lax.rem(x - d + 4, 4), 1)] = a_refs[d][...].reshape(8, 1, 8, 1024)


def attend_body(
    at_ref, len_ref, normed_ref, other_ref, nlast_ref, cos_ref, sin_ref, kv_ref, *refs
):
    q_refs = refs[0:4]
    kproj_ref, krot_ref, vcast_ref, qproj_ref, qrot_ref, attn_ref, ctx_ref, qr_scr, ctx_scr = refs[4:]
    x = at_ref[1]
    mask, even = block_mask()
    lane = lax.broadcasted_iota(jnp.int32, (8, SEQ), 1)
    for side, rows_ref in enumerate((normed_ref, other_ref)):

        @pl.loop(0, 2)
        def _(i):
            src = pl.ds(pl.multiple_of(i * 256, 256), 256)
            dst = pl.ds(pl.multiple_of(side * ROWS + i * 256, 256), 256)
            kv = dot(rows_ref[src, :], kv_ref[...])
            kproj_ref[dst, :] = kv[:, 0:256]
            vcast_ref[dst, :] = kv[:, 256:512].astype(BF16)

    q = jnp.zeros((8, 512), F32)
    for d in range(4):
        q = q + dot(nlast_ref[:, block_at(x, -d, 256)], q_refs[d][...])
    qproj_ref[...] = q
    cos_q, sin_q = query_tables(len_ref, cos_ref, sin_ref)
    for h in range(4):
        q = qproj_ref[:, h * HW : (h + 1) * HW]
        u = q * lax.rsqrt(jnp.mean(q * q, axis=-1, keepdims=True) + EPS)
        r = u * cos_q + half_turn(u) * sin_q
        qr_scr[:, h * HW : (h + 1) * HW] = r
        qrot_ref[:, h * HW : (h + 1) * HW] = r.astype(BF16)
    for p in range(BOTH):
        rows = slice(p * SEQ, (p + 1) * SEQ)
        for g in range(2):
            k = kproj_ref[rows, g * HW : (g + 1) * HW]
            u = k * lax.rsqrt(jnp.mean(k * k, axis=-1, keepdims=True) + EPS)
            r = u * cos_ref[...] + half_turn(u) * sin_ref[...]
            krot_ref[rows, g * HW : (g + 1) * HW] = r.astype(BF16)
        qb = to_blocks(qr_scr[p : p + 1, :], mask, even).astype(BF16)
        logits = dot(qb, krot_ref[rows, :], LAST) * SCALE
        ex = jnp.where(lane <= len_ref[p] - 1, jnp.exp(logits), 0.0)
        w = ex / jnp.sum(ex, axis=-1, keepdims=True)
        attn_ref[p * 8 : (p + 1) * 8, :] = w
        c = dot(w.astype(BF16), vcast_ref[rows, :])
        ctx_scr[p : p + 1, :] = from_blocks(c, mask, even)
    ctx_ref[...] = ctx_scr[...].astype(BF16)


def attended_body(at_ref, ctx_ref, *refs):
    o_refs, out_ref = refs[0:4], refs[4]
    for d in range(4):
        out_ref[:, block_at(at_ref[0], -d, 256)] = dot(ctx_ref[...], o_refs[d][...], LAST)


def score_body(teach_ref, mine_ref, theirs_ref, xlast_ref, fg_ref, sv_ref, *refs):
    unit_ref, oscale_ref, score_ref, tot_ref, line_ref = refs
    res = xlast_ref[...] + (mine_ref[...] + pltpu.roll(theirs_ref[...], PAIRS, 0))
    sc = lax.rsqrt(jnp.mean(res * res, axis=-1, keepdims=True) + EPS)
    unit = res * sc
    unit_ref[...] = unit
    oscale_ref[...] = jnp.broadcast_to(sc, (8, HW))
    s = jnp.sum(unit * fg_ref[...] * sv_ref[...], axis=-1, keepdims=True)
    s = jnp.broadcast_to(s, (8, HW))
    score_ref[...] = s
    row = lax.broadcasted_iota(jnp.int32, (8, HW), 0)
    lane = lax.broadcasted_iota(jnp.int32, (8, HW), 1)
    line_ref[...] = jnp.sum(jnp.where(row == lane, s, 0.0), axis=0, keepdims=True)[:, 0:PAIRS]
    scaled = teach_ref[...] / 2.0
    es = jnp.exp(s)
    et = jnp.exp(scaled)
    v = jnp.where(lane == 0, es, jnp.where(lane == 1, et, et * (scaled - s)))
    v = jnp.where((row < PAIRS) & (lane < 3), v, 0.0)
    tot_ref[...] = jnp.broadcast_to(jnp.sum(v, axis=0, keepdims=True), (8, HW))


def unit_back_body(
    at_ref,
    len_ref,
    krot_ref,
    vcast_ref,
    kproj_ref,
    qproj_ref,
    qrot_ref,
    attn_ref,
    unit_ref,
    oscale_ref,
    fg_ref,
    sv_ref,
    cos_ref,
    sin_ref,
    *refs,
):
    o_refs, q_refs, kv_ref = refs[0:4], refs[4:8], refs[8]
    gkv_ref, gq_ref, gr_ref, last_ref, send_ref, gc_scr, gq_scr, qr_scr, gr_scr = refs[9:]
    mask, even = block_mask()
    unit = unit_ref[...]
    gu = sv_ref[...] * fg_ref[...]
    gr = oscale_ref[:, 0:1] * (gu - unit * jnp.mean(gu * unit, axis=-1, keepdims=True))
    gr_ref[...] = gr
    gr_scr[...] = gr.astype(BF16)
    gc = jnp.zeros((8, 512), F32)
    for d in range(4):
        gc = gc + dot(gr_scr[:, block_at(at_ref[0], -d, 256)], o_refs[d][...])
    gc_scr[...] = gc
    qr_scr[...] = qrot_ref[...].astype(F32)
    for p in range(BOTH):
        rows = slice(p * SEQ, (p + 1) * SEQ)
        gb = to_blocks(gc_scr[p : p + 1, :], mask, even).astype(BF16)
        qb = to_blocks(qr_scr[p : p + 1, :], mask, even).astype(BF16)
        w = attn_ref[p * 8 : (p + 1) * 8, :]
        gp = dot(gb, vcast_ref[rows, :], LAST)
        gkv_ref[rows, 256:512] = dot(w.astype(BF16), gb, FIRST)
        spread = jnp.sum(w * gp, axis=-1, keepdims=True)
        dl = (w * (gp - spread)).astype(BF16)
        gq_scr[p : p + 1, :] = from_blocks(dot(dl, krot_ref[rows, :]) * SCALE, mask, even)
        gk = dot(dl, qb, FIRST) * SCALE
        for g in range(2):
            cols = slice(g * HW, (g + 1) * HW)
            k = kproj_ref[rows, cols]
            sc = lax.rsqrt(jnp.mean(k * k, axis=-1, keepdims=True) + EPS)
            u = k * sc
            r = gk[:, cols]
            t = r * cos_ref[...] + half_turn(r * sin_ref[...])
            gkv_ref[rows, cols] = sc * (t - u * jnp.mean(t * u, axis=-1, keepdims=True))
    cos_q, sin_q = query_tables(len_ref, cos_ref, sin_ref)
    for h in range(4):
        q = qproj_ref[:, h * HW : (h + 1) * HW]
        sc = lax.rsqrt(jnp.mean(q * q, axis=-1, keepdims=True) + EPS)
        u = q * sc
        r = gq_scr[:, h * HW : (h + 1) * HW]
        t = r * cos_q + half_turn(r * sin_q)
        gq_ref[:, h * HW : (h + 1) * HW] = sc * (
            t - u * jnp.mean(t * u, axis=-1, keepdims=True)
        )
    gqb = gq_ref[...].astype(BF16)
    for d in range(4):
        last_ref[:, block_at(at_ref[1], -d, 256)] = dot(gqb, q_refs[d][...], LAST)

    @pl.loop(0, 2)
    def _(i):
        src = pl.ds(pl.multiple_of(ROWS + i * 256, 256), 256)
        gn = dot(gkv_ref[src, :].astype(BF16), kv_ref[...], LAST)
        send_ref[pl.ds(pl.multiple_of(i * 256, 256), 256), :] = gn.astype(BF16)


def weight_body(
    at_ref,
    tot_ref,
    score_ref,
    teach_ref,
    gkv_ref,
    gq_ref,
    gr_ref,
    grturn_ref,
    turned_ref,
    turned_other_ref,
    nlast_ref,
    ctx_ref,
    *refs,
):
    out_a, outs_b, loss_ref, skv_ref, g_ref, sr_ref = refs[0], refs[1:5], *refs[5:9]
    srow_scr, sturn_scr, b_scr, sq_scr = refs[9:]
    pb, x = at_ref[0], at_ref[1]
    lane = lax.broadcasted_iota(jnp.int32, (1, HW), 1)

    def pick(v, i):
        return jnp.sum(jnp.where(lane == i, v, 0.0), axis=-1, keepdims=True)

    loss = jnp.zeros((1, 1), F32)
    mine = jnp.zeros((1, HW), F32)
    for q in range(4):
        t = jnp.sum(tot_ref[q * 64 : (q + 1) * 64, :], axis=0, keepdims=True)
        ts, tt, cr = pick(t, 0), pick(t, 1), pick(t, 2)
        loss = loss + (cr / tt - jnp.log(tt) + jnp.log(ts))
        mine = mine + jnp.where(pb == q, t, 0.0)
    loss_ref[...] = loss
    ts, tt = pick(mine, 0), pick(mine, 1)
    row = lax.broadcasted_iota(jnp.int32, (8, HW), 0)
    g = GRAD_SCALE * (jnp.exp(score_ref[...]) / ts - jnp.exp(teach_ref[...] / 2.0) / tt)
    gcol = g[:, 0:1]
    sr = gr_ref[...] * gcol
    sr_ref[...] = sr
    g_ref[...] = g
    sq_scr[...] = (gq_ref[...] * gcol).astype(BF16)
    srow_scr[...] = sr.astype(BF16)
    sturn_scr[...] = (grturn_ref[...] * gcol).astype(BF16)
    for p in range(BOTH):
        rows = slice(p * SEQ, (p + 1) * SEQ)
        skv_ref[rows, :] = (gkv_ref[rows, :] * gcol[p : p + 1, :]).astype(BF16)

    @pl.loop(0, 4)
    def _(i):
        rows = pl.ds(pl.multiple_of(i * 256, 256), 256)
        kv = dot(turned_ref[rows, :], skv_ref[0:ROWS, :]) + dot(
            turned_other_ref[rows, :], skv_ref[ROWS : 2 * ROWS, :]
        )
        o_low = dot(srow_scr[:, rows], ctx_ref[:, 0:256], FIRST)
        rows_x = block_at(x, i, 256)
        q = dot(nlast_ref[:, rows_x], sq_scr[...], FIRST)
        o_high = dot(sturn_scr[:, rows_x], ctx_ref[:, 256:512], FIRST)
        here = pl.ds(i, 1)
        out_a[here, :, 0:512] = kv.astype(BF16)[None]
        out_a[here, :, 512:768] = o_low.astype(BF16)[None]
        b_scr[here, :, 0:512] = q.astype(BF16)[None]
        b_scr[here, :, 512:768] = o_high.astype(BF16)[None]

    for d in range(4):
        outs_b[d][...] = b_scr[d]


def middle_body(at_ref, got_a_ref, *refs):
    b_refs, out_a, out_b, a_scr = refs[0:4], refs[4:8], refs[8], refs[9]
    x = at_ref[1]
    total_a = got_a_ref[0].astype(F32)
    total_b = b_refs[0][...].astype(F32)
    for d in range(1, 4):
        total_a = total_a + got_a_ref[d].astype(F32)
        total_b = total_b + b_refs[d][...].astype(F32)
    out_b[...] = total_b.astype(BF16)
    a_scr[...] = total_a.reshape(8, 4, 8, 768)
    for d in range(4):
        out_a[d][...] = a_scr[:, pl.ds(lax.rem(x + d, 4), 1)].reshape(64, 768).astype(BF16)


def hidden_body(len_ref, h_ref, gain_ref, skv_ref, g_ref, last_ref, other_ref, sr_ref, kv_ref, got_ref, out_ref):
    pos = lax.broadcasted_iota(jnp.int32, (SEQ, 1), 0)

    @pl.loop(0, PAIRS)
    def _(p):
        rows = pl.ds(pl.multiple_of(p * SEQ, SEQ), SEQ)
        at = pos == len_ref[p] - 1
        last = last_ref[pl.ds(p, 1), :] + other_ref[pl.ds(PAIRS + p, 1), :]
        unit = got_ref[rows, :].astype(F32) + jnp.where(at, last, 0.0)
        gn = dot(skv_ref[rows, :], kv_ref[...], LAST) + g_ref[pl.ds(p, 1), 0:1] * unit
        x = h_ref[rows, :].astype(F32)
        inv = lax.rsqrt(jnp.mean(x * x, axis=-1, keepdims=True) + EPS)
        s = gn * gain_ref[...]
        gi = inv * s - x * (inv * inv * inv * jnp.mean(s * x, axis=-1, keepdims=True))
        gi = gi + jnp.where(at, sr_ref[pl.ds(p, 1), :], 0.0)
        out_ref[rows, :] = gi.astype(BF16)


def everyone(x, axes, count):
    return lax.all_to_all(
        jnp.broadcast_to(x[None], (count, *x.shape)), axes, 0, 0, tiled=True
    )


def from_ring(x, axis):
    return [x] + [
        lax.ppermute(x, axis, [(i, (i + d) % 4) for i in range(4)]) for d in range(1, 4)
    ]


def along_ring(pieces, axis):
    return [pieces[0]] + [
        lax.ppermute(pieces[d], axis, [(i, (i + d) % 4) for i in range(4)]) for d in range(1, 4)
    ]


def chunk_turn(v):
    return jnp.transpose(v.reshape(8, 32, 4, 8), (0, 2, 1, 3)).reshape(8, D)


def chunk_back(v):
    return jnp.transpose(v.reshape(8, 4, 32, 8), (0, 2, 1, 3)).reshape(8, D)


def swap(x):
    return lax.ppermute(x, "c", [(0, 1), (1, 0)])


def shards(
    hidden,
    lengths,
    teacher,
    norm_gain,
    final_gain,
    score_vector,
    query_weight,
    key_matrix,
    value_matrix,
    out_weight,
):
    c = lax.axis_index("c")
    first = c == 0
    at = jnp.stack([lax.axis_index("pb"), lax.axis_index("x")]).astype(jnp.int32)
    tokens = hidden.reshape(ROWS, D)
    lens = lengths[0]
    gain = norm_gain[None]
    fg = final_gain[None]
    sv = score_vector[None]
    cos_np, sin_np = rope_consts()
    cos, sin = jnp.asarray(cos_np), jnp.asarray(sin_np)
    turned_out = out_weight.T
    halves = [
        jnp.concatenate(
            [
                key_matrix[:, h * 256 : h * 256 + 256],
                value_matrix[:, h * 256 : h * 256 + 256],
                query_weight[:, h * 512 : h * 512 + 512],
                turned_out[:, h * 512 : h * 512 + 512],
            ],
            axis=1,
        )
        for h in range(2)
    ]
    mine = jnp.where(first, halves[0], halves[1])
    theirs = swap(jnp.where(first, halves[1], halves[0]))
    block = jnp.concatenate(
        [jnp.where(first, mine, theirs), jnp.where(first, theirs, mine)], axis=0
    )
    wide = jnp.concatenate([block[:, 0:512], block[:, 1024:1536], block[:, 512:1024]], axis=1)
    column = everyone(wide, "z", 8).reshape(64, 1536)
    normed, turned, nlast, xlast = call(
        prep_body,
        [lens],
        [tokens, gain],
        [((ROWS, D), BF16), ((D, ROWS), BF16), ((8, D), BF16), ((8, D), F32)],
        flops=10_000_000,
    )
    column, normed, turned, nlast, xlast, lens_late, teach_late = lax.optimization_barrier(
        (column, normed, turned, nlast, xlast, lens, teacher[0])
    )
    lens_both = jnp.concatenate([lens_late, swap(lens_late)])
    teach = jnp.concatenate([teach_late, swap(teach_late)])
    teach = jnp.broadcast_to(teach[:, None], (8, HW))
    other, turned_other = swap(normed), swap(turned)
    nlast = chunk_turn(jnp.concatenate([nlast[0:PAIRS], swap(nlast)[0:PAIRS]], axis=0))
    xlast = jnp.concatenate([xlast[0:PAIRS], swap(xlast)[0:PAIRS]], axis=0)
    slab_b = everyone(column[:, 1024:1536], "pb", 4).reshape(256, 512)
    ring_a = from_ring(column[:, 0:1024], "x")
    (slab_a,) = call(arrange_body, [at], ring_a, [((8, 4, 8, 1024), BF16)])
    slab_a, slab_b = lax.optimization_barrier((slab_a, slab_b))
    slab_a = slab_a.reshape(256, 1024)
    qa = from_ring(slab_b, "x")
    kva = everyone(slab_a[:, 0:512], "pb", 4).reshape(1024, 512)
    oa = from_ring(slab_a[:, 512:1024], "pb")

    kproj, krot, vcast, qproj, qrot, attn, ctx = call(
        attend_body,
        [at, lens_both],
        [normed, other, nlast, cos, sin, kva, *qa],
        [
            ((2 * ROWS, 256), F32),
            ((2 * ROWS, 256), BF16),
            ((2 * ROWS, 256), BF16),
            ((8, 512), F32),
            ((8, 512), BF16),
            ((64, SEQ), F32),
            ((8, 512), BF16),
        ],
        [((8, 512), F32), ((8, 512), F32)],
        flops=1_100_000_000,
    )
    (attended,) = call(attended_body, [at], [ctx, *oa], [((8, D), F32)], flops=10_000_000)
    unit, oscale, score, tot, line = call(
        score_body,
        [],
        [teach, attended, swap(attended), xlast, fg, sv],
        [((8, D), F32), ((8, HW), F32), ((8, HW), F32), ((8, HW), F32), ((1, PAIRS), F32)],
        flops=1_000_000,
    )

    totals = everyone(tot[0:1], AXES, 256).reshape(256, HW)

    gkv, gq, gr, last, send = call(
        unit_back_body,
        [at, lens_both],
        [krot, vcast, kproj, qproj, qrot, attn, unit, oscale, fg, sv, cos, sin, *oa, *qa, kva],
        [((2 * ROWS, 512), F32), ((8, 512), F32), ((8, D), F32), ((8, D), F32), ((ROWS, D), BF16)],
        [((8, 512), F32), ((8, 512), F32), ((8, 512), F32), ((8, D), BF16)],
        flops=200_000_000,
    )
    grturn = chunk_turn(gr)
    last = chunk_back(last)
    got = swap(send)

    pieces = ((4, 256, 768), BF16)
    chip_a, *rest = call(
        weight_body,
        [at],
        [totals, score, teach, gkv, gq, gr, grturn, turned, turned_other, nlast, ctx],
        [pieces]
        + [((256, 768), BF16)] * 4
        + [((1, 1), F32), ((ROWS * 2, 512), BF16), ((8, HW), F32), ((8, D), F32)],
        [((8, D), BF16), ((8, D), BF16), pieces, ((8, 512), BF16)],
        flops=1_100_000_000,
    )
    chip_b, (loss, skv, g, sr) = rest[0:4], rest[4:]
    got_a = lax.all_to_all(chip_a, "pb", 0, 0, tiled=True)
    got_b = along_ring(chip_b, "x")
    (grad_hidden,) = call(
        hidden_body,
        [lens_both],
        [tokens, gain, skv, g, last, swap(last), sr, kva, got],
        [((ROWS, D), BF16)],
        flops=600_000_000,
    )
    got_a, got_b, grad_hidden = lax.optimization_barrier((got_a, got_b, grad_hidden))
    *mid_a, mid_b = call(
        middle_body,
        [at],
        [got_a, *got_b],
        [((64, 768), BF16)] * 4 + [((256, 768), BF16)],
        [((8, 4, 8, 768), F32)],
    )
    done_a = along_ring(mid_a, "x")
    done_b = lax.all_to_all(mid_b.reshape(4, 64, 768), "pb", 0, 0, tiled=True)

    def added(parts):
        total = parts[0].astype(F32)
        for part in parts[1:]:
            total = total + part.astype(F32)
        return total.astype(BF16)

    part = jnp.concatenate([added(done_a), added(done_b)], axis=1)
    rec = lax.all_to_all(part.reshape(8, 8, 1536), "z", 0, 0, tiled=True)
    rec = jnp.sum(rec.astype(F32), axis=0)
    reduced = jnp.concatenate(
        [rec[:, 0:512], rec[:, 768:1280], rec[:, 512:768], rec[:, 1280:1536]], axis=1
    )

    keep = jnp.where(first, reduced[0:4], reduced[4:8])
    got = swap(jnp.where(first, reduced[4:8], reduced[0:4]))
    low = jnp.where(first, keep, got)
    high = jnp.where(first, got, keep)

    def both(a, b):
        return jnp.concatenate([low[:, a:b], high[:, a:b]], axis=1)

    return (
        line,
        loss.reshape(()),
        grad_hidden.reshape(hidden.shape),
        both(512, 1024),
        both(0, 256),
        both(256, 512),
        both(1024, 1536).T,
    )


def solution(mesh):
    torus = Mesh(mesh.devices.reshape(mesh.shape["pb"], 8, 4, 2), AXES)
    placed = (
        P("pb", NEG, None, None),
        P("pb", NEG),
        P("pb", NEG),
        P(),
        P(),
        P(),
        P(AXES, None),
        P(AXES, None),
        P(AXES, None),
        P(None, AXES),
    )
    return jax.shard_map(
        shards,
        mesh=torus,
        in_specs=placed,
        out_specs=(
            P("pb", NEG),
            P(),
            P("pb", NEG, None, None),
            P(AXES, None),
            P(AXES, None),
            P(AXES, None),
            P(None, AXES),
        ),
        check_vma=False,
    )
```

```python
import jax
import jax.numpy as jnp
import numpy as np
from jax import lax
from jax.experimental import pallas as pl
from jax.experimental.pallas import tpu as pltpu
from jax.sharding import Mesh
from jax.sharding import PartitionSpec as P

HW = 128
AXES = ("pb", "z", "x", "c")
NEG = ("z", "x", "c")
EPS = 1e-06
ROPE_BASE = 1000000.0
GRAD_SCALE = 512.0
PAIRS = 4
SEQ = 128
D = 1024
ROWS = PAIRS * SEQ
BOTH = 2 * PAIRS
F32 = jnp.float32
BF16 = jnp.bfloat16
SM = pl.BlockSpec(memory_space=pltpu.SMEM)
LAST = (((1,), (1,)), ((), ()))
FIRST = (((0,), (0,)), ((), ()))
SCALE = HW ** (-0.5)


def rope_consts():
    freqs = np.float32(ROPE_BASE) ** (-(np.arange(HW // 2, dtype=np.float32) * 2.0) / HW)
    angles = np.arange(SEQ, dtype=np.float32)[:, None] * freqs.astype(np.float32)[None, :]
    angles = np.concatenate([angles, angles], axis=1)
    sign = np.where(np.arange(HW) < HW // 2, -1.0, 1.0)
    return (
        np.cos(angles).astype(np.float32),
        (np.sin(angles) * sign[None, :]).astype(np.float32),
    )


def whole(shape):
    return pl.BlockSpec(shape, lambda i: (0,) * len(shape), pipeline_mode=pl.Buffered(1))


def call(body, scalars, arrays, outs, scratch=(), flops=0, grant=52, light=False):
    moved = sum(a.size * a.dtype.itemsize for a in arrays)
    moved += sum(int(np.prod(o)) * np.dtype(d).itemsize for o, d in outs)
    if light:
        moved = flops = 1024
    return pl.pallas_call(
        body,
        grid=(1,),
        out_shape=[jax.ShapeDtypeStruct(o, d) for o, d in outs],
        in_specs=[SM] * len(scalars) + [whole(a.shape) for a in arrays],
        out_specs=[whole(o) for o, _ in outs],
        scratch_shapes=[pltpu.VMEM(o, d) for o, d in scratch],
        compiler_params=pltpu.CompilerParams(vmem_limit_bytes=grant << 20),
        cost_estimate=pl.CostEstimate(flops=flops, bytes_accessed=moved, transcendentals=0),
    )(*scalars, *arrays)


def block_at(me, step, width):
    return pl.ds(pl.multiple_of(lax.rem(me + step + 4, 4) * width, width), width)


def dot(a, b, dims=(((1,), (0,)), ((), ()))):
    return lax.dot_general(a, b, dims, preferred_element_type=F32)


def half_turn(v):
    return pltpu.roll(v, HW // 2, 1)


def heads(v, n):
    return [v[:, i * HW : (i + 1) * HW] for i in range(n)]


def block_mask():
    row = lax.broadcasted_iota(jnp.int32, (8, 256), 0)
    lane = lax.broadcasted_iota(jnp.int32, (8, 256), 1)
    return (lane // HW) == (row // 2), (row % 2) == 0


def to_blocks(row, mask, even):
    h = heads(row, 4)
    e = jnp.broadcast_to(jnp.concatenate(h[0::2], axis=1), (8, 256))
    o = jnp.broadcast_to(jnp.concatenate(h[1::2], axis=1), (8, 256))
    return jnp.where(mask, jnp.where(even, e, o), 0.0)


def from_blocks(blocks, mask, even):
    e = jnp.sum(jnp.where(mask & even, blocks, 0.0), axis=0, keepdims=True)
    o = jnp.sum(jnp.where(mask & (~even), blocks, 0.0), axis=0, keepdims=True)
    return jnp.concatenate([e[:, 0:HW], o[:, 0:HW], e[:, HW:], o[:, HW:]], axis=1)


def query_tables(len_ref, cos_ref, sin_ref):
    return [
        jnp.concatenate([t[pl.ds(len_ref[p] - 1, 1), :] for p in range(BOTH)], axis=0)
        for t in (cos_ref, sin_ref)
    ]


def prep_body(len_ref, h_ref, gain_ref, normed_ref, turned_ref, nlast_ref, xlast_ref):
    row = lax.broadcasted_iota(jnp.int32, (8, SEQ), 0)
    lane = lax.broadcasted_iota(jnp.int32, (8, SEQ), 1)
    nl = jnp.zeros((8, D), F32)
    xl = jnp.zeros((8, D), F32)
    for p in range(PAIRS):
        raw = h_ref[p * SEQ : (p + 1) * SEQ, :]
        x = raw.astype(F32)
        inv = lax.rsqrt(jnp.mean(x * x, axis=-1, keepdims=True) + EPS)
        n = (x * inv * gain_ref[...]).astype(BF16)
        normed_ref[p * SEQ : (p + 1) * SEQ, :] = n
        turned_ref[:, p * SEQ : (p + 1) * SEQ] = n.T
        e = len_ref[p] - 1
        hot = jnp.where((row == p) & (lane == e), 1.0, 0.0).astype(BF16)
        nl = nl + dot(hot, n)
        xl = xl + dot(hot, raw)
    nlast_ref[...] = nl.astype(BF16)
    xlast_ref[...] = xl


def arrange_body(at_ref, *refs):
    a_refs, out_ref = refs[0:4], refs[4]
    x = at_ref[1]
    for d in range(4):
        out_ref[:, pl.ds(lax.rem(x - d + 4, 4), 1)] = a_refs[d][...].reshape(8, 1, 8, 768)


def attend_body(
    at_ref, len_ref, normed_ref, other_ref, nlast_ref, cos_ref, sin_ref, kv_ref, *refs
):
    q_refs = refs[0:4]
    kproj_ref, krot_ref, vcast_ref, qproj_ref, qrot_ref, attn_ref, ctx_ref, qr_scr, ctx_scr = refs[4:]
    x = at_ref[1]
    mask, even = block_mask()
    lane = lax.broadcasted_iota(jnp.int32, (8, SEQ), 1)
    for side, rows_ref in enumerate((normed_ref, other_ref)):

        @pl.loop(0, 2)
        def _(i):
            src = pl.ds(pl.multiple_of(i * 256, 256), 256)
            dst = pl.ds(pl.multiple_of(side * ROWS + i * 256, 256), 256)
            kv = dot(rows_ref[src, :], kv_ref[:, 0:512])
            kproj_ref[dst, :] = kv[:, 0:256]
            vcast_ref[dst, :] = kv[:, 256:512].astype(BF16)

    q = jnp.zeros((8, 512), F32)
    for d in range(4):
        q = q + dot(nlast_ref[:, block_at(x, -d, 256)], q_refs[d][:, 0:512])
    qproj_ref[...] = q
    cos_q, sin_q = query_tables(len_ref, cos_ref, sin_ref)
    for h in range(4):
        q = qproj_ref[:, h * HW : (h + 1) * HW]
        u = q * lax.rsqrt(jnp.mean(q * q, axis=-1, keepdims=True) + EPS)
        r = u * cos_q + half_turn(u) * sin_q
        qr_scr[:, h * HW : (h + 1) * HW] = r
        qrot_ref[:, h * HW : (h + 1) * HW] = r.astype(BF16)
    for p in range(BOTH):
        rows = slice(p * SEQ, (p + 1) * SEQ)
        for g in range(2):
            k = kproj_ref[rows, g * HW : (g + 1) * HW]
            u = k * lax.rsqrt(jnp.mean(k * k, axis=-1, keepdims=True) + EPS)
            r = u * cos_ref[...] + half_turn(u) * sin_ref[...]
            krot_ref[rows, g * HW : (g + 1) * HW] = r.astype(BF16)
        qb = to_blocks(qr_scr[p : p + 1, :], mask, even).astype(BF16)
        logits = dot(qb, krot_ref[rows, :], LAST) * SCALE
        ex = jnp.where(lane <= len_ref[p] - 1, jnp.exp(logits), 0.0)
        w = ex / jnp.sum(ex, axis=-1, keepdims=True)
        attn_ref[p * 8 : (p + 1) * 8, :] = w
        c = dot(w.astype(BF16), vcast_ref[rows, :])
        ctx_scr[p : p + 1, :] = from_blocks(c, mask, even)
    ctx_ref[...] = ctx_scr[...].astype(BF16)


def attended_body(at_ref, ctx_ref, kvo_ref, *refs):
    qo_refs, out_ref, o_ref, turn_scr = refs[0:4], refs[4], refs[5], refs[6]
    for d in range(4):
        turn_scr[:, pl.ds(lax.rem(at_ref[1] - d + 4, 4), 1)] = qo_refs[d][:, 512:768].reshape(
            32, 1, 8, 256
        )
    o_ref[:, 0:256] = kvo_ref[:, 512:768]
    o_ref[:, 256:512] = turn_scr[...].reshape(1024, 256)
    out_ref[...] = dot(ctx_ref[...], o_ref[...], LAST)


def score_body(teach_ref, mine_ref, theirs_ref, xlast_ref, fg_ref, sv_ref, *refs):
    unit_ref, oscale_ref, score_ref, tot_ref, line_ref = refs
    res = xlast_ref[...] + (mine_ref[...] + pltpu.roll(theirs_ref[...], PAIRS, 0))
    sc = lax.rsqrt(jnp.mean(res * res, axis=-1, keepdims=True) + EPS)
    unit = res * sc
    unit_ref[...] = unit
    oscale_ref[...] = jnp.broadcast_to(sc, (8, HW))
    s = jnp.sum(unit * fg_ref[...] * sv_ref[...], axis=-1, keepdims=True)
    s = jnp.broadcast_to(s, (8, HW))
    score_ref[...] = s
    row = lax.broadcasted_iota(jnp.int32, (8, HW), 0)
    lane = lax.broadcasted_iota(jnp.int32, (8, HW), 1)
    line_ref[...] = jnp.sum(jnp.where(row == lane, s, 0.0), axis=0, keepdims=True)[:, 0:PAIRS]
    scaled = teach_ref[...] / 2.0
    es = jnp.exp(s)
    et = jnp.exp(scaled)
    v = jnp.where(lane == 0, es, jnp.where(lane == 1, et, et * (scaled - s)))
    v = jnp.where((row < PAIRS) & (lane < 3), v, 0.0)
    tot_ref[...] = jnp.broadcast_to(jnp.sum(v, axis=0, keepdims=True), (8, HW))


def unit_back_body(
    at_ref,
    len_ref,
    krot_ref,
    vcast_ref,
    kproj_ref,
    qproj_ref,
    qrot_ref,
    attn_ref,
    unit_ref,
    oscale_ref,
    fg_ref,
    sv_ref,
    cos_ref,
    sin_ref,
    *refs,
):
    o_ref, q_refs, kv_ref = refs[0], refs[1:5], refs[5]
    gkv_ref, gq_ref, gr_ref, last_ref, send_ref, gc_scr, gq_scr, qr_scr = refs[6:]
    mask, even = block_mask()
    unit = unit_ref[...]
    gu = sv_ref[...] * fg_ref[...]
    gr = oscale_ref[:, 0:1] * (gu - unit * jnp.mean(gu * unit, axis=-1, keepdims=True))
    gr_ref[...] = gr
    gc_scr[...] = dot(gr.astype(BF16), o_ref[...])
    qr_scr[...] = qrot_ref[...].astype(F32)
    for p in range(BOTH):
        rows = slice(p * SEQ, (p + 1) * SEQ)
        gb = to_blocks(gc_scr[p : p + 1, :], mask, even).astype(BF16)
        qb = to_blocks(qr_scr[p : p + 1, :], mask, even).astype(BF16)
        w = attn_ref[p * 8 : (p + 1) * 8, :]
        gp = dot(gb, vcast_ref[rows, :], LAST)
        gkv_ref[rows, 256:512] = dot(w.astype(BF16), gb, FIRST)
        spread = jnp.sum(w * gp, axis=-1, keepdims=True)
        dl = (w * (gp - spread)).astype(BF16)
        gq_scr[p : p + 1, :] = from_blocks(dot(dl, krot_ref[rows, :]) * SCALE, mask, even)
        gk = dot(dl, qb, FIRST) * SCALE
        for g in range(2):
            cols = slice(g * HW, (g + 1) * HW)
            k = kproj_ref[rows, cols]
            sc = lax.rsqrt(jnp.mean(k * k, axis=-1, keepdims=True) + EPS)
            u = k * sc
            r = gk[:, cols]
            t = r * cos_ref[...] + half_turn(r * sin_ref[...])
            gkv_ref[rows, cols] = sc * (t - u * jnp.mean(t * u, axis=-1, keepdims=True))
    cos_q, sin_q = query_tables(len_ref, cos_ref, sin_ref)
    for h in range(4):
        q = qproj_ref[:, h * HW : (h + 1) * HW]
        sc = lax.rsqrt(jnp.mean(q * q, axis=-1, keepdims=True) + EPS)
        u = q * sc
        r = gq_scr[:, h * HW : (h + 1) * HW]
        t = r * cos_q + half_turn(r * sin_q)
        gq_ref[:, h * HW : (h + 1) * HW] = sc * (
            t - u * jnp.mean(t * u, axis=-1, keepdims=True)
        )
    gqb = gq_ref[...].astype(BF16)
    for d in range(4):
        last_ref[:, block_at(at_ref[1], -d, 256)] = dot(gqb, q_refs[d][:, 0:512], LAST)

    @pl.loop(0, 2)
    def _(i):
        src = pl.ds(pl.multiple_of(ROWS + i * 256, 256), 256)
        gn = dot(gkv_ref[src, :].astype(BF16), kv_ref[:, 0:512], LAST)
        send_ref[pl.ds(pl.multiple_of(i * 256, 256), 256), :] = gn.astype(BF16)


def weight_body(
    at_ref,
    tot_ref,
    score_ref,
    teach_ref,
    gkv_ref,
    gq_ref,
    gr_ref,
    grturn_ref,
    turned_ref,
    turned_other_ref,
    nlast_ref,
    ctx_ref,
    *refs,
):
    out_a, outs_b, loss_ref, skv_ref, g_ref, sr_ref = refs[0], refs[1:5], *refs[5:9]
    srow_scr, sturn_scr, b_scr, sq_scr = refs[9:]
    pb, x = at_ref[0], at_ref[1]
    lane = lax.broadcasted_iota(jnp.int32, (1, HW), 1)

    def pick(v, i):
        return jnp.sum(jnp.where(lane == i, v, 0.0), axis=-1, keepdims=True)

    loss = jnp.zeros((1, 1), F32)
    mine = jnp.zeros((1, HW), F32)
    for q in range(4):
        t = jnp.sum(tot_ref[q * 64 : (q + 1) * 64, :], axis=0, keepdims=True)
        ts, tt, cr = pick(t, 0), pick(t, 1), pick(t, 2)
        loss = loss + (cr / tt - jnp.log(tt) + jnp.log(ts))
        mine = mine + jnp.where(pb == q, t, 0.0)
    loss_ref[...] = loss
    ts, tt = pick(mine, 0), pick(mine, 1)
    row = lax.broadcasted_iota(jnp.int32, (8, HW), 0)
    g = GRAD_SCALE * (jnp.exp(score_ref[...]) / ts - jnp.exp(teach_ref[...] / 2.0) / tt)
    gcol = g[:, 0:1]
    sr = gr_ref[...] * gcol
    sr_ref[...] = sr
    g_ref[...] = g
    sq_scr[...] = (gq_ref[...] * gcol).astype(BF16)
    srow_scr[...] = sr.astype(BF16)
    sturn_scr[...] = (grturn_ref[...] * gcol).astype(BF16)
    for p in range(BOTH):
        rows = slice(p * SEQ, (p + 1) * SEQ)
        skv_ref[rows, :] = (gkv_ref[rows, :] * gcol[p : p + 1, :]).astype(BF16)

    @pl.loop(0, 4)
    def _(i):
        rows = pl.ds(pl.multiple_of(i * 256, 256), 256)
        kv = dot(turned_ref[rows, :], skv_ref[0:ROWS, :]) + dot(
            turned_other_ref[rows, :], skv_ref[ROWS : 2 * ROWS, :]
        )
        o_low = dot(srow_scr[:, rows], ctx_ref[:, 0:256], FIRST)
        rows_x = block_at(x, i, 256)
        q = dot(nlast_ref[:, rows_x], sq_scr[...], FIRST)
        o_high = dot(sturn_scr[:, rows_x], ctx_ref[:, 256:512], FIRST)
        here = pl.ds(i, 1)
        out_a[here, :, 0:512] = kv.astype(BF16)[None]
        out_a[here, :, 512:768] = o_low.astype(BF16)[None]
        b_scr[here, :, 0:512] = q.astype(BF16)[None]
        b_scr[here, :, 512:768] = o_high.astype(BF16)[None]

    for d in range(4):
        outs_b[d][...] = b_scr[d]


def middle_body(at_ref, got_a_ref, *refs):
    b_refs, out_a, out_b, a_scr = refs[0:4], refs[4:8], refs[8], refs[9]
    x = at_ref[1]
    total_a = got_a_ref[0].astype(F32)
    total_b = b_refs[0][...].astype(F32)
    for d in range(1, 4):
        total_a = total_a + got_a_ref[d].astype(F32)
        total_b = total_b + b_refs[d][...].astype(F32)
    out_b[...] = total_b.astype(BF16)
    a_scr[...] = total_a.reshape(8, 4, 8, 768)
    for d in range(4):
        out_a[d][...] = a_scr[:, pl.ds(lax.rem(x + d, 4), 1)].reshape(64, 768).astype(BF16)


def hidden_body(len_ref, h_ref, gain_ref, skv_ref, g_ref, last_ref, other_ref, sr_ref, kv_ref, got_ref, out_ref):
    pos = lax.broadcasted_iota(jnp.int32, (SEQ, 1), 0)

    @pl.loop(0, PAIRS)
    def _(p):
        rows = pl.ds(pl.multiple_of(p * SEQ, SEQ), SEQ)
        at = pos == len_ref[p] - 1
        last = last_ref[pl.ds(p, 1), :] + other_ref[pl.ds(PAIRS + p, 1), :]
        unit = got_ref[rows, :].astype(F32) + jnp.where(at, last, 0.0)
        gn = dot(skv_ref[rows, :], kv_ref[:, 0:512], LAST) + g_ref[pl.ds(p, 1), 0:1] * unit
        x = h_ref[rows, :].astype(F32)
        inv = lax.rsqrt(jnp.mean(x * x, axis=-1, keepdims=True) + EPS)
        s = gn * gain_ref[...]
        gi = inv * s - x * (inv * inv * inv * jnp.mean(s * x, axis=-1, keepdims=True))
        gi = gi + jnp.where(at, sr_ref[pl.ds(p, 1), :], 0.0)
        out_ref[rows, :] = gi.astype(BF16)


def finish_body(rec_ref, gq_ref, gk_ref, gv_ref, go_ref):
    for h in range(2):
        total = rec_ref[0, h].astype(F32)
        for z in range(1, 8):
            total = total + rec_ref[z, h].astype(F32)
        gk_ref[:, h * 256 : h * 256 + 256] = total[:, 0:256]
        gv_ref[:, h * 256 : h * 256 + 256] = total[:, 256:512]
        go_ref[:, h * 512 : h * 512 + 256] = total[:, 512:768]
        gq_ref[:, h * 512 : h * 512 + 512] = total[:, 768:1280]
        go_ref[:, h * 512 + 256 : h * 512 + 512] = total[:, 1280:1536]


def everyone(x, axes, count):
    return lax.all_to_all(
        jnp.broadcast_to(x[None], (count, *x.shape)), axes, 0, 0, tiled=True
    )


def from_ring(x, axis):
    return [x] + [
        lax.ppermute(x, axis, [(i, (i + d) % 4) for i in range(4)]) for d in range(1, 4)
    ]


def along_ring(pieces, axis):
    return [pieces[0]] + [
        lax.ppermute(pieces[d], axis, [(i, (i + d) % 4) for i in range(4)]) for d in range(1, 4)
    ]


def chunk_turn(v):
    return jnp.transpose(v.reshape(8, 32, 4, 8), (0, 2, 1, 3)).reshape(8, D)


def chunk_back(v):
    return jnp.transpose(v.reshape(8, 4, 32, 8), (0, 2, 1, 3)).reshape(8, D)


def swap(x):
    return lax.ppermute(x, "c", [(0, 1), (1, 0)])


def shards(
    hidden,
    lengths,
    teacher,
    norm_gain,
    final_gain,
    score_vector,
    query_weight,
    key_matrix,
    value_matrix,
    out_weight,
):
    at = jnp.stack([lax.axis_index("pb"), lax.axis_index("x")]).astype(jnp.int32)
    tokens = hidden.reshape(ROWS, D)
    lens = lengths[0]
    gain = norm_gain[None]
    fg = final_gain[None]
    sv = score_vector[None]
    cos_np, sin_np = rope_consts()
    cos, sin = jnp.asarray(cos_np), jnp.asarray(sin_np)
    turned_out = out_weight.T
    halves = [
        jnp.concatenate(
            [
                key_matrix[:, h * 256 : h * 256 + 256],
                value_matrix[:, h * 256 : h * 256 + 256],
                turned_out[:, h * 512 : h * 512 + 256],
                query_weight[:, h * 512 : h * 512 + 512],
                turned_out[:, h * 512 + 256 : h * 512 + 512],
            ],
            axis=1,
        )
        for h in range(2)
    ]
    both_halves = jnp.broadcast_to(jnp.stack(halves)[None], (8, 2, 4, 1536)).reshape(16, 4, 1536)
    column = lax.all_to_all(both_halves, ("z", "c"), 0, 0, tiled=True).reshape(64, 1536)
    normed, turned, nlast, xlast = call(
        prep_body,
        [lens],
        [tokens, gain],
        [((ROWS, D), BF16), ((D, ROWS), BF16), ((8, D), BF16), ((8, D), F32)],
        flops=10_000_000,
    )
    nlast = chunk_turn(nlast)
    wide = (PAIRS, HW)
    pack = jnp.concatenate(
        [
            xlast[0:PAIRS],
            nlast[0:PAIRS].astype(F32),
            jnp.broadcast_to(lens.astype(F32)[:, None], wide),
            jnp.broadcast_to(teacher[0][:, None], wide),
        ],
        axis=1,
    )
    column, normed, turned, pack = lax.optimization_barrier((column, normed, turned, pack))
    other = swap(normed)
    got = swap(pack)
    slab_b = everyone(column[:, 768:1536], "pb", 4).reshape(256, 768)
    ring_a = from_ring(column[:, 0:768], "x")
    (slab_a,) = call(arrange_body, [at], ring_a, [((8, 4, 8, 768), BF16)])
    slab_a, slab_b, other, got = lax.optimization_barrier((slab_a, slab_b, other, got))
    packed = jnp.concatenate([pack, got], axis=0)
    xlast = packed[:, 0:1024]
    nlast = packed[:, 1024:2048].astype(BF16)
    lens_both = packed[:, 2048].astype(jnp.int32)
    teach = packed[:, 2048 + HW :]
    kvo = everyone(slab_a.reshape(256, 768), "pb", 4).reshape(1024, 768)
    qo = from_ring(slab_b, "x")

    kproj, krot, vcast, qproj, qrot, attn, ctx = call(
        attend_body,
        [at, lens_both],
        [normed, other, nlast, cos, sin, kvo, *qo],
        [
            ((2 * ROWS, 256), F32),
            ((2 * ROWS, 256), BF16),
            ((2 * ROWS, 256), BF16),
            ((8, 512), F32),
            ((8, 512), BF16),
            ((64, SEQ), F32),
            ((8, 512), BF16),
        ],
        [((8, 512), F32), ((8, 512), F32)],
        flops=1_100_000_000,
    )
    ctx, turned_late = lax.optimization_barrier((ctx, turned))
    turned_other = swap(turned_late)
    attended, oa = call(
        attended_body,
        [at],
        [ctx, kvo, *qo],
        [((8, D), F32), ((D, 512), BF16)],
        [((32, 4, 8, 256), BF16)],
        flops=10_000_000,
    )
    unit, oscale, score, tot, line = call(
        score_body,
        [],
        [teach, attended, swap(attended), xlast, fg, sv],
        [((8, D), F32), ((8, HW), F32), ((8, HW), F32), ((8, HW), F32), ((1, PAIRS), F32)],
        flops=1_000_000,
    )

    totals = everyone(tot[0:1], AXES, 256).reshape(256, HW)

    gkv, gq, gr, last, send = call(
        unit_back_body,
        [at, lens_both],
        [krot, vcast, kproj, qproj, qrot, attn, unit, oscale, fg, sv, cos, sin, oa, *qo, kvo],
        [((2 * ROWS, 512), F32), ((8, 512), F32), ((8, D), F32), ((8, D), F32), ((ROWS, D), BF16)],
        [((8, 512), F32), ((8, 512), F32), ((8, 512), F32)],
        flops=200_000_000,
    )
    grturn = chunk_turn(gr)
    last = chunk_back(last)
    got = swap(send)

    pieces = ((4, 256, 768), BF16)
    chip_a, *rest = call(
        weight_body,
        [at],
        [totals, score, teach, gkv, gq, gr, grturn, turned, turned_other, nlast, ctx],
        [pieces]
        + [((256, 768), BF16)] * 4
        + [((1, 1), F32), ((ROWS * 2, 512), BF16), ((8, HW), F32), ((8, D), F32)],
        [((8, D), BF16), ((8, D), BF16), pieces, ((8, 512), BF16)],
        flops=1_100_000_000,
    )
    chip_b, (loss, skv, g, sr) = rest[0:4], rest[4:]
    got_a = lax.all_to_all(chip_a, "pb", 0, 0, tiled=True)
    got_b = along_ring(chip_b, "x")
    (grad_hidden,) = call(
        hidden_body,
        [lens_both],
        [tokens, gain, skv, g, last, swap(last), sr, kvo, got],
        [((ROWS, D), BF16)],
        flops=600_000_000,
    )
    got_a, got_b, grad_hidden = lax.optimization_barrier((got_a, got_b, grad_hidden))
    *mid_a, mid_b = call(
        middle_body,
        [at],
        [got_a, *got_b],
        [((64, 768), BF16)] * 4 + [((256, 768), BF16)],
        [((8, 4, 8, 768), F32)],
    )
    done_a = along_ring(mid_a, "x")
    done_b = lax.all_to_all(mid_b.reshape(4, 64, 768), "pb", 0, 0, tiled=True)

    def added(parts):
        total = parts[0].astype(F32)
        for part in parts[1:]:
            total = total + part.astype(F32)
        return total.astype(BF16)

    part = jnp.concatenate([added(done_a), added(done_b)], axis=1)
    rec = lax.all_to_all(part.reshape(16, 4, 1536), ("z", "c"), 0, 0, tiled=True)
    grad_query, grad_key, grad_value, grad_out = call(
        finish_body,
        [],
        [rec.reshape(8, 2, 4, 1536)],
        [((4, D), F32), ((4, 512), F32), ((4, 512), F32), ((4, D), F32)],
    )

    return (
        line,
        loss.reshape(()),
        grad_hidden.reshape(hidden.shape),
        grad_query,
        grad_key,
        grad_value,
        grad_out.T,
    )


def solution(mesh):
    torus = Mesh(mesh.devices.reshape(mesh.shape["pb"], 8, 4, 2), AXES)
    placed = (
        P("pb", NEG, None, None),
        P("pb", NEG),
        P("pb", NEG),
        P(),
        P(),
        P(),
        P(AXES, None),
        P(AXES, None),
        P(AXES, None),
        P(None, AXES),
    )
    return jax.shard_map(
        shards,
        mesh=torus,
        in_specs=placed,
        out_specs=(
            P("pb", NEG),
            P(),
            P("pb", NEG, None, None),
            P(AXES, None),
            P(AXES, None),
            P(AXES, None),
            P(None, AXES),
        ),
        check_vma=False,
    )
```

```python
import jax
import jax.numpy as jnp
import numpy as np
from jax import lax
from jax.experimental import pallas as pl
from jax.experimental.pallas import tpu as pltpu
from jax.sharding import Mesh
from jax.sharding import PartitionSpec as P

HW = 128
AXES = ("pb", "z", "x", "c")
NEG = ("z", "x", "c")
EPS = 1e-06
ROPE_BASE = 1000000.0
GRAD_SCALE = 512.0
PAIRS = 4
SEQ = 128
D = 1024
ROWS = PAIRS * SEQ
BOTH = 2 * PAIRS
F32 = jnp.float32
BF16 = jnp.bfloat16
SM = pl.BlockSpec(memory_space=pltpu.SMEM)
LAST = (((1,), (1,)), ((), ()))
FIRST = (((0,), (0,)), ((), ()))
SCALE = HW ** (-0.5)


def rope_consts():
    freqs = np.float32(ROPE_BASE) ** (-(np.arange(HW // 2, dtype=np.float32) * 2.0) / HW)
    angles = np.arange(SEQ, dtype=np.float32)[:, None] * freqs.astype(np.float32)[None, :]
    angles = np.concatenate([angles, angles], axis=1)
    sign = np.where(np.arange(HW) < HW // 2, -1.0, 1.0)
    return (
        np.cos(angles).astype(np.float32),
        (np.sin(angles) * sign[None, :]).astype(np.float32),
    )


def whole(shape):
    return pl.BlockSpec(shape, lambda i: (0,) * len(shape), pipeline_mode=pl.Buffered(1))


def call(body, scalars, arrays, outs, scratch=(), flops=0, grant=52, light=False):
    moved = sum(a.size * a.dtype.itemsize for a in arrays)
    moved += sum(int(np.prod(o)) * np.dtype(d).itemsize for o, d in outs)
    if light:
        moved = flops = 1024
    return pl.pallas_call(
        body,
        grid=(1,),
        out_shape=[jax.ShapeDtypeStruct(o, d) for o, d in outs],
        in_specs=[SM] * len(scalars) + [whole(a.shape) for a in arrays],
        out_specs=[whole(o) for o, _ in outs],
        scratch_shapes=[pltpu.VMEM(o, d) for o, d in scratch],
        compiler_params=pltpu.CompilerParams(vmem_limit_bytes=grant << 20),
        cost_estimate=pl.CostEstimate(flops=flops, bytes_accessed=moved, transcendentals=0),
    )(*scalars, *arrays)


def block_at(me, step, width):
    return pl.ds(pl.multiple_of(lax.rem(me + step + 4, 4) * width, width), width)


def dot(a, b, dims=(((1,), (0,)), ((), ()))):
    return lax.dot_general(a, b, dims, preferred_element_type=F32)


def half_turn(v):
    return pltpu.roll(v, HW // 2, 1)


def heads(v, n):
    return [v[:, i * HW : (i + 1) * HW] for i in range(n)]


def block_mask():
    row = lax.broadcasted_iota(jnp.int32, (8, 256), 0)
    lane = lax.broadcasted_iota(jnp.int32, (8, 256), 1)
    return (lane // HW) == (row // 2), (row % 2) == 0


def to_blocks(row, mask, even):
    h = heads(row, 4)
    e = jnp.broadcast_to(jnp.concatenate(h[0::2], axis=1), (8, 256))
    o = jnp.broadcast_to(jnp.concatenate(h[1::2], axis=1), (8, 256))
    return jnp.where(mask, jnp.where(even, e, o), 0.0)


def from_blocks(blocks, mask, even):
    e = jnp.sum(jnp.where(mask & even, blocks, 0.0), axis=0, keepdims=True)
    o = jnp.sum(jnp.where(mask & (~even), blocks, 0.0), axis=0, keepdims=True)
    return jnp.concatenate([e[:, 0:HW], o[:, 0:HW], e[:, HW:], o[:, HW:]], axis=1)


def query_tables(len_ref, cos_ref, sin_ref):
    return [
        jnp.concatenate([t[pl.ds(len_ref[p] - 1, 1), :] for p in range(BOTH)], axis=0)
        for t in (cos_ref, sin_ref)
    ]


def pack_body(k_ref, v_ref, q_ref, o_ref, out_ref):
    for h in range(2):
        wide, tall = slice(h * 256, h * 256 + 256), h * 512
        out_ref[0, h, :, 0:256] = k_ref[:, wide]
        out_ref[0, h, :, 256:512] = v_ref[:, wide]
        out_ref[0, h, :, 512:768] = o_ref[:, tall : tall + 256]
        out_ref[0, h, :, 768:1280] = q_ref[:, tall : tall + 512]
        out_ref[0, h, :, 1280:1536] = o_ref[:, tall + 256 : tall + 512]
    for z in range(1, 8):
        out_ref[z] = out_ref[0]


def prep_body(len_ref, h_ref, gain_ref, normed_ref, turned_ref, nlast_ref, xlast_ref):
    row = lax.broadcasted_iota(jnp.int32, (8, SEQ), 0)
    lane = lax.broadcasted_iota(jnp.int32, (8, SEQ), 1)
    nl = jnp.zeros((8, D), F32)
    xl = jnp.zeros((8, D), F32)
    for p in range(PAIRS):
        raw = h_ref[p * SEQ : (p + 1) * SEQ, :]
        x = raw.astype(F32)
        inv = lax.rsqrt(jnp.mean(x * x, axis=-1, keepdims=True) + EPS)
        n = (x * inv * gain_ref[...]).astype(BF16)
        normed_ref[p * SEQ : (p + 1) * SEQ, :] = n
        turned_ref[:, p * SEQ : (p + 1) * SEQ] = n.T
        e = len_ref[p] - 1
        hot = jnp.where((row == p) & (lane == e), 1.0, 0.0).astype(BF16)
        nl = nl + dot(hot, n)
        xl = xl + dot(hot, raw)
    nlast_ref[...] = nl.astype(BF16)
    xlast_ref[...] = xl


def arrange_body(at_ref, *refs):
    a_refs, out_ref, slab_scr = refs[0:4], refs[4], refs[5]
    x = at_ref[1]
    for d in range(4):
        slab_scr[:, pl.ds(lax.rem(x - d + 4, 4), 1)] = a_refs[d][...].reshape(8, 1, 8, 768)
    slab = slab_scr[...].reshape(256, 768)
    for y in range(4):
        out_ref[y] = slab


def attend_body(
    at_ref, len_ref, normed_ref, other_ref, nlast_ref, cos_ref, sin_ref, kv_ref, *refs
):
    out_ref, o_ref, turn_scr = refs[11], refs[12], refs[15]
    q_refs = refs[0:4]
    kproj_ref, krot_ref, vcast_ref, qproj_ref, qrot_ref, attn_ref, ctx_ref = refs[4:11]
    qr_scr, ctx_scr = refs[13:15]
    x = at_ref[1]
    mask, even = block_mask()
    lane = lax.broadcasted_iota(jnp.int32, (8, SEQ), 1)
    for side, rows_ref in enumerate((normed_ref, other_ref)):

        @pl.loop(0, 2)
        def _(i):
            src = pl.ds(pl.multiple_of(i * 256, 256), 256)
            dst = pl.ds(pl.multiple_of(side * ROWS + i * 256, 256), 256)
            kv = dot(rows_ref[src, :], kv_ref[:, 0:512])
            kproj_ref[dst, :] = kv[:, 0:256]
            vcast_ref[dst, :] = kv[:, 256:512].astype(BF16)

    q = jnp.zeros((8, 512), F32)
    for d in range(4):
        q = q + dot(nlast_ref[:, block_at(x, -d, 256)], q_refs[d][:, 0:512])
    qproj_ref[...] = q
    cos_q, sin_q = query_tables(len_ref, cos_ref, sin_ref)
    for h in range(4):
        q = qproj_ref[:, h * HW : (h + 1) * HW]
        u = q * lax.rsqrt(jnp.mean(q * q, axis=-1, keepdims=True) + EPS)
        r = u * cos_q + half_turn(u) * sin_q
        qr_scr[:, h * HW : (h + 1) * HW] = r
        qrot_ref[:, h * HW : (h + 1) * HW] = r.astype(BF16)
    for p in range(BOTH):
        rows = slice(p * SEQ, (p + 1) * SEQ)
        for g in range(2):
            k = kproj_ref[rows, g * HW : (g + 1) * HW]
            u = k * lax.rsqrt(jnp.mean(k * k, axis=-1, keepdims=True) + EPS)
            r = u * cos_ref[...] + half_turn(u) * sin_ref[...]
            krot_ref[rows, g * HW : (g + 1) * HW] = r.astype(BF16)
        qb = to_blocks(qr_scr[p : p + 1, :], mask, even).astype(BF16)
        logits = dot(qb, krot_ref[rows, :], LAST) * SCALE
        ex = jnp.where(lane <= len_ref[p] - 1, jnp.exp(logits), 0.0)
        w = ex / jnp.sum(ex, axis=-1, keepdims=True)
        attn_ref[p * 8 : (p + 1) * 8, :] = w
        c = dot(w.astype(BF16), vcast_ref[rows, :])
        ctx_scr[p : p + 1, :] = from_blocks(c, mask, even)
    ctx_ref[...] = ctx_scr[...].astype(BF16)
    for d in range(4):
        turn_scr[:, pl.ds(lax.rem(x - d + 4, 4), 1)] = q_refs[d][:, 512:768].reshape(32, 1, 8, 256)
    o_ref[:, 0:256] = kv_ref[:, 512:768]
    o_ref[:, 256:512] = turn_scr[...].reshape(1024, 256)
    out_ref[...] = dot(ctx_ref[...], o_ref[...], LAST)


def score_body(teach_ref, mine_ref, theirs_ref, xlast_ref, fg_ref, sv_ref, *refs):
    unit_ref, oscale_ref, score_ref, tot_ref, line_ref = refs
    res = xlast_ref[...] + (mine_ref[...] + pltpu.roll(theirs_ref[...], PAIRS, 0))
    sc = lax.rsqrt(jnp.mean(res * res, axis=-1, keepdims=True) + EPS)
    unit = res * sc
    unit_ref[...] = unit
    oscale_ref[...] = jnp.broadcast_to(sc, (8, HW))
    s = jnp.sum(unit * fg_ref[...] * sv_ref[...], axis=-1, keepdims=True)
    s = jnp.broadcast_to(s, (8, HW))
    score_ref[...] = s
    row = lax.broadcasted_iota(jnp.int32, (8, HW), 0)
    lane = lax.broadcasted_iota(jnp.int32, (8, HW), 1)
    line_ref[...] = jnp.sum(jnp.where(row == lane, s, 0.0), axis=0, keepdims=True)[:, 0:PAIRS]
    scaled = teach_ref[...] / 2.0
    es = jnp.exp(s)
    et = jnp.exp(scaled)
    v = jnp.where(lane == 0, es, jnp.where(lane == 1, et, et * (scaled - s)))
    v = jnp.where(lane < 3, v + pltpu.roll(v, PAIRS, 0), 0.0)
    tot_ref[...] = jnp.broadcast_to(jnp.sum(v[0:PAIRS], axis=0, keepdims=True)[None], (32, 1, HW))


def unit_back_body(
    at_ref,
    len_ref,
    krot_ref,
    vcast_ref,
    kproj_ref,
    qproj_ref,
    qrot_ref,
    attn_ref,
    unit_ref,
    oscale_ref,
    fg_ref,
    sv_ref,
    cos_ref,
    sin_ref,
    *refs,
):
    o_ref, q_refs, kv_ref = refs[0], refs[1:5], refs[5]
    gkv_ref, gq_ref, gr_ref, last_ref, send_ref, gc_scr, gq_scr, qr_scr = refs[6:]
    mask, even = block_mask()
    unit = unit_ref[...]
    gu = sv_ref[...] * fg_ref[...]
    gr = oscale_ref[:, 0:1] * (gu - unit * jnp.mean(gu * unit, axis=-1, keepdims=True))
    gr_ref[...] = gr
    gc_scr[...] = dot(gr.astype(BF16), o_ref[...])
    qr_scr[...] = qrot_ref[...].astype(F32)
    for p in range(BOTH):
        rows = slice(p * SEQ, (p + 1) * SEQ)
        gb = to_blocks(gc_scr[p : p + 1, :], mask, even).astype(BF16)
        qb = to_blocks(qr_scr[p : p + 1, :], mask, even).astype(BF16)
        w = attn_ref[p * 8 : (p + 1) * 8, :]
        gp = dot(gb, vcast_ref[rows, :], LAST)
        gkv_ref[rows, 256:512] = dot(w.astype(BF16), gb, FIRST)
        spread = jnp.sum(w * gp, axis=-1, keepdims=True)
        dl = (w * (gp - spread)).astype(BF16)
        gq_scr[p : p + 1, :] = from_blocks(dot(dl, krot_ref[rows, :]) * SCALE, mask, even)
        gk = dot(dl, qb, FIRST) * SCALE
        for g in range(2):
            cols = slice(g * HW, (g + 1) * HW)
            k = kproj_ref[rows, cols]
            sc = lax.rsqrt(jnp.mean(k * k, axis=-1, keepdims=True) + EPS)
            u = k * sc
            r = gk[:, cols]
            t = r * cos_ref[...] + half_turn(r * sin_ref[...])
            gkv_ref[rows, cols] = sc * (t - u * jnp.mean(t * u, axis=-1, keepdims=True))
    cos_q, sin_q = query_tables(len_ref, cos_ref, sin_ref)
    for h in range(4):
        q = qproj_ref[:, h * HW : (h + 1) * HW]
        sc = lax.rsqrt(jnp.mean(q * q, axis=-1, keepdims=True) + EPS)
        u = q * sc
        r = gq_scr[:, h * HW : (h + 1) * HW]
        t = r * cos_q + half_turn(r * sin_q)
        gq_ref[:, h * HW : (h + 1) * HW] = sc * (
            t - u * jnp.mean(t * u, axis=-1, keepdims=True)
        )
    gqb = gq_ref[...].astype(BF16)
    for d in range(4):
        last_ref[:, block_at(at_ref[1], -d, 256)] = dot(gqb, q_refs[d][:, 0:512], LAST)

    @pl.loop(0, 2)
    def _(i):
        src = pl.ds(pl.multiple_of(ROWS + i * 256, 256), 256)
        gn = dot(gkv_ref[src, :].astype(BF16), kv_ref[:, 0:512], LAST)
        send_ref[pl.ds(pl.multiple_of(i * 256, 256), 256), :] = gn.astype(BF16)


def weight_body(
    at_ref,
    tot_ref,
    score_ref,
    teach_ref,
    gkv_ref,
    gq_ref,
    gr_ref,
    grturn_ref,
    turned_ref,
    turned_other_ref,
    nlast_ref,
    ctx_ref,
    *refs,
):
    out_a, outs_b, loss_ref, skv_ref, g_ref, sr_ref = refs[0], refs[1:5], *refs[5:9]
    srow_scr, sturn_scr, b_scr, sq_scr = refs[9:]
    x = at_ref[1]
    lane = lax.broadcasted_iota(jnp.int32, (1, HW), 1)

    def pick(v, i):
        return jnp.sum(jnp.where(lane == i, v, 0.0), axis=-1, keepdims=True)

    t = tot_ref[0]
    for i in range(1, 32):
        t = t + tot_ref[i]
    ts, tt, cr = pick(t, 0), pick(t, 1), pick(t, 2)
    loss_ref[...] = jnp.broadcast_to(cr / tt - jnp.log(tt) + jnp.log(ts), (8, HW))
    row = lax.broadcasted_iota(jnp.int32, (8, HW), 0)
    g = GRAD_SCALE * (jnp.exp(score_ref[...]) / ts - jnp.exp(teach_ref[...] / 2.0) / tt)
    gcol = g[:, 0:1]
    sr = gr_ref[...] * gcol
    sr_ref[...] = sr
    g_ref[...] = g
    sq_scr[...] = (gq_ref[...] * gcol).astype(BF16)
    srow_scr[...] = sr.astype(BF16)
    sturn_scr[...] = (grturn_ref[...] * gcol).astype(BF16)
    for p in range(BOTH):
        rows = slice(p * SEQ, (p + 1) * SEQ)
        skv_ref[rows, :] = (gkv_ref[rows, :] * gcol[p : p + 1, :]).astype(BF16)

    @pl.loop(0, 4)
    def _(i):
        rows = pl.ds(pl.multiple_of(i * 256, 256), 256)
        kv = dot(turned_ref[rows, :], skv_ref[0:ROWS, :]) + dot(
            turned_other_ref[rows, :], skv_ref[ROWS : 2 * ROWS, :]
        )
        o_low = dot(srow_scr[:, rows], ctx_ref[:, 0:256], FIRST)
        rows_x = block_at(x, i, 256)
        q = dot(nlast_ref[:, rows_x], sq_scr[...], FIRST)
        o_high = dot(sturn_scr[:, rows_x], ctx_ref[:, 256:512], FIRST)
        here = pl.ds(i, 1)
        out_a[here, :, 0:512] = kv.astype(BF16)[None]
        out_a[here, :, 512:768] = o_low.astype(BF16)[None]
        b_scr[here, :, 0:512] = q.astype(BF16)[None]
        b_scr[here, :, 512:768] = o_high.astype(BF16)[None]

    for d in range(4):
        outs_b[d][...] = b_scr[d]


def middle_body(at_ref, loss_ref, got_a_ref, *refs):
    b_refs, out_a, out_b, a_scr = refs[0:4], refs[4:8], refs[8], refs[9]
    x = at_ref[1]
    total_a = got_a_ref[0].astype(F32)
    total_b = b_refs[0][...].astype(F32)
    for d in range(1, 4):
        total_a = total_a + got_a_ref[d].astype(F32)
        total_b = total_b + b_refs[d][...].astype(F32)
    out_b[:, 0:64, :] = total_b.reshape(4, 64, 768).astype(BF16)
    rest = jnp.broadcast_to(loss_ref[0:1, 0:1], (16, 768))
    lane = lax.broadcasted_iota(jnp.int32, (16, 768), 1)
    parts = jnp.zeros((16, 768), F32)
    for i in range(3):
        part = rest.astype(BF16).astype(F32)
        parts = jnp.where(lane == i, part, parts)
        rest = rest - part
    for y in range(4):
        out_b[y, 64:80, :] = parts.astype(BF16)
    a_scr[...] = total_a.reshape(8, 4, 8, 768)
    for d in range(4):
        out_a[d][...] = a_scr[:, pl.ds(lax.rem(x + d, 4), 1)].reshape(64, 768).astype(BF16)


def hidden_body(len_ref, h_ref, gain_ref, skv_ref, g_ref, last_ref, other_ref, sr_ref, kv_ref, got_ref, out_ref):
    pos = lax.broadcasted_iota(jnp.int32, (SEQ, 1), 0)

    @pl.loop(0, PAIRS)
    def _(p):
        rows = pl.ds(pl.multiple_of(p * SEQ, SEQ), SEQ)
        at = pos == len_ref[p] - 1
        last = last_ref[pl.ds(p, 1), :] + other_ref[pl.ds(PAIRS + p, 1), :]
        unit = got_ref[rows, :].astype(F32) + jnp.where(at, last, 0.0)
        gn = dot(skv_ref[rows, :], kv_ref[:, 0:512], LAST) + g_ref[pl.ds(p, 1), 0:1] * unit
        x = h_ref[rows, :].astype(F32)
        inv = lax.rsqrt(jnp.mean(x * x, axis=-1, keepdims=True) + EPS)
        s = gn * gain_ref[...]
        gi = inv * s - x * (inv * inv * inv * jnp.mean(s * x, axis=-1, keepdims=True))
        gi = gi + jnp.where(at, sr_ref[pl.ds(p, 1), :], 0.0)
        out_ref[rows, :] = gi.astype(BF16)


def finish_body(rec_ref, gq_ref, gk_ref, gv_ref, go_ref):
    for h in range(2):
        total = rec_ref[0, h].astype(F32)
        for z in range(1, 8):
            total = total + rec_ref[z, h].astype(F32)
        gk_ref[:, h * 256 : h * 256 + 256] = total[:, 0:256]
        gv_ref[:, h * 256 : h * 256 + 256] = total[:, 256:512]
        go_ref[:, h * 512 : h * 512 + 256] = total[:, 512:768]
        gq_ref[:, h * 512 : h * 512 + 512] = total[:, 768:1280]
        go_ref[:, h * 512 + 256 : h * 512 + 512] = total[:, 1280:1536]


def everyone(x, axes, count):
    return lax.all_to_all(
        jnp.broadcast_to(x[None], (count, *x.shape)), axes, 0, 0, tiled=True
    )


def from_ring(x, axis):
    return [x] + [
        lax.ppermute(x, axis, [(i, (i + d) % 4) for i in range(4)]) for d in range(1, 4)
    ]


def along_ring(pieces, axis):
    return [pieces[0]] + [
        lax.ppermute(pieces[d], axis, [(i, (i + d) % 4) for i in range(4)]) for d in range(1, 4)
    ]


def chunk_turn(v):
    return jnp.transpose(v.reshape(8, 32, 4, 8), (0, 2, 1, 3)).reshape(8, D)


def chunk_back(v):
    return jnp.transpose(v.reshape(8, 4, 32, 8), (0, 2, 1, 3)).reshape(8, D)


def swap(x):
    return lax.ppermute(x, "c", [(0, 1), (1, 0)])


def shards(
    hidden,
    lengths,
    teacher,
    norm_gain,
    final_gain,
    score_vector,
    query_weight,
    key_matrix,
    value_matrix,
    out_weight,
):
    at = jnp.stack([lax.axis_index("pb"), lax.axis_index("x")]).astype(jnp.int32)
    tokens = hidden.reshape(ROWS, D)
    lens = lengths[0]
    gain = norm_gain[None]
    fg = final_gain[None]
    sv = score_vector[None]
    cos_np, sin_np = rope_consts()
    cos, sin = jnp.asarray(cos_np), jnp.asarray(sin_np)
    (both_halves,) = call(
        pack_body,
        [],
        [key_matrix, value_matrix, query_weight, out_weight.T],
        [((8, 2, 4, 1536), BF16)],
    )
    both_halves = both_halves.reshape(16, 4, 1536)
    column = lax.all_to_all(both_halves, ("z", "c"), 0, 0, tiled=True).reshape(64, 1536)
    normed, turned, nlast, xlast = call(
        prep_body,
        [lens],
        [tokens, gain],
        [((ROWS, D), BF16), ((D, ROWS), BF16), ((8, D), BF16), ((8, D), F32)],
        flops=10_000_000,
    )
    nlast = chunk_turn(nlast)
    wide = (PAIRS, HW)
    pack = jnp.concatenate(
        [
            xlast[0:PAIRS],
            nlast[0:PAIRS].astype(F32),
            jnp.broadcast_to(lens.astype(F32)[:, None], wide),
            jnp.broadcast_to(teacher[0][:, None], wide),
        ],
        axis=1,
    )
    column, normed, turned, pack = lax.optimization_barrier((column, normed, turned, pack))
    other = swap(normed)
    got = swap(pack)
    slab_b = everyone(column[:, 768:1536], "pb", 4).reshape(256, 768)
    ring_a = from_ring(column[:, 0:768], "x")
    (slab_a,) = call(arrange_body, [at], ring_a, [((4, 256, 768), BF16)], [((8, 4, 8, 768), BF16)])
    slab_a, slab_b, other, got = lax.optimization_barrier((slab_a, slab_b, other, got))
    packed = jnp.concatenate([pack, got], axis=0)
    xlast = packed[:, 0:1024]
    nlast = packed[:, 1024:2048].astype(BF16)
    lens_both = packed[:, 2048].astype(jnp.int32)
    teach = packed[:, 2048 + HW :]
    kvo = lax.all_to_all(slab_a, "pb", 0, 0, tiled=True).reshape(1024, 768)
    qo = from_ring(slab_b, "x")

    kproj, krot, vcast, qproj, qrot, attn, ctx, attended, oa = call(
        attend_body,
        [at, lens_both],
        [normed, other, nlast, cos, sin, kvo, *qo],
        [
            ((2 * ROWS, 256), F32),
            ((2 * ROWS, 256), BF16),
            ((2 * ROWS, 256), BF16),
            ((8, 512), F32),
            ((8, 512), BF16),
            ((64, SEQ), F32),
            ((8, 512), BF16),
            ((8, D), F32),
            ((D, 512), BF16),
        ],
        [((8, 512), F32), ((8, 512), F32), ((32, 4, 8, 256), BF16)],
        flops=1_100_000_000,
    )
    ctx, turned_late = lax.optimization_barrier((ctx, turned))
    turned_other = swap(turned_late)
    unit, oscale, score, tot, line = call(
        score_body,
        [],
        [teach, attended, swap(attended), xlast, fg, sv],
        [((8, D), F32), ((8, HW), F32), ((8, HW), F32), ((32, 1, HW), F32), ((1, PAIRS), F32)],
        flops=1_000_000,
    )

    totals = lax.all_to_all(tot, ("z", "x"), 0, 0, tiled=True)

    gkv, gq, gr, last, send = call(
        unit_back_body,
        [at, lens_both],
        [krot, vcast, kproj, qproj, qrot, attn, unit, oscale, fg, sv, cos, sin, oa, *qo, kvo],
        [((2 * ROWS, 512), F32), ((8, 512), F32), ((8, D), F32), ((8, D), F32), ((ROWS, D), BF16)],
        [((8, 512), F32), ((8, 512), F32), ((8, 512), F32)],
        flops=200_000_000,
    )
    grturn = chunk_turn(gr)
    last = chunk_back(last)
    got = swap(send)

    pieces = ((4, 256, 768), BF16)
    chip_a, *rest = call(
        weight_body,
        [at],
        [totals, score, teach, gkv, gq, gr, grturn, turned, turned_other, nlast, ctx],
        [pieces]
        + [((256, 768), BF16)] * 4
        + [((8, HW), F32), ((ROWS * 2, 512), BF16), ((8, HW), F32), ((8, D), F32)],
        [((8, D), BF16), ((8, D), BF16), pieces, ((8, 512), BF16)],
        flops=1_100_000_000,
    )
    chip_b, (loss, skv, g, sr) = rest[0:4], rest[4:]
    got_a = lax.all_to_all(chip_a, "pb", 0, 0, tiled=True)
    got_b = along_ring(chip_b, "x")
    (grad_hidden,) = call(
        hidden_body,
        [lens_both],
        [tokens, gain, skv, g, last, swap(last), sr, kvo, got],
        [((ROWS, D), BF16)],
        flops=600_000_000,
    )
    got_a, got_b, grad_hidden = lax.optimization_barrier((got_a, got_b, grad_hidden))
    *mid_a, mid_b = call(
        middle_body,
        [at],
        [loss, got_a, *got_b],
        [((64, 768), BF16)] * 4 + [((4, 80, 768), BF16)],
        [((8, 4, 8, 768), F32)],
    )
    done_a = along_ring(mid_a, "x")
    done_b = lax.all_to_all(mid_b, "pb", 0, 0, tiled=True)
    loss = jnp.sum(done_b[:, 64, 0:3].astype(F32), axis=1)
    loss = (loss[0] + loss[1]) + (loss[2] + loss[3])
    done_b = done_b[:, 0:64]

    def added(parts):
        total = parts[0].astype(F32)
        for part in parts[1:]:
            total = total + part.astype(F32)
        return total.astype(BF16)

    part = jnp.concatenate([added(done_a), added(done_b)], axis=1)
    rec = lax.all_to_all(part.reshape(16, 4, 1536), ("z", "c"), 0, 0, tiled=True)
    grad_query, grad_key, grad_value, grad_out = call(
        finish_body,
        [],
        [rec.reshape(8, 2, 4, 1536)],
        [((4, D), F32), ((4, 512), F32), ((4, 512), F32), ((4, D), F32)],
    )

    return (
        line,
        loss,
        grad_hidden.reshape(hidden.shape),
        grad_query,
        grad_key,
        grad_value,
        grad_out.T,
    )


def solution(mesh):
    torus = Mesh(mesh.devices.reshape(mesh.shape["pb"], 8, 4, 2), AXES)
    placed = (
        P("pb", NEG, None, None),
        P("pb", NEG),
        P("pb", NEG),
        P(),
        P(),
        P(),
        P(AXES, None),
        P(AXES, None),
        P(AXES, None),
        P(None, AXES),
    )
    return jax.shard_map(
        shards,
        mesh=torus,
        in_specs=placed,
        out_specs=(
            P("pb", NEG),
            P(),
            P("pb", NEG, None, None),
            P(AXES, None),
            P(AXES, None),
            P(AXES, None),
            P(None, AXES),
        ),
        check_vma=False,
    )
```

```python
import jax
import jax.numpy as jnp
import numpy as np
from jax import lax
from jax.experimental import pallas as pl
from jax.experimental.pallas import tpu as pltpu
from jax.sharding import Mesh
from jax.sharding import PartitionSpec as P

HW = 128
AXES = ("pb", "z", "x", "c")
NEG = ("z", "x", "c")
EPS = 1e-06
ROPE_BASE = 1000000.0
GRAD_SCALE = 512.0
PAIRS = 4
SEQ = 128
D = 1024
ROWS = PAIRS * SEQ
BOTH = 2 * PAIRS
F32 = jnp.float32
BF16 = jnp.bfloat16
SM = pl.BlockSpec(memory_space=pltpu.SMEM)
LAST = (((1,), (1,)), ((), ()))
FIRST = (((0,), (0,)), ((), ()))
SCALE = HW ** (-0.5)


def rope_consts():
    freqs = np.float32(ROPE_BASE) ** (-(np.arange(HW // 2, dtype=np.float32) * 2.0) / HW)
    angles = np.arange(SEQ, dtype=np.float32)[:, None] * freqs.astype(np.float32)[None, :]
    angles = np.concatenate([angles, angles], axis=1)
    sign = np.where(np.arange(HW) < HW // 2, -1.0, 1.0)
    return (
        np.cos(angles).astype(np.float32),
        (np.sin(angles) * sign[None, :]).astype(np.float32),
    )


def whole(shape):
    return pl.BlockSpec(shape, lambda i: (0,) * len(shape), pipeline_mode=pl.Buffered(1))


def block(cuts, key, shape):
    if key in cuts:
        return pl.BlockSpec(cuts[key], lambda i: (i,) + (0,) * (len(shape) - 1))
    return whole(shape)


def call(body, scalars, arrays, outs, scratch=(), flops=0, grant=52, cuts=()):
    moved = sum(a.size * a.dtype.itemsize for a in arrays)
    moved += sum(int(np.prod(o)) * np.dtype(d).itemsize for o, d in outs)
    return pl.pallas_call(
        body,
        grid=(4 if cuts else 1,),
        out_shape=[jax.ShapeDtypeStruct(o, d) for o, d in outs],
        in_specs=[SM] * len(scalars)
        + [block(cuts, k, a.shape) for k, a in enumerate(arrays)],
        out_specs=[block(cuts, -1 - k, o) for k, (o, _) in enumerate(outs)],
        scratch_shapes=[pltpu.VMEM(o, d) for o, d in scratch],
        compiler_params=pltpu.CompilerParams(vmem_limit_bytes=grant << 20),
        cost_estimate=pl.CostEstimate(flops=flops, bytes_accessed=moved, transcendentals=0),
    )(*scalars, *arrays)


def block_at(me, step, width):
    return pl.ds(pl.multiple_of(lax.rem(me + step + 4, 4) * width, width), width)


def dot(a, b, dims=(((1,), (0,)), ((), ()))):
    return lax.dot_general(a, b, dims, preferred_element_type=F32)


def half_turn(v):
    return pltpu.roll(v, HW // 2, 1)


def heads(v, n):
    return [v[:, i * HW : (i + 1) * HW] for i in range(n)]


def block_mask():
    row = lax.broadcasted_iota(jnp.int32, (8, 256), 0)
    lane = lax.broadcasted_iota(jnp.int32, (8, 256), 1)
    return (lane // HW) == (row // 2), (row % 2) == 0


def to_blocks(row, mask, even):
    h = heads(row, 4)
    e = jnp.broadcast_to(jnp.concatenate(h[0::2], axis=1), (8, 256))
    o = jnp.broadcast_to(jnp.concatenate(h[1::2], axis=1), (8, 256))
    return jnp.where(mask, jnp.where(even, e, o), 0.0)


def from_blocks(blocks, mask, even):
    e = jnp.sum(jnp.where(mask & even, blocks, 0.0), axis=0, keepdims=True)
    o = jnp.sum(jnp.where(mask & (~even), blocks, 0.0), axis=0, keepdims=True)
    return jnp.concatenate([e[:, 0:HW], o[:, 0:HW], e[:, HW:], o[:, HW:]], axis=1)


def query_tables(len_ref, cos_ref, sin_ref):
    return [
        jnp.concatenate([t[pl.ds(len_ref[p] - 1, 1), :] for p in range(BOTH)], axis=0)
        for t in (cos_ref, sin_ref)
    ]


def pack_body(k_ref, v_ref, q_ref, o_ref, out_ref):
    for h in range(2):
        wide, tall = slice(h * 256, h * 256 + 256), h * 512
        out_ref[0, h, :, 0:256] = k_ref[:, wide]
        out_ref[0, h, :, 256:512] = v_ref[:, wide]
        out_ref[0, h, :, 512:768] = o_ref[:, tall : tall + 256]
        out_ref[0, h, :, 768:1280] = q_ref[:, tall : tall + 512]
        out_ref[0, h, :, 1280:1536] = o_ref[:, tall + 256 : tall + 512]
    for z in range(1, 8):
        out_ref[z] = out_ref[0]


def prep_body(len_ref, h_ref, gain_ref, normed_ref, turned_ref, nlast_ref, xlast_ref):
    row = lax.broadcasted_iota(jnp.int32, (8, SEQ), 0)
    lane = lax.broadcasted_iota(jnp.int32, (8, SEQ), 1)
    nl = jnp.zeros((8, D), F32)
    xl = jnp.zeros((8, D), F32)
    for p in range(PAIRS):
        raw = h_ref[p * SEQ : (p + 1) * SEQ, :]
        x = raw.astype(F32)
        inv = lax.rsqrt(jnp.mean(x * x, axis=-1, keepdims=True) + EPS)
        n = (x * inv * gain_ref[...]).astype(BF16)
        normed_ref[p * SEQ : (p + 1) * SEQ, :] = n
        turned_ref[:, p * SEQ : (p + 1) * SEQ] = n.T
        e = len_ref[p] - 1
        hot = jnp.where((row == p) & (lane == e), 1.0, 0.0).astype(BF16)
        nl = nl + dot(hot, n)
        xl = xl + dot(hot, raw)
    nlast_ref[...] = nl.astype(BF16)
    xlast_ref[...] = xl


def arrange_body(at_ref, *refs):
    a_refs, out_ref, slab_scr = refs[0:4], refs[4], refs[5]
    x = at_ref[1]
    for d in range(4):
        slab_scr[:, pl.ds(lax.rem(x - d + 4, 4), 1)] = a_refs[d][...].reshape(8, 1, 8, 768)
    slab = slab_scr[...].reshape(256, 768)
    for y in range(4):
        out_ref[y] = slab


def attend_body(
    at_ref, len_ref, normed_ref, other_ref, nlast_ref, cos_ref, sin_ref, kv_ref, *refs
):
    out_ref, o_ref, turn_scr, lg_scr = refs[11], refs[12], refs[15], refs[16]
    q_refs = refs[0:4]
    kproj_ref, krot_ref, vcast_ref, qproj_ref, qrot_ref, attn_ref, ctx_ref = refs[4:11]
    qr_scr, ctx_scr = refs[13:15]
    x = at_ref[1]
    mask, even = block_mask()
    lane = lax.broadcasted_iota(jnp.int32, (8 * BOTH, SEQ), 1)
    for side, rows_ref in enumerate((normed_ref, other_ref)):

        @pl.loop(0, 2)
        def _(i):
            src = pl.ds(pl.multiple_of(i * 256, 256), 256)
            dst = pl.ds(pl.multiple_of(side * ROWS + i * 256, 256), 256)
            kv = dot(rows_ref[src, :], kv_ref[:, 0:512])
            kproj_ref[dst, :] = kv[:, 0:256]
            vcast_ref[dst, :] = kv[:, 256:512].astype(BF16)

    q = jnp.zeros((8, 512), F32)
    for d in range(4):
        q = q + dot(nlast_ref[:, block_at(x, -d, 256)], q_refs[d][:, 0:512])
    qproj_ref[...] = q
    cos_q, sin_q = query_tables(len_ref, cos_ref, sin_ref)
    for h in range(4):
        q = qproj_ref[:, h * HW : (h + 1) * HW]
        u = q * lax.rsqrt(jnp.mean(q * q, axis=-1, keepdims=True) + EPS)
        r = u * cos_q + half_turn(u) * sin_q
        qr_scr[:, h * HW : (h + 1) * HW] = r
        qrot_ref[:, h * HW : (h + 1) * HW] = r.astype(BF16)
    for p in range(BOTH):
        rows = slice(p * SEQ, (p + 1) * SEQ)
        for g in range(2):
            k = kproj_ref[rows, g * HW : (g + 1) * HW]
            u = k * lax.rsqrt(jnp.mean(k * k, axis=-1, keepdims=True) + EPS)
            r = u * cos_ref[...] + half_turn(u) * sin_ref[...]
            krot_ref[rows, g * HW : (g + 1) * HW] = r.astype(BF16)
    for p in range(BOTH):
        rows = slice(p * SEQ, (p + 1) * SEQ)
        qb = to_blocks(qr_scr[p : p + 1, :], mask, even).astype(BF16)
        lg_scr[p * 8 : (p + 1) * 8, :] = dot(qb, krot_ref[rows, :], LAST)
    last = jnp.concatenate(
        [jnp.full((8, SEQ), len_ref[p] - 1, jnp.int32) for p in range(BOTH)], axis=0
    )
    ex = jnp.where(lane <= last, jnp.exp(lg_scr[...] * SCALE), 0.0)
    w = ex / jnp.sum(ex, axis=-1, keepdims=True)
    attn_ref[...] = w
    probs = w.astype(BF16)
    for p in range(BOTH):
        c = dot(probs[p * 8 : (p + 1) * 8, :], vcast_ref[p * SEQ : (p + 1) * SEQ, :])
        ctx_scr[p : p + 1, :] = from_blocks(c, mask, even)
    ctx_ref[...] = ctx_scr[...].astype(BF16)
    for d in range(4):
        turn_scr[:, pl.ds(lax.rem(x - d + 4, 4), 1)] = q_refs[d][:, 512:768].reshape(32, 1, 8, 256)
    o_ref[:, 0:256] = kv_ref[:, 512:768]
    o_ref[:, 256:512] = turn_scr[...].reshape(1024, 256)
    out_ref[...] = dot(ctx_ref[...], o_ref[...], LAST)


def score_body(teach_ref, mine_ref, theirs_ref, xlast_ref, fg_ref, sv_ref, *refs):
    unit_ref, oscale_ref, score_ref, tot_ref, line_ref = refs
    res = xlast_ref[...] + (mine_ref[...] + pltpu.roll(theirs_ref[...], PAIRS, 0))
    sc = lax.rsqrt(jnp.mean(res * res, axis=-1, keepdims=True) + EPS)
    unit = res * sc
    unit_ref[...] = unit
    oscale_ref[...] = jnp.broadcast_to(sc, (8, HW))
    s = jnp.sum(unit * fg_ref[...] * sv_ref[...], axis=-1, keepdims=True)
    s = jnp.broadcast_to(s, (8, HW))
    score_ref[...] = s
    row = lax.broadcasted_iota(jnp.int32, (8, HW), 0)
    lane = lax.broadcasted_iota(jnp.int32, (8, HW), 1)
    line_ref[...] = jnp.sum(jnp.where(row == lane, s, 0.0), axis=0, keepdims=True)[:, 0:PAIRS]
    scaled = teach_ref[...] / 2.0
    es = jnp.exp(s)
    et = jnp.exp(scaled)
    v = jnp.where(lane == 0, es, jnp.where(lane == 1, et, et * (scaled - s)))
    v = jnp.where(lane < 3, v + pltpu.roll(v, PAIRS, 0), 0.0)
    tot_ref[...] = jnp.broadcast_to(jnp.sum(v[0:PAIRS], axis=0, keepdims=True)[None], (32, 1, HW))


def unit_back_body(
    at_ref,
    len_ref,
    krot_ref,
    vcast_ref,
    kproj_ref,
    qproj_ref,
    qrot_ref,
    attn_ref,
    unit_ref,
    oscale_ref,
    fg_ref,
    sv_ref,
    cos_ref,
    sin_ref,
    *refs,
):
    o_ref, q_refs, kv_ref = refs[0], refs[1:5], refs[5]
    gkv_ref, gq_ref, gr_ref, last_ref, send_ref, gc_scr, gq_scr, qr_scr, gp_scr = refs[6:]
    mask, even = block_mask()
    unit = unit_ref[...]
    gu = sv_ref[...] * fg_ref[...]
    gr = oscale_ref[:, 0:1] * (gu - unit * jnp.mean(gu * unit, axis=-1, keepdims=True))
    gr_ref[...] = gr
    gc_scr[...] = dot(gr.astype(BF16), o_ref[...])
    qr_scr[...] = qrot_ref[...].astype(F32)
    blocks = []
    for p in range(BOTH):
        rows = slice(p * SEQ, (p + 1) * SEQ)
        gb = to_blocks(gc_scr[p : p + 1, :], mask, even).astype(BF16)
        blocks.append(gb)
        gp_scr[p * 8 : (p + 1) * 8, :] = dot(gb, vcast_ref[rows, :], LAST)
    w = attn_ref[...]
    gp = gp_scr[...]
    spread = jnp.sum(w * gp, axis=-1, keepdims=True)
    dls = (w * (gp - spread)).astype(BF16)
    probs = w.astype(BF16)
    for p in range(BOTH):
        rows = slice(p * SEQ, (p + 1) * SEQ)
        eight = slice(p * 8, (p + 1) * 8)
        qb = to_blocks(qr_scr[p : p + 1, :], mask, even).astype(BF16)
        gkv_ref[rows, 256:512] = dot(probs[eight, :], blocks[p], FIRST)
        dl = dls[eight, :]
        gq_scr[p : p + 1, :] = from_blocks(dot(dl, krot_ref[rows, :]) * SCALE, mask, even)
        gk = dot(dl, qb, FIRST) * SCALE
        for g in range(2):
            cols = slice(g * HW, (g + 1) * HW)
            k = kproj_ref[rows, cols]
            sc = lax.rsqrt(jnp.mean(k * k, axis=-1, keepdims=True) + EPS)
            u = k * sc
            r = gk[:, cols]
            t = r * cos_ref[...] + half_turn(r * sin_ref[...])
            gkv_ref[rows, cols] = sc * (t - u * jnp.mean(t * u, axis=-1, keepdims=True))
    cos_q, sin_q = query_tables(len_ref, cos_ref, sin_ref)
    for h in range(4):
        q = qproj_ref[:, h * HW : (h + 1) * HW]
        sc = lax.rsqrt(jnp.mean(q * q, axis=-1, keepdims=True) + EPS)
        u = q * sc
        r = gq_scr[:, h * HW : (h + 1) * HW]
        t = r * cos_q + half_turn(r * sin_q)
        gq_ref[:, h * HW : (h + 1) * HW] = sc * (
            t - u * jnp.mean(t * u, axis=-1, keepdims=True)
        )
    gqb = gq_ref[...].astype(BF16)
    for d in range(4):
        last_ref[:, block_at(at_ref[1], -d, 256)] = dot(gqb, q_refs[d][:, 0:512], LAST)

    @pl.loop(0, 2)
    def _(i):
        src = pl.ds(pl.multiple_of(ROWS + i * 256, 256), 256)
        gn = dot(gkv_ref[src, :].astype(BF16), kv_ref[:, 0:512], LAST)
        send_ref[pl.ds(pl.multiple_of(i * 256, 256), 256), :] = gn.astype(BF16)


def weight_body(
    at_ref,
    tot_ref,
    score_ref,
    teach_ref,
    gkv_ref,
    gq_ref,
    gr_ref,
    grturn_ref,
    turned_ref,
    turned_other_ref,
    nlast_ref,
    ctx_ref,
    *refs,
):
    out_a, outs_b, loss_ref, skv_ref, g_ref, sr_ref = refs[0], refs[1:5], *refs[5:9]
    srow_scr, sturn_scr, sq_scr = refs[9:]
    x = at_ref[1]
    i = pl.program_id(0)

    @pl.when(i == 0)
    def _():
        lane = lax.broadcasted_iota(jnp.int32, (1, HW), 1)

        def pick(v, i):
            return jnp.sum(jnp.where(lane == i, v, 0.0), axis=-1, keepdims=True)

        t = tot_ref[0]
        for i in range(1, 32):
            t = t + tot_ref[i]
        ts, tt, cr = pick(t, 0), pick(t, 1), pick(t, 2)
        loss_ref[...] = jnp.broadcast_to(cr / tt - jnp.log(tt) + jnp.log(ts), (8, HW))
        row = lax.broadcasted_iota(jnp.int32, (8, HW), 0)
        g = GRAD_SCALE * (jnp.exp(score_ref[...]) / ts - jnp.exp(teach_ref[...] / 2.0) / tt)
        gcol = g[:, 0:1]
        sr = gr_ref[...] * gcol
        sr_ref[...] = sr
        g_ref[...] = g
        sq_scr[...] = (gq_ref[...] * gcol).astype(BF16)
        srow_scr[...] = sr.astype(BF16)
        sturn_scr[...] = (grturn_ref[...] * gcol).astype(BF16)
        for p in range(BOTH):
            rows = slice(p * SEQ, (p + 1) * SEQ)
            skv_ref[rows, :] = (gkv_ref[rows, :] * gcol[p : p + 1, :]).astype(BF16)

    rows = pl.ds(pl.multiple_of(i * 256, 256), 256)
    kv = dot(turned_ref[...], skv_ref[0:ROWS, :]) + dot(
        turned_other_ref[...], skv_ref[ROWS : 2 * ROWS, :]
    )
    o_low = dot(srow_scr[:, rows], ctx_ref[:, 0:256], FIRST)
    rows_x = block_at(x, i, 256)
    q = dot(nlast_ref[:, rows_x], sq_scr[...], FIRST)
    o_high = dot(sturn_scr[:, rows_x], ctx_ref[:, 256:512], FIRST)
    out_a[0, :, 0:512] = kv.astype(BF16)
    out_a[0, :, 512:768] = o_low.astype(BF16)
    q, o_high = q.astype(BF16), o_high.astype(BF16)
    for d in range(4):

        @pl.when(i == d)
        def _():
            outs_b[d][:, 0:512] = q
            outs_b[d][:, 512:768] = o_high


def middle_body(at_ref, loss_ref, got_a_ref, *refs):
    b_refs, out_a, out_b, a_scr = refs[0:4], refs[4:8], refs[8], refs[9]
    x = at_ref[1]
    total_a = got_a_ref[0].astype(F32)
    total_b = b_refs[0][...].astype(F32)
    for d in range(1, 4):
        total_a = total_a + got_a_ref[d].astype(F32)
        total_b = total_b + b_refs[d][...].astype(F32)
    out_b[:, 0:64, :] = total_b.reshape(4, 64, 768).astype(BF16)
    rest = jnp.broadcast_to(loss_ref[0:1, 0:1], (16, 768))
    lane = lax.broadcasted_iota(jnp.int32, (16, 768), 1)
    parts = jnp.zeros((16, 768), F32)
    for i in range(3):
        part = rest.astype(BF16).astype(F32)
        parts = jnp.where(lane == i, part, parts)
        rest = rest - part
    for y in range(4):
        out_b[y, 64:80, :] = parts.astype(BF16)
    a_scr[...] = total_a.reshape(8, 4, 8, 768)
    for d in range(4):
        out_a[d][...] = a_scr[:, pl.ds(lax.rem(x + d, 4), 1)].reshape(64, 768).astype(BF16)


def hidden_body(len_ref, h_ref, gain_ref, skv_ref, g_ref, last_ref, other_ref, sr_ref, kv_ref, got_ref, out_ref):
    pos = lax.broadcasted_iota(jnp.int32, (SEQ, 1), 0)

    @pl.loop(0, PAIRS)
    def _(p):
        rows = pl.ds(pl.multiple_of(p * SEQ, SEQ), SEQ)
        at = pos == len_ref[p] - 1
        last = last_ref[pl.ds(p, 1), :] + other_ref[pl.ds(PAIRS + p, 1), :]
        unit = got_ref[rows, :].astype(F32) + jnp.where(at, last, 0.0)
        gn = dot(skv_ref[rows, :], kv_ref[:, 0:512], LAST) + g_ref[pl.ds(p, 1), 0:1] * unit
        x = h_ref[rows, :].astype(F32)
        inv = lax.rsqrt(jnp.mean(x * x, axis=-1, keepdims=True) + EPS)
        s = gn * gain_ref[...]
        gi = inv * s - x * (inv * inv * inv * jnp.mean(s * x, axis=-1, keepdims=True))
        gi = gi + jnp.where(at, sr_ref[pl.ds(p, 1), :], 0.0)
        out_ref[rows, :] = gi.astype(BF16)


def finish_body(rec_ref, gq_ref, gk_ref, gv_ref, go_ref):
    for h in range(2):
        total = rec_ref[0, h].astype(F32)
        for z in range(1, 8):
            total = total + rec_ref[z, h].astype(F32)
        gk_ref[:, h * 256 : h * 256 + 256] = total[:, 0:256]
        gv_ref[:, h * 256 : h * 256 + 256] = total[:, 256:512]
        go_ref[:, h * 512 : h * 512 + 256] = total[:, 512:768]
        gq_ref[:, h * 512 : h * 512 + 512] = total[:, 768:1280]
        go_ref[:, h * 512 + 256 : h * 512 + 512] = total[:, 1280:1536]


def everyone(x, axes, count):
    return lax.all_to_all(
        jnp.broadcast_to(x[None], (count, *x.shape)), axes, 0, 0, tiled=True
    )


def from_ring(x, axis):
    return [x] + [
        lax.ppermute(x, axis, [(i, (i + d) % 4) for i in range(4)]) for d in range(1, 4)
    ]


def along_ring(pieces, axis):
    return [pieces[0]] + [
        lax.ppermute(pieces[d], axis, [(i, (i + d) % 4) for i in range(4)]) for d in range(1, 4)
    ]


def chunk_turn(v):
    return jnp.transpose(v.reshape(8, 32, 4, 8), (0, 2, 1, 3)).reshape(8, D)


def chunk_back(v):
    return jnp.transpose(v.reshape(8, 4, 32, 8), (0, 2, 1, 3)).reshape(8, D)


def swap(x):
    return lax.ppermute(x, "c", [(0, 1), (1, 0)])


def shards(
    hidden,
    lengths,
    teacher,
    norm_gain,
    final_gain,
    score_vector,
    query_weight,
    key_matrix,
    value_matrix,
    out_weight,
):
    at = jnp.stack([lax.axis_index("pb"), lax.axis_index("x")]).astype(jnp.int32)
    tokens = hidden.reshape(ROWS, D)
    lens = lengths[0]
    gain = norm_gain[None]
    fg = final_gain[None]
    sv = score_vector[None]
    cos_np, sin_np = rope_consts()
    cos, sin = jnp.asarray(cos_np), jnp.asarray(sin_np)
    (both_halves,) = call(
        pack_body,
        [],
        [key_matrix, value_matrix, query_weight, out_weight.T],
        [((8, 2, 4, 1536), BF16)],
        grant=62,
    )
    both_halves = both_halves.reshape(16, 4, 1536)
    column = lax.all_to_all(both_halves, ("z", "c"), 0, 0, tiled=True).reshape(64, 1536)
    normed, turned, nlast, xlast = call(
        prep_body,
        [lens],
        [tokens, gain],
        [((ROWS, D), BF16), ((D, ROWS), BF16), ((8, D), BF16), ((8, D), F32)],
        flops=10_000_000,
    )
    nlast = chunk_turn(nlast)
    wide = (PAIRS, HW)
    pack = jnp.concatenate(
        [
            xlast[0:PAIRS],
            nlast[0:PAIRS].astype(F32),
            jnp.broadcast_to(lens.astype(F32)[:, None], wide),
            jnp.broadcast_to(teacher[0][:, None], wide),
        ],
        axis=1,
    )
    column, normed, turned, pack = lax.optimization_barrier((column, normed, turned, pack))
    other = swap(normed)
    got = swap(pack)
    slab_b = everyone(column[:, 768:1536], "pb", 4).reshape(256, 768)
    ring_a = from_ring(column[:, 0:768], "x")
    (slab_a,) = call(arrange_body, [at], ring_a, [((4, 256, 768), BF16)], [((8, 4, 8, 768), BF16)])
    slab_a, slab_b, got = lax.optimization_barrier((slab_a, slab_b, got))
    packed = jnp.concatenate([pack, got], axis=0)
    xlast = packed[:, 0:1024]
    nlast = packed[:, 1024:2048].astype(BF16)
    lens_both = packed[:, 2048].astype(jnp.int32)
    teach = packed[:, 2048 + HW :]
    kvo = lax.all_to_all(slab_a, "pb", 0, 0, tiled=True).reshape(1024, 768)
    qo = from_ring(slab_b, "x")

    kproj, krot, vcast, qproj, qrot, attn, ctx, attended, oa = call(
        attend_body,
        [at, lens_both],
        [normed, other, nlast, cos, sin, kvo, *qo],
        [
            ((2 * ROWS, 256), F32),
            ((2 * ROWS, 256), BF16),
            ((2 * ROWS, 256), BF16),
            ((8, 512), F32),
            ((8, 512), BF16),
            ((64, SEQ), F32),
            ((8, 512), BF16),
            ((8, D), F32),
            ((D, 512), BF16),
        ],
        [((8, 512), F32), ((8, 512), F32), ((32, 4, 8, 256), BF16), ((8 * BOTH, SEQ), F32)],
        flops=1_100_000_000,
    )
    ctx, turned_late = lax.optimization_barrier((ctx, turned))
    turned_other = swap(turned_late)
    unit, oscale, score, tot, line = call(
        score_body,
        [],
        [teach, attended, swap(attended), xlast, fg, sv],
        [((8, D), F32), ((8, HW), F32), ((8, HW), F32), ((32, 1, HW), F32), ((1, PAIRS), F32)],
        flops=1_000_000,
    )

    totals = lax.all_to_all(tot, ("z", "x"), 0, 0, tiled=True)

    gkv, gq, gr, last, send = call(
        unit_back_body,
        [at, lens_both],
        [krot, vcast, kproj, qproj, qrot, attn, unit, oscale, fg, sv, cos, sin, oa, *qo, kvo],
        [((2 * ROWS, 512), F32), ((8, 512), F32), ((8, D), F32), ((8, D), F32), ((ROWS, D), BF16)],
        [((8, 512), F32), ((8, 512), F32), ((8, 512), F32), ((8 * BOTH, SEQ), F32)],
        flops=200_000_000,
    )
    grturn = chunk_turn(gr)
    last = chunk_back(last)
    got = swap(send)

    pieces = ((4, 256, 768), BF16)
    chip_a, *rest = call(
        weight_body,
        [at],
        [totals, score, teach, gkv, gq, gr, grturn, turned, turned_other, nlast, ctx],
        [pieces]
        + [((256, 768), BF16)] * 4
        + [((8, HW), F32), ((ROWS * 2, 512), BF16), ((8, HW), F32), ((8, D), F32)],
        [((8, D), BF16), ((8, D), BF16), ((8, 512), BF16)],
        flops=1_100_000_000,
        cuts={7: (256, 512), 8: (256, 512), -1: (1, 256, 768)},
    )
    chip_b, (loss, skv, g, sr) = rest[0:4], rest[4:]
    got_a = lax.all_to_all(chip_a, "pb", 0, 0, tiled=True)
    got_b = along_ring(chip_b, "x")
    (grad_hidden,) = call(
        hidden_body,
        [lens_both],
        [tokens, gain, skv, g, last, swap(last), sr, kvo, got],
        [((ROWS, D), BF16)],
        flops=600_000_000,
    )
    got_a, got_b, grad_hidden = lax.optimization_barrier((got_a, got_b, grad_hidden))
    *mid_a, mid_b = call(
        middle_body,
        [at],
        [loss, got_a, *got_b],
        [((64, 768), BF16)] * 4 + [((4, 80, 768), BF16)],
        [((8, 4, 8, 768), F32)],
    )
    done_a = along_ring(mid_a, "x")
    done_b = lax.all_to_all(mid_b, "pb", 0, 0, tiled=True)
    loss = jnp.sum(done_b[:, 64, 0:3].astype(F32), axis=1)
    loss = (loss[0] + loss[1]) + (loss[2] + loss[3])
    done_b = done_b[:, 0:64]

    def added(parts):
        total = parts[0].astype(F32)
        for part in parts[1:]:
            total = total + part.astype(F32)
        return total.astype(BF16)

    part = jnp.concatenate([added(done_a), added(done_b)], axis=1)
    rec = lax.all_to_all(part.reshape(16, 4, 1536), ("z", "c"), 0, 0, tiled=True)
    grad_query, grad_key, grad_value, grad_out = call(
        finish_body,
        [],
        [rec.reshape(8, 2, 4, 1536)],
        [((4, D), F32), ((4, 512), F32), ((4, 512), F32), ((4, D), F32)],
    )

    return (
        line,
        loss,
        grad_hidden.reshape(hidden.shape),
        grad_query,
        grad_key,
        grad_value,
        grad_out.T,
    )


def solution(mesh):
    torus = Mesh(mesh.devices.reshape(mesh.shape["pb"], 8, 4, 2), AXES)
    placed = (
        P("pb", NEG, None, None),
        P("pb", NEG),
        P("pb", NEG),
        P(),
        P(),
        P(),
        P(AXES, None),
        P(AXES, None),
        P(AXES, None),
        P(None, AXES),
    )
    return jax.shard_map(
        shards,
        mesh=torus,
        in_specs=placed,
        out_specs=(
            P("pb", NEG),
            P(),
            P("pb", NEG, None, None),
            P(AXES, None),
            P(AXES, None),
            P(AXES, None),
            P(None, AXES),
        ),
        check_vma=False,
    )
```

```python
import jax
import jax.numpy as jnp
import numpy as np
from jax import lax
from jax.experimental import pallas as pl
from jax.experimental.pallas import tpu as pltpu
from jax.sharding import Mesh
from jax.sharding import PartitionSpec as P

HW = 128
AXES = ("pb", "z", "x", "c")
NEG = ("z", "x", "c")
EPS = 1e-06
ROPE_BASE = 1000000.0
GRAD_SCALE = 512.0
PAIRS = 4
SEQ = 128
D = 1024
ROWS = PAIRS * SEQ
BOTH = 2 * PAIRS
LOW = 384
WA = 512 + LOW
WB = 1024 - LOW
F32 = jnp.float32
BF16 = jnp.bfloat16
SM = pl.BlockSpec(memory_space=pltpu.SMEM)
LAST = (((1,), (1,)), ((), ()))
FIRST = (((0,), (0,)), ((), ()))
SCALE = HW ** (-0.5)


def rope_consts():
    freqs = np.float32(ROPE_BASE) ** (-(np.arange(HW // 2, dtype=np.float32) * 2.0) / HW)
    angles = np.arange(SEQ, dtype=np.float32)[:, None] * freqs.astype(np.float32)[None, :]
    angles = np.concatenate([angles, angles], axis=1)
    sign = np.where(np.arange(HW) < HW // 2, -1.0, 1.0)
    return (
        np.cos(angles).astype(np.float32),
        (np.sin(angles) * sign[None, :]).astype(np.float32),
    )


def whole(shape):
    return pl.BlockSpec(shape, lambda i: (0,) * len(shape), pipeline_mode=pl.Buffered(1))


def call(body, scalars, arrays, outs, scratch=(), flops=0, grant=52):
    moved = sum(a.size * a.dtype.itemsize for a in arrays)
    moved += sum(int(np.prod(o)) * np.dtype(d).itemsize for o, d in outs)
    return pl.pallas_call(
        body,
        grid=(1,),
        out_shape=[jax.ShapeDtypeStruct(o, d) for o, d in outs],
        in_specs=[SM] * len(scalars) + [whole(a.shape) for a in arrays],
        out_specs=[whole(o) for o, _ in outs],
        scratch_shapes=[pltpu.VMEM(o, d) for o, d in scratch],
        compiler_params=pltpu.CompilerParams(vmem_limit_bytes=grant << 20),
        cost_estimate=pl.CostEstimate(flops=flops, bytes_accessed=moved, transcendentals=0),
    )(*scalars, *arrays)


def block_at(me, step, width):
    return pl.ds(pl.multiple_of(lax.rem(me + step + 4, 4) * width, width), width)


def dot(a, b, dims=(((1,), (0,)), ((), ()))):
    return lax.dot_general(a, b, dims, preferred_element_type=F32)


def half_turn(v):
    return pltpu.roll(v, HW // 2, 1)


def heads(v, n):
    return [v[:, i * HW : (i + 1) * HW] for i in range(n)]


def block_mask():
    row = lax.broadcasted_iota(jnp.int32, (8, 256), 0)
    lane = lax.broadcasted_iota(jnp.int32, (8, 256), 1)
    return (lane // HW) == (row // 2), (row % 2) == 0


def to_blocks(row, mask, even):
    h = heads(row, 4)
    e = jnp.broadcast_to(jnp.concatenate(h[0::2], axis=1), (8, 256))
    o = jnp.broadcast_to(jnp.concatenate(h[1::2], axis=1), (8, 256))
    return jnp.where(mask, jnp.where(even, e, o), 0.0)


def from_blocks(blocks, mask, even):
    e = jnp.sum(jnp.where(mask & even, blocks, 0.0), axis=0, keepdims=True)
    o = jnp.sum(jnp.where(mask & (~even), blocks, 0.0), axis=0, keepdims=True)
    return jnp.concatenate([e[:, 0:HW], o[:, 0:HW], e[:, HW:], o[:, HW:]], axis=1)


def query_tables(len_ref, cos_ref, sin_ref):
    return [
        jnp.concatenate([t[pl.ds(len_ref[p] - 1, 1), :] for p in range(BOTH)], axis=0)
        for t in (cos_ref, sin_ref)
    ]


def pack_body(k_ref, v_ref, q_ref, o_ref, out_ref):
    for h in range(2):
        wide, tall = slice(h * 256, h * 256 + 256), h * 512
        out_ref[0, h, :, 0:256] = k_ref[:, wide]
        out_ref[0, h, :, 256:512] = v_ref[:, wide]
        out_ref[0, h, :, 512:WA] = o_ref[:, tall : tall + LOW]
        out_ref[0, h, :, WA : WA + 512] = q_ref[:, tall : tall + 512]
        out_ref[0, h, :, WA + 512 : 1536] = o_ref[:, tall + LOW : tall + 512]
    for z in range(1, 8):
        out_ref[z] = out_ref[0]


def prep_body(len_ref, h_ref, gain_ref, normed_ref, turned_ref, nlast_ref, xlast_ref):
    row = lax.broadcasted_iota(jnp.int32, (8, SEQ), 0)
    lane = lax.broadcasted_iota(jnp.int32, (8, SEQ), 1)
    nl = jnp.zeros((8, D), F32)
    xl = jnp.zeros((8, D), F32)
    for p in range(PAIRS):
        raw = h_ref[p * SEQ : (p + 1) * SEQ, :]
        x = raw.astype(F32)
        inv = lax.rsqrt(jnp.mean(x * x, axis=-1, keepdims=True) + EPS)
        n = (x * inv * gain_ref[...]).astype(BF16)
        normed_ref[p * SEQ : (p + 1) * SEQ, :] = n
        turned_ref[:, p * SEQ : (p + 1) * SEQ] = n.T
        e = len_ref[p] - 1
        hot = jnp.where((row == p) & (lane == e), 1.0, 0.0).astype(BF16)
        nl = nl + dot(hot, n)
        xl = xl + dot(hot, raw)
    nlast_ref[...] = nl.astype(BF16)
    xlast_ref[...] = xl


def arrange_body(at_ref, *refs):
    a_refs, out_ref, slab_scr = refs[0:4], refs[4], refs[5]
    x = at_ref[1]
    for d in range(4):
        slab_scr[:, pl.ds(lax.rem(x - d + 4, 4), 1)] = a_refs[d][...].reshape(8, 1, 8, WA)
    slab = slab_scr[...].reshape(256, WA)
    for y in range(4):
        out_ref[y] = slab


def attend_body(
    at_ref, len_ref, normed_ref, other_ref, nlast_ref, cos_ref, sin_ref, kv_ref, *refs
):
    out_ref, o_ref, turn_scr, lg_scr = refs[11], refs[12], refs[15], refs[16]
    q_refs = refs[0:4]
    kproj_ref, krot_ref, vcast_ref, qproj_ref, qrot_ref, attn_ref, ctx_ref = refs[4:11]
    qr_scr, ctx_scr = refs[13:15]
    x = at_ref[1]
    mask, even = block_mask()
    lane = lax.broadcasted_iota(jnp.int32, (8 * BOTH, SEQ), 1)
    for side, rows_ref in enumerate((normed_ref, other_ref)):
        here = slice(side * ROWS, (side + 1) * ROWS)
        kv = dot(rows_ref[...], kv_ref[:, 0:512])
        kproj_ref[here, :] = kv[:, 0:256]
        vcast_ref[here, :] = kv[:, 256:512].astype(BF16)

    q = jnp.zeros((8, 512), F32)
    for d in range(4):
        q = q + dot(nlast_ref[:, block_at(x, -d, 256)], q_refs[d][:, 0:512])
    qproj_ref[...] = q
    cos_q, sin_q = query_tables(len_ref, cos_ref, sin_ref)
    for h in range(4):
        q = qproj_ref[:, h * HW : (h + 1) * HW]
        u = q * lax.rsqrt(jnp.mean(q * q, axis=-1, keepdims=True) + EPS)
        r = u * cos_q + half_turn(u) * sin_q
        qr_scr[:, h * HW : (h + 1) * HW] = r
        qrot_ref[:, h * HW : (h + 1) * HW] = r.astype(BF16)
    for p in range(BOTH):
        rows = slice(p * SEQ, (p + 1) * SEQ)
        for g in range(2):
            k = kproj_ref[rows, g * HW : (g + 1) * HW]
            u = k * lax.rsqrt(jnp.mean(k * k, axis=-1, keepdims=True) + EPS)
            r = u * cos_ref[...] + half_turn(u) * sin_ref[...]
            krot_ref[rows, g * HW : (g + 1) * HW] = r.astype(BF16)
    for p in range(BOTH):
        rows = slice(p * SEQ, (p + 1) * SEQ)
        qb = to_blocks(qr_scr[p : p + 1, :], mask, even).astype(BF16)
        lg_scr[p * 8 : (p + 1) * 8, :] = dot(qb, krot_ref[rows, :], LAST)
    last = jnp.concatenate(
        [jnp.full((8, SEQ), len_ref[p] - 1, jnp.int32) for p in range(BOTH)], axis=0
    )
    ex = jnp.where(lane <= last, jnp.exp(lg_scr[...] * SCALE), 0.0)
    w = ex / jnp.sum(ex, axis=-1, keepdims=True)
    attn_ref[...] = w
    probs = w.astype(BF16)
    for p in range(BOTH):
        c = dot(probs[p * 8 : (p + 1) * 8, :], vcast_ref[p * SEQ : (p + 1) * SEQ, :])
        ctx_scr[p : p + 1, :] = from_blocks(c, mask, even)
    ctx_ref[...] = ctx_scr[...].astype(BF16)
    for d in range(4):
        turn_scr[:, pl.ds(lax.rem(x - d + 4, 4), 1)] = q_refs[d][:, 512:WB].reshape(
            32, 1, 8, 512 - LOW
        )
    o_ref[:, 0:LOW] = kv_ref[:, 512:WA]
    o_ref[:, LOW:512] = turn_scr[...].reshape(1024, 512 - LOW)
    out_ref[...] = dot(ctx_ref[...], o_ref[...], LAST)


def score_body(teach_ref, mine_ref, theirs_ref, xlast_ref, fg_ref, sv_ref, *refs):
    unit_ref, oscale_ref, score_ref, tot_ref, line_ref = refs
    res = xlast_ref[...] + (mine_ref[...] + pltpu.roll(theirs_ref[...], PAIRS, 0))
    sc = lax.rsqrt(jnp.mean(res * res, axis=-1, keepdims=True) + EPS)
    unit = res * sc
    unit_ref[...] = unit
    oscale_ref[...] = jnp.broadcast_to(sc, (8, HW))
    s = jnp.sum(unit * fg_ref[...] * sv_ref[...], axis=-1, keepdims=True)
    s = jnp.broadcast_to(s, (8, HW))
    score_ref[...] = s
    row = lax.broadcasted_iota(jnp.int32, (8, HW), 0)
    lane = lax.broadcasted_iota(jnp.int32, (8, HW), 1)
    line_ref[...] = jnp.sum(jnp.where(row == lane, s, 0.0), axis=0, keepdims=True)[:, 0:PAIRS]
    scaled = teach_ref[...] / 2.0
    es = jnp.exp(s)
    et = jnp.exp(scaled)
    v = jnp.where(lane == 0, es, jnp.where(lane == 1, et, et * (scaled - s)))
    v = jnp.where(lane < 3, v + pltpu.roll(v, PAIRS, 0), 0.0)
    tot_ref[...] = jnp.broadcast_to(jnp.sum(v[0:PAIRS], axis=0, keepdims=True)[None], (32, 1, HW))


def unit_back_body(
    at_ref,
    len_ref,
    krot_ref,
    vcast_ref,
    kproj_ref,
    qproj_ref,
    qrot_ref,
    attn_ref,
    unit_ref,
    oscale_ref,
    fg_ref,
    sv_ref,
    cos_ref,
    sin_ref,
    *refs,
):
    o_ref, q_refs, kv_ref = refs[0], refs[1:5], refs[5]
    gkv_ref, gq_ref, gr_ref, last_ref, send_ref, gc_scr, gq_scr, qr_scr, gp_scr = refs[6:]
    mask, even = block_mask()
    unit = unit_ref[...]
    gu = sv_ref[...] * fg_ref[...]
    gr = oscale_ref[:, 0:1] * (gu - unit * jnp.mean(gu * unit, axis=-1, keepdims=True))
    gr_ref[...] = gr
    gc_scr[...] = dot(gr.astype(BF16), o_ref[...])
    qr_scr[...] = qrot_ref[...].astype(F32)
    blocks = []
    for p in range(BOTH):
        rows = slice(p * SEQ, (p + 1) * SEQ)
        gb = to_blocks(gc_scr[p : p + 1, :], mask, even).astype(BF16)
        blocks.append(gb)
        gp_scr[p * 8 : (p + 1) * 8, :] = dot(gb, vcast_ref[rows, :], LAST)
    w = attn_ref[...]
    gp = gp_scr[...]
    spread = jnp.sum(w * gp, axis=-1, keepdims=True)
    dls = (w * (gp - spread)).astype(BF16)
    probs = w.astype(BF16)
    for p in range(BOTH):
        rows = slice(p * SEQ, (p + 1) * SEQ)
        eight = slice(p * 8, (p + 1) * 8)
        qb = to_blocks(qr_scr[p : p + 1, :], mask, even).astype(BF16)
        gkv_ref[rows, 256:512] = dot(probs[eight, :], blocks[p], FIRST)
        dl = dls[eight, :]
        gq_scr[p : p + 1, :] = from_blocks(dot(dl, krot_ref[rows, :]) * SCALE, mask, even)
        gk = dot(dl, qb, FIRST) * SCALE
        for g in range(2):
            cols = slice(g * HW, (g + 1) * HW)
            k = kproj_ref[rows, cols]
            sc = lax.rsqrt(jnp.mean(k * k, axis=-1, keepdims=True) + EPS)
            u = k * sc
            r = gk[:, cols]
            t = r * cos_ref[...] + half_turn(r * sin_ref[...])
            gkv_ref[rows, cols] = sc * (t - u * jnp.mean(t * u, axis=-1, keepdims=True))
    cos_q, sin_q = query_tables(len_ref, cos_ref, sin_ref)
    for h in range(4):
        q = qproj_ref[:, h * HW : (h + 1) * HW]
        sc = lax.rsqrt(jnp.mean(q * q, axis=-1, keepdims=True) + EPS)
        u = q * sc
        r = gq_scr[:, h * HW : (h + 1) * HW]
        t = r * cos_q + half_turn(r * sin_q)
        gq_ref[:, h * HW : (h + 1) * HW] = sc * (
            t - u * jnp.mean(t * u, axis=-1, keepdims=True)
        )
    gqb = gq_ref[...].astype(BF16)
    for d in range(4):
        last_ref[:, block_at(at_ref[1], -d, 256)] = dot(gqb, q_refs[d][:, 0:512], LAST)

    gn = dot(gkv_ref[ROWS : 2 * ROWS, :].astype(BF16), kv_ref[:, 0:512], LAST)
    send_ref[...] = gn.astype(BF16)


def weight_body(
    at_ref,
    tot_ref,
    score_ref,
    teach_ref,
    gkv_ref,
    gq_ref,
    gr_ref,
    grturn_ref,
    turned_ref,
    turned_other_ref,
    nlast_ref,
    ctx_ref,
    *refs,
):
    out_a, outs_b, loss_ref, skv_ref, g_ref, sr_ref = refs[0], refs[1:5], *refs[5:9]
    srow_scr, sturn_scr, sq_scr, b_scr = refs[9:]
    x = at_ref[1]
    lane = lax.broadcasted_iota(jnp.int32, (1, HW), 1)

    def pick(v, i):
        return jnp.sum(jnp.where(lane == i, v, 0.0), axis=-1, keepdims=True)

    t = tot_ref[0]
    for i in range(1, 32):
        t = t + tot_ref[i]
    ts, tt, cr = pick(t, 0), pick(t, 1), pick(t, 2)
    loss_ref[...] = jnp.broadcast_to(cr / tt - jnp.log(tt) + jnp.log(ts), (8, HW))
    row = lax.broadcasted_iota(jnp.int32, (8, HW), 0)
    g = GRAD_SCALE * (jnp.exp(score_ref[...]) / ts - jnp.exp(teach_ref[...] / 2.0) / tt)
    gcol = g[:, 0:1]
    sr = gr_ref[...] * gcol
    sr_ref[...] = sr
    g_ref[...] = g
    sq_scr[...] = (gq_ref[...] * gcol).astype(BF16)
    srow_scr[...] = sr.astype(BF16)
    sturn_scr[...] = (grturn_ref[...] * gcol).astype(BF16)
    for p in range(BOTH):
        rows = slice(p * SEQ, (p + 1) * SEQ)
        skv_ref[rows, :] = (gkv_ref[rows, :] * gcol[p : p + 1, :]).astype(BF16)

    kv = dot(turned_ref[...], skv_ref[0:ROWS, :]) + dot(
        turned_other_ref[...], skv_ref[ROWS : 2 * ROWS, :]
    )
    out_a[:, :, 0:512] = kv.astype(BF16).reshape(4, 256, 512)
    o_low = dot(srow_scr[...], ctx_ref[:, 0:LOW], FIRST)
    out_a[:, :, 512:WA] = o_low.astype(BF16).reshape(4, 256, LOW)
    q = dot(nlast_ref[...], sq_scr[...], FIRST)
    b_scr[:, :, 0:512] = q.astype(BF16).reshape(4, 256, 512)
    o_high = dot(sturn_scr[...], ctx_ref[:, LOW:512], FIRST)
    b_scr[:, :, 512:WB] = o_high.astype(BF16).reshape(4, 256, 512 - LOW)
    for d in range(4):
        outs_b[d][...] = b_scr[lax.rem(x + d, 4)]


def middle_body(at_ref, loss_ref, got_a_ref, *refs):
    b_refs, out_a, out_b, a_scr = refs[0:4], refs[4:8], refs[8], refs[9]
    x = at_ref[1]
    total_a = got_a_ref[0].astype(F32)
    total_b = b_refs[0][...].astype(F32)
    for d in range(1, 4):
        total_a = total_a + got_a_ref[d].astype(F32)
        total_b = total_b + b_refs[d][...].astype(F32)
    out_b[:, 0:64, :] = total_b.reshape(4, 64, WB).astype(BF16)
    rest = jnp.broadcast_to(loss_ref[0:1, 0:1], (16, WB))
    lane = lax.broadcasted_iota(jnp.int32, (16, WB), 1)
    parts = jnp.zeros((16, WB), F32)
    for i in range(3):
        part = rest.astype(BF16).astype(F32)
        parts = jnp.where(lane == i, part, parts)
        rest = rest - part
    for y in range(4):
        out_b[y, 64:80, :] = parts.astype(BF16)
    a_scr[...] = total_a.reshape(8, 4, 8, WA)
    for d in range(4):
        out_a[d][...] = a_scr[:, pl.ds(lax.rem(x + d, 4), 1)].reshape(64, WA).astype(BF16)


def hidden_body(len_ref, h_ref, gain_ref, skv_ref, g_ref, last_ref, other_ref, sr_ref, kv_ref, got_ref, out_ref):
    pos = lax.broadcasted_iota(jnp.int32, (SEQ, 1), 0)

    @pl.loop(0, PAIRS)
    def _(p):
        rows = pl.ds(pl.multiple_of(p * SEQ, SEQ), SEQ)
        at = pos == len_ref[p] - 1
        last = last_ref[pl.ds(p, 1), :] + other_ref[pl.ds(PAIRS + p, 1), :]
        unit = got_ref[rows, :].astype(F32) + jnp.where(at, last, 0.0)
        gn = dot(skv_ref[rows, :], kv_ref[:, 0:512], LAST) + g_ref[pl.ds(p, 1), 0:1] * unit
        x = h_ref[rows, :].astype(F32)
        inv = lax.rsqrt(jnp.mean(x * x, axis=-1, keepdims=True) + EPS)
        s = gn * gain_ref[...]
        gi = inv * s - x * (inv * inv * inv * jnp.mean(s * x, axis=-1, keepdims=True))
        gi = gi + jnp.where(at, sr_ref[pl.ds(p, 1), :], 0.0)
        out_ref[rows, :] = gi.astype(BF16)


def finish_body(rec_ref, gq_ref, gk_ref, gv_ref, go_ref):
    for h in range(2):
        total = rec_ref[0, h].astype(F32)
        for z in range(1, 8):
            total = total + rec_ref[z, h].astype(F32)
        gk_ref[:, h * 256 : h * 256 + 256] = total[:, 0:256]
        gv_ref[:, h * 256 : h * 256 + 256] = total[:, 256:512]
        go_ref[:, h * 512 : h * 512 + LOW] = total[:, 512:WA]
        gq_ref[:, h * 512 : h * 512 + 512] = total[:, WA : WA + 512]
        go_ref[:, h * 512 + LOW : h * 512 + 512] = total[:, WA + 512 : 1536]


def everyone(x, axes, count):
    return lax.all_to_all(
        jnp.broadcast_to(x[None], (count, *x.shape)), axes, 0, 0, tiled=True
    )


def from_ring(x, axis):
    return [x] + [
        lax.ppermute(x, axis, [(i, (i + d) % 4) for i in range(4)]) for d in range(1, 4)
    ]


def along_ring(pieces, axis):
    return [pieces[0]] + [
        lax.ppermute(pieces[d], axis, [(i, (i + d) % 4) for i in range(4)]) for d in range(1, 4)
    ]


def chunk_turn(v):
    return jnp.transpose(v.reshape(8, 32, 4, 8), (0, 2, 1, 3)).reshape(8, D)


def chunk_back(v):
    return jnp.transpose(v.reshape(8, 4, 32, 8), (0, 2, 1, 3)).reshape(8, D)


def swap(x):
    return lax.ppermute(x, "c", [(0, 1), (1, 0)])


def shards(
    hidden,
    lengths,
    teacher,
    norm_gain,
    final_gain,
    score_vector,
    query_weight,
    key_matrix,
    value_matrix,
    out_weight,
):
    at = jnp.stack([lax.axis_index("pb"), lax.axis_index("x")]).astype(jnp.int32)
    tokens = hidden.reshape(ROWS, D)
    lens = lengths[0]
    gain = norm_gain[None]
    fg = final_gain[None]
    sv = score_vector[None]
    cos_np, sin_np = rope_consts()
    cos, sin = jnp.asarray(cos_np), jnp.asarray(sin_np)
    (both_halves,) = call(
        pack_body,
        [],
        [key_matrix, value_matrix, query_weight, out_weight.T],
        [((8, 2, 4, 1536), BF16)],
        grant=62,
    )
    both_halves = both_halves.reshape(16, 4, 1536)
    column = lax.all_to_all(both_halves, ("z", "c"), 0, 0, tiled=True).reshape(64, 1536)
    normed, turned, nlast, xlast = call(
        prep_body,
        [lens],
        [tokens, gain],
        [((ROWS, D), BF16), ((D, ROWS), BF16), ((8, D), BF16), ((8, D), F32)],
        flops=10_000_000,
    )
    nlast = chunk_turn(nlast)
    wide = (PAIRS, HW)
    pack = jnp.concatenate(
        [
            xlast[0:PAIRS],
            nlast[0:PAIRS].astype(F32),
            jnp.broadcast_to(lens.astype(F32)[:, None], wide),
            jnp.broadcast_to(teacher[0][:, None], wide),
        ],
        axis=1,
    )
    column, normed, turned, pack = lax.optimization_barrier((column, normed, turned, pack))
    other = swap(normed)
    got = swap(pack)
    slab_b = everyone(column[:, WA:1536], "pb", 4).reshape(256, WB)
    ring_a = from_ring(column[:, 0:WA], "x")
    (slab_a,) = call(arrange_body, [at], ring_a, [((4, 256, WA), BF16)], [((8, 4, 8, WA), BF16)], grant=10)
    slab_a, slab_b, got = lax.optimization_barrier((slab_a, slab_b, got))
    packed = jnp.concatenate([pack, got], axis=0)
    xlast = packed[:, 0:1024]
    nlast = packed[:, 1024:2048].astype(BF16)
    lens_both = packed[:, 2048].astype(jnp.int32)
    teach = packed[:, 2048 + HW :]
    kvo = lax.all_to_all(slab_a, "pb", 0, 0, tiled=True).reshape(1024, WA)
    qo = from_ring(slab_b, "x")

    kproj, krot, vcast, qproj, qrot, attn, ctx, attended, oa = call(
        attend_body,
        [at, lens_both],
        [normed, other, nlast, cos, sin, kvo, *qo],
        [
            ((2 * ROWS, 256), F32),
            ((2 * ROWS, 256), BF16),
            ((2 * ROWS, 256), BF16),
            ((8, 512), F32),
            ((8, 512), BF16),
            ((64, SEQ), F32),
            ((8, 512), BF16),
            ((8, D), F32),
            ((D, 512), BF16),
        ],
        [((8, 512), F32), ((8, 512), F32), ((32, 4, 8, 512 - LOW), BF16), ((8 * BOTH, SEQ), F32)],
        flops=1_100_000_000,
    )
    ctx, turned_late = lax.optimization_barrier((ctx, turned))
    turned_other = swap(turned_late)
    unit, oscale, score, tot, line = call(
        score_body,
        [],
        [teach, attended, swap(attended), xlast, fg, sv],
        [((8, D), F32), ((8, HW), F32), ((8, HW), F32), ((32, 1, HW), F32), ((1, PAIRS), F32)],
        flops=1_000_000,
    )

    totals = lax.all_to_all(tot, ("z", "x"), 0, 0, tiled=True)

    gkv, gq, gr, last, send = call(
        unit_back_body,
        [at, lens_both],
        [krot, vcast, kproj, qproj, qrot, attn, unit, oscale, fg, sv, cos, sin, oa, *qo, kvo],
        [((2 * ROWS, 512), F32), ((8, 512), F32), ((8, D), F32), ((8, D), F32), ((ROWS, D), BF16)],
        [((8, 512), F32), ((8, 512), F32), ((8, 512), F32), ((8 * BOTH, SEQ), F32)],
        flops=200_000_000,
    )
    grturn = chunk_turn(gr)
    last = chunk_back(last)
    got = swap(send)

    pieces = ((4, 256, WA), BF16)
    chip_a, *rest = call(
        weight_body,
        [at],
        [totals, score, teach, gkv, gq, gr, grturn, turned, turned_other, nlast, ctx],
        [pieces]
        + [((256, WB), BF16)] * 4
        + [((8, HW), F32), ((ROWS * 2, 512), BF16), ((8, HW), F32), ((8, D), F32)],
        [((8, D), BF16), ((8, D), BF16), ((8, 512), BF16), ((4, 256, WB), BF16)],
        flops=1_100_000_000,
    )
    chip_b, (loss, skv, g, sr) = rest[0:4], rest[4:]
    got_a = lax.all_to_all(chip_a, "pb", 0, 0, tiled=True)
    got_b = along_ring(chip_b, "x")
    (grad_hidden,) = call(
        hidden_body,
        [lens_both],
        [tokens, gain, skv, g, last, swap(last), sr, kvo, got],
        [((ROWS, D), BF16)],
        flops=600_000_000,
    )
    got_a, got_b, grad_hidden = lax.optimization_barrier((got_a, got_b, grad_hidden))
    *mid_a, mid_b = call(
        middle_body,
        [at],
        [loss, got_a, *got_b],
        [((64, WA), BF16)] * 4 + [((4, 80, WB), BF16)],
        [((8, 4, 8, WA), F32)],
        grant=52,
    )
    done_a = along_ring(mid_a, "x")
    done_b = lax.all_to_all(mid_b, "pb", 0, 0, tiled=True)
    loss = jnp.sum(done_b[:, 64, 0:3].astype(F32), axis=1)
    loss = (loss[0] + loss[1]) + (loss[2] + loss[3])
    done_b = done_b[:, 0:64]

    def added(parts):
        total = parts[0].astype(F32)
        for part in parts[1:]:
            total = total + part.astype(F32)
        return total.astype(BF16)

    part = jnp.concatenate([added(done_a), added(done_b)], axis=1)
    rec = lax.all_to_all(part.reshape(16, 4, 1536), ("z", "c"), 0, 0, tiled=True)
    grad_query, grad_key, grad_value, grad_out = call(
        finish_body,
        [],
        [rec.reshape(8, 2, 4, 1536)],
        [((4, D), F32), ((4, 512), F32), ((4, 512), F32), ((4, D), F32)],
    )

    return (
        line,
        loss,
        grad_hidden.reshape(hidden.shape),
        grad_query,
        grad_key,
        grad_value,
        grad_out.T,
    )


def solution(mesh):
    torus = Mesh(mesh.devices.reshape(mesh.shape["pb"], 8, 4, 2), AXES)
    placed = (
        P("pb", NEG, None, None),
        P("pb", NEG),
        P("pb", NEG),
        P(),
        P(),
        P(),
        P(AXES, None),
        P(AXES, None),
        P(AXES, None),
        P(None, AXES),
    )
    return jax.shard_map(
        shards,
        mesh=torus,
        in_specs=placed,
        out_specs=(
            P("pb", NEG),
            P(),
            P("pb", NEG, None, None),
            P(AXES, None),
            P(AXES, None),
            P(AXES, None),
            P(None, AXES),
        ),
        check_vma=False,
    )
```

```python
import jax
import jax.numpy as jnp
import numpy as np
from jax import lax
from jax.experimental import pallas as pl
from jax.experimental.pallas import tpu as pltpu
from jax.sharding import Mesh
from jax.sharding import PartitionSpec as P

HW = 128
AXES = ("pb", "z", "x", "c")
NEG = ("z", "x", "c")
EPS = 1e-06
ROPE_BASE = 1000000.0
GRAD_SCALE = 512.0
PAIRS = 4
SEQ = 128
D = 1024
ROWS = PAIRS * SEQ
BOTH = 2 * PAIRS
LOW = 256
WA = 512 + LOW
WB = 1024 - LOW
F32 = jnp.float32
BF16 = jnp.bfloat16
SM = pl.BlockSpec(memory_space=pltpu.SMEM)
LAST = (((1,), (1,)), ((), ()))
FIRST = (((0,), (0,)), ((), ()))
SCALE = HW ** (-0.5)


def rope_consts():
    freqs = np.float32(ROPE_BASE) ** (-(np.arange(HW // 2, dtype=np.float32) * 2.0) / HW)
    angles = np.arange(SEQ, dtype=np.float32)[:, None] * freqs.astype(np.float32)[None, :]
    angles = np.concatenate([angles, angles], axis=1)
    sign = np.where(np.arange(HW) < HW // 2, -1.0, 1.0)
    return (
        np.cos(angles).astype(np.float32),
        (np.sin(angles) * sign[None, :]).astype(np.float32),
    )


def whole(shape):
    return pl.BlockSpec(shape, lambda i: (0,) * len(shape), pipeline_mode=pl.Buffered(1))


def call(body, scalars, arrays, outs, scratch=(), flops=0, grant=52):
    moved = sum(a.size * a.dtype.itemsize for a in arrays)
    moved += sum(int(np.prod(o)) * np.dtype(d).itemsize for o, d in outs)
    return pl.pallas_call(
        body,
        grid=(1,),
        out_shape=[jax.ShapeDtypeStruct(o, d) for o, d in outs],
        in_specs=[SM] * len(scalars) + [whole(a.shape) for a in arrays],
        out_specs=[whole(o) for o, _ in outs],
        scratch_shapes=[pltpu.VMEM(o, d) for o, d in scratch],
        compiler_params=pltpu.CompilerParams(vmem_limit_bytes=grant << 20),
        cost_estimate=pl.CostEstimate(flops=flops, bytes_accessed=moved, transcendentals=0),
    )(*scalars, *arrays)


def block_at(me, step, width):
    return pl.ds(pl.multiple_of(lax.rem(me + step + 4, 4) * width, width), width)


def dot(a, b, dims=(((1,), (0,)), ((), ()))):
    return lax.dot_general(a, b, dims, preferred_element_type=F32)


def half_turn(v):
    return pltpu.roll(v, HW // 2, 1)


def heads(v, n):
    return [v[:, i * HW : (i + 1) * HW] for i in range(n)]


def block_mask():
    row = lax.broadcasted_iota(jnp.int32, (8, 256), 0)
    lane = lax.broadcasted_iota(jnp.int32, (8, 256), 1)
    return (lane // HW) == (row // 2), (row % 2) == 0


def to_blocks(row, mask, even):
    h = heads(row, 4)
    e = jnp.broadcast_to(jnp.concatenate(h[0::2], axis=1), (8, 256))
    o = jnp.broadcast_to(jnp.concatenate(h[1::2], axis=1), (8, 256))
    return jnp.where(mask, jnp.where(even, e, o), 0.0)


def from_blocks(blocks, mask, even):
    e = jnp.sum(jnp.where(mask & even, blocks, 0.0), axis=0, keepdims=True)
    o = jnp.sum(jnp.where(mask & (~even), blocks, 0.0), axis=0, keepdims=True)
    return jnp.concatenate([e[:, 0:HW], o[:, 0:HW], e[:, HW:], o[:, HW:]], axis=1)


def query_tables(len_ref, cos_ref, sin_ref):
    return [
        jnp.concatenate([t[pl.ds(len_ref[p] - 1, 1), :] for p in range(BOTH)], axis=0)
        for t in (cos_ref, sin_ref)
    ]


def pack_body(k_ref, v_ref, q_ref, o_ref, out_ref):
    for h in range(2):
        wide, tall = slice(h * 256, h * 256 + 256), h * 512
        out_ref[0, h, :, 0:256] = k_ref[:, wide]
        out_ref[0, h, :, 256:512] = v_ref[:, wide]
        out_ref[0, h, :, 512:WA] = o_ref[:, tall : tall + LOW]
        out_ref[0, h, :, WA : WA + 512] = q_ref[:, tall : tall + 512]
        out_ref[0, h, :, WA + 512 : 1536] = o_ref[:, tall + LOW : tall + 512]
    for z in range(1, 8):
        out_ref[z] = out_ref[0]


def prep_body(len_ref, h_ref, gain_ref, normed_ref, turned_ref, nlast_ref, xlast_ref):
    row = lax.broadcasted_iota(jnp.int32, (8, SEQ), 0)
    lane = lax.broadcasted_iota(jnp.int32, (8, SEQ), 1)
    nl = jnp.zeros((8, D), F32)
    xl = jnp.zeros((8, D), F32)
    for p in range(PAIRS):
        raw = h_ref[p * SEQ : (p + 1) * SEQ, :]
        x = raw.astype(F32)
        inv = lax.rsqrt(jnp.mean(x * x, axis=-1, keepdims=True) + EPS)
        n = (x * inv * gain_ref[...]).astype(BF16)
        normed_ref[p * SEQ : (p + 1) * SEQ, :] = n
        turned_ref[:, p * SEQ : (p + 1) * SEQ] = n.T
        e = len_ref[p] - 1
        hot = jnp.where((row == p) & (lane == e), 1.0, 0.0).astype(BF16)
        nl = nl + dot(hot, n)
        xl = xl + dot(hot, raw)
    nlast_ref[...] = nl.astype(BF16)
    xlast_ref[...] = xl


def arrange_body(at_ref, *refs):
    a_refs, out_ref, slab_scr = refs[0:4], refs[4], refs[5]
    x = at_ref[1]
    for d in range(4):
        slab_scr[:, pl.ds(lax.rem(x - d + 4, 4), 1)] = a_refs[d][...].reshape(8, 1, 8, WA)
    slab = slab_scr[...].reshape(256, WA)
    for y in range(4):
        out_ref[y] = slab


def attend_body(
    at_ref, len_ref, normed_ref, other_ref, nlast_ref, cos_ref, sin_ref, kv_ref, *refs
):
    out_ref, o_ref, turn_scr, lg_scr = refs[11], refs[12], refs[15], refs[16]
    q_refs = refs[0:4]
    kproj_ref, krot_ref, vcast_ref, qproj_ref, qrot_ref, attn_ref, ctx_ref = refs[4:11]
    qr_scr, ctx_scr = refs[13:15]
    x = at_ref[1]
    mask, even = block_mask()
    lane = lax.broadcasted_iota(jnp.int32, (8 * BOTH, SEQ), 1)
    for side, rows_ref in enumerate((normed_ref, other_ref)):
        here = slice(side * ROWS, (side + 1) * ROWS)
        kv = dot(rows_ref[...], kv_ref[:, 0:512])
        kproj_ref[here, :] = kv[:, 0:256]
        vcast_ref[here, :] = kv[:, 256:512].astype(BF16)

    q = jnp.zeros((8, 512), F32)
    for d in range(4):
        q = q + dot(nlast_ref[:, block_at(x, -d, 256)], q_refs[d][:, 0:512])
    qproj_ref[...] = q
    cos_q, sin_q = query_tables(len_ref, cos_ref, sin_ref)
    for h in range(4):
        q = qproj_ref[:, h * HW : (h + 1) * HW]
        u = q * lax.rsqrt(jnp.mean(q * q, axis=-1, keepdims=True) + EPS)
        r = u * cos_q + half_turn(u) * sin_q
        qr_scr[:, h * HW : (h + 1) * HW] = r
        qrot_ref[:, h * HW : (h + 1) * HW] = r.astype(BF16)
    for p in range(BOTH):
        rows = slice(p * SEQ, (p + 1) * SEQ)
        for g in range(2):
            k = kproj_ref[rows, g * HW : (g + 1) * HW]
            u = k * lax.rsqrt(jnp.mean(k * k, axis=-1, keepdims=True) + EPS)
            r = u * cos_ref[...] + half_turn(u) * sin_ref[...]
            krot_ref[rows, g * HW : (g + 1) * HW] = r.astype(BF16)
    for p in range(BOTH):
        rows = slice(p * SEQ, (p + 1) * SEQ)
        qb = to_blocks(qr_scr[p : p + 1, :], mask, even).astype(BF16)
        lg_scr[p * 8 : (p + 1) * 8, :] = dot(qb, krot_ref[rows, :], LAST)
    last = jnp.concatenate(
        [jnp.full((8, SEQ), len_ref[p] - 1, jnp.int32) for p in range(BOTH)], axis=0
    )
    ex = jnp.where(lane <= last, jnp.exp(lg_scr[...] * SCALE), 0.0)
    w = ex / jnp.sum(ex, axis=-1, keepdims=True)
    attn_ref[...] = w
    probs = w.astype(BF16)
    for p in range(BOTH):
        c = dot(probs[p * 8 : (p + 1) * 8, :], vcast_ref[p * SEQ : (p + 1) * SEQ, :])
        ctx_scr[p : p + 1, :] = from_blocks(c, mask, even)
    ctx_ref[...] = ctx_scr[...].astype(BF16)
    for d in range(4):
        turn_scr[:, pl.ds(lax.rem(x - d + 4, 4), 1)] = q_refs[d][:, 512:WB].reshape(
            32, 1, 8, 512 - LOW
        )
    o_ref[:, 0:LOW] = kv_ref[:, 512:WA]
    o_ref[:, LOW:512] = turn_scr[...].reshape(1024, 512 - LOW)
    out_ref[...] = dot(ctx_ref[...], o_ref[...], LAST)


def score_body(teach_ref, mine_ref, theirs_ref, xlast_ref, fg_ref, sv_ref, *refs):
    unit_ref, oscale_ref, score_ref, tot_ref, line_ref = refs
    res = xlast_ref[...] + (mine_ref[...] + pltpu.roll(theirs_ref[...], PAIRS, 0))
    sc = lax.rsqrt(jnp.mean(res * res, axis=-1, keepdims=True) + EPS)
    unit = res * sc
    unit_ref[...] = unit
    oscale_ref[...] = jnp.broadcast_to(sc, (8, HW))
    s = jnp.sum(unit * fg_ref[...] * sv_ref[...], axis=-1, keepdims=True)
    s = jnp.broadcast_to(s, (8, HW))
    score_ref[...] = s
    row = lax.broadcasted_iota(jnp.int32, (8, HW), 0)
    lane = lax.broadcasted_iota(jnp.int32, (8, HW), 1)
    line_ref[...] = jnp.sum(jnp.where(row == lane, s, 0.0), axis=0, keepdims=True)[:, 0:PAIRS]
    scaled = teach_ref[...] / 2.0
    es = jnp.exp(s)
    et = jnp.exp(scaled)
    v = jnp.where(lane == 0, es, jnp.where(lane == 1, et, et * (scaled - s)))
    v = jnp.where(lane < 3, v + pltpu.roll(v, PAIRS, 0), 0.0)
    tot_ref[...] = jnp.broadcast_to(jnp.sum(v[0:PAIRS], axis=0, keepdims=True)[None], (32, 1, HW))


def unit_back_body(
    at_ref,
    len_ref,
    krot_ref,
    vcast_ref,
    kproj_ref,
    qproj_ref,
    qrot_ref,
    attn_ref,
    unit_ref,
    oscale_ref,
    fg_ref,
    sv_ref,
    cos_ref,
    sin_ref,
    *refs,
):
    o_ref, q_refs, kv_ref = refs[0], refs[1:5], refs[5]
    gkv_ref, gq_ref, gr_ref, last_ref, send_ref, gc_scr, gq_scr, qr_scr, gp_scr = refs[6:]
    mask, even = block_mask()
    unit = unit_ref[...]
    gu = sv_ref[...] * fg_ref[...]
    gr = oscale_ref[:, 0:1] * (gu - unit * jnp.mean(gu * unit, axis=-1, keepdims=True))
    gr_ref[...] = gr
    gc_scr[...] = dot(gr.astype(BF16), o_ref[...])
    qr_scr[...] = qrot_ref[...].astype(F32)
    blocks = []
    for p in range(BOTH):
        rows = slice(p * SEQ, (p + 1) * SEQ)
        gb = to_blocks(gc_scr[p : p + 1, :], mask, even).astype(BF16)
        blocks.append(gb)
        gp_scr[p * 8 : (p + 1) * 8, :] = dot(gb, vcast_ref[rows, :], LAST)
    w = attn_ref[...]
    gp = gp_scr[...]
    spread = jnp.sum(w * gp, axis=-1, keepdims=True)
    dls = (w * (gp - spread)).astype(BF16)
    probs = w.astype(BF16)
    for p in range(BOTH):
        rows = slice(p * SEQ, (p + 1) * SEQ)
        eight = slice(p * 8, (p + 1) * 8)
        qb = to_blocks(qr_scr[p : p + 1, :], mask, even).astype(BF16)
        gkv_ref[rows, 256:512] = dot(probs[eight, :], blocks[p], FIRST)
        dl = dls[eight, :]
        gq_scr[p : p + 1, :] = from_blocks(dot(dl, krot_ref[rows, :]) * SCALE, mask, even)
        gk = dot(dl, qb, FIRST) * SCALE
        for g in range(2):
            cols = slice(g * HW, (g + 1) * HW)
            k = kproj_ref[rows, cols]
            sc = lax.rsqrt(jnp.mean(k * k, axis=-1, keepdims=True) + EPS)
            u = k * sc
            r = gk[:, cols]
            t = r * cos_ref[...] + half_turn(r * sin_ref[...])
            gkv_ref[rows, cols] = sc * (t - u * jnp.mean(t * u, axis=-1, keepdims=True))
    cos_q, sin_q = query_tables(len_ref, cos_ref, sin_ref)
    for h in range(4):
        q = qproj_ref[:, h * HW : (h + 1) * HW]
        sc = lax.rsqrt(jnp.mean(q * q, axis=-1, keepdims=True) + EPS)
        u = q * sc
        r = gq_scr[:, h * HW : (h + 1) * HW]
        t = r * cos_q + half_turn(r * sin_q)
        gq_ref[:, h * HW : (h + 1) * HW] = sc * (
            t - u * jnp.mean(t * u, axis=-1, keepdims=True)
        )
    gqb = gq_ref[...].astype(BF16)
    for d in range(4):
        last_ref[:, block_at(at_ref[1], -d, 256)] = dot(gqb, q_refs[d][:, 0:512], LAST)

    gn = dot(gkv_ref[ROWS : 2 * ROWS, :].astype(BF16), kv_ref[:, 0:512], LAST)
    send_ref[...] = gn.astype(BF16)


def weight_body(
    at_ref,
    tot_ref,
    score_ref,
    teach_ref,
    gkv_ref,
    gq_ref,
    gr_ref,
    grturn_ref,
    turned_ref,
    turned_other_ref,
    nlast_ref,
    ctx_ref,
    *refs,
):
    out_a, outs_b, loss_ref, skv_ref, g_ref, sr_ref = refs[0], refs[1:5], *refs[5:9]
    srow_scr, sturn_scr, sq_scr, b_scr = refs[9:]
    x = at_ref[1]
    lane = lax.broadcasted_iota(jnp.int32, (1, HW), 1)

    def pick(v, i):
        return jnp.sum(jnp.where(lane == i, v, 0.0), axis=-1, keepdims=True)

    t = tot_ref[0]
    for i in range(1, 32):
        t = t + tot_ref[i]
    ts, tt, cr = pick(t, 0), pick(t, 1), pick(t, 2)
    loss_ref[...] = jnp.broadcast_to(cr / tt - jnp.log(tt) + jnp.log(ts), (8, HW))
    row = lax.broadcasted_iota(jnp.int32, (8, HW), 0)
    g = GRAD_SCALE * (jnp.exp(score_ref[...]) / ts - jnp.exp(teach_ref[...] / 2.0) / tt)
    gcol = g[:, 0:1]
    sr = gr_ref[...] * gcol
    sr_ref[...] = sr
    g_ref[...] = g
    sq_scr[...] = (gq_ref[...] * gcol).astype(BF16)
    srow_scr[...] = sr.astype(BF16)
    sturn_scr[...] = (grturn_ref[...] * gcol).astype(BF16)
    for p in range(BOTH):
        rows = slice(p * SEQ, (p + 1) * SEQ)
        skv_ref[rows, :] = (gkv_ref[rows, :] * gcol[p : p + 1, :]).astype(BF16)

    kv = dot(turned_ref[...], skv_ref[0:ROWS, :]) + dot(
        turned_other_ref[...], skv_ref[ROWS : 2 * ROWS, :]
    )
    out_a[:, :, 0:512] = kv.astype(BF16).reshape(4, 256, 512)
    o_low = dot(srow_scr[...], ctx_ref[:, 0:LOW], FIRST)
    out_a[:, :, 512:WA] = o_low.astype(BF16).reshape(4, 256, LOW)
    q = dot(nlast_ref[...], sq_scr[...], FIRST)
    b_scr[:, :, 0:512] = q.astype(BF16).reshape(4, 256, 512)
    o_high = dot(sturn_scr[...], ctx_ref[:, LOW:512], FIRST)
    b_scr[:, :, 512:WB] = o_high.astype(BF16).reshape(4, 256, 512 - LOW)
    for d in range(4):
        outs_b[d][...] = b_scr[lax.rem(x + d, 4)]


def middle_body(at_ref, loss_ref, got_a_ref, *refs):
    b_refs, out_a, out_b, a_scr = refs[0:4], refs[4:8], refs[8], refs[9]
    x = at_ref[1]
    total_a = got_a_ref[0].astype(F32)
    total_b = b_refs[0][...].astype(F32)
    for d in range(1, 4):
        total_a = total_a + got_a_ref[d].astype(F32)
        total_b = total_b + b_refs[d][...].astype(F32)
    out_b[:, 0:64, :] = total_b.reshape(4, 64, WB).astype(BF16)
    rest = jnp.broadcast_to(loss_ref[0:1, 0:1], (16, WB))
    lane = lax.broadcasted_iota(jnp.int32, (16, WB), 1)
    parts = jnp.zeros((16, WB), F32)
    for i in range(3):
        part = rest.astype(BF16).astype(F32)
        parts = jnp.where(lane == i, part, parts)
        rest = rest - part
    for y in range(4):
        out_b[y, 64:80, :] = parts.astype(BF16)
    a_scr[...] = total_a.reshape(8, 4, 8, WA)
    for d in range(4):
        out_a[d][...] = a_scr[:, pl.ds(lax.rem(x + d, 4), 1)].reshape(64, WA).astype(BF16)


def hidden_body(len_ref, h_ref, gain_ref, skv_ref, g_ref, last_ref, other_ref, sr_ref, kv_ref, got_ref, out_ref):
    pos = lax.broadcasted_iota(jnp.int32, (SEQ, 1), 0)

    @pl.loop(0, PAIRS)
    def _(p):
        rows = pl.ds(pl.multiple_of(p * SEQ, SEQ), SEQ)
        at = pos == len_ref[p] - 1
        last = last_ref[pl.ds(p, 1), :] + other_ref[pl.ds(PAIRS + p, 1), :]
        unit = got_ref[rows, :].astype(F32) + jnp.where(at, last, 0.0)
        gn = dot(skv_ref[rows, :], kv_ref[:, 0:512], LAST) + g_ref[pl.ds(p, 1), 0:1] * unit
        x = h_ref[rows, :].astype(F32)
        inv = lax.rsqrt(jnp.mean(x * x, axis=-1, keepdims=True) + EPS)
        s = gn * gain_ref[...]
        gi = inv * s - x * (inv * inv * inv * jnp.mean(s * x, axis=-1, keepdims=True))
        gi = gi + jnp.where(at, sr_ref[pl.ds(p, 1), :], 0.0)
        out_ref[rows, :] = gi.astype(BF16)


def finish_body(rec_ref, gq_ref, gk_ref, gv_ref, go_ref):
    for h in range(2):
        total = rec_ref[0, h].astype(F32)
        for z in range(1, 8):
            total = total + rec_ref[z, h].astype(F32)
        gk_ref[:, h * 256 : h * 256 + 256] = total[:, 0:256]
        gv_ref[:, h * 256 : h * 256 + 256] = total[:, 256:512]
        go_ref[:, h * 512 : h * 512 + LOW] = total[:, 512:WA]
        gq_ref[:, h * 512 : h * 512 + 512] = total[:, WA : WA + 512]
        go_ref[:, h * 512 + LOW : h * 512 + 512] = total[:, WA + 512 : 1536]


def everyone(x, axes, count):
    return lax.all_to_all(
        jnp.broadcast_to(x[None], (count, *x.shape)), axes, 0, 0, tiled=True
    )


def from_ring(x, axis):
    return [x] + [
        lax.ppermute(x, axis, [(i, (i + d) % 4) for i in range(4)]) for d in range(1, 4)
    ]


def along_ring(pieces, axis):
    return [pieces[0]] + [
        lax.ppermute(pieces[d], axis, [(i, (i + d) % 4) for i in range(4)]) for d in range(1, 4)
    ]


def chunk_turn(v):
    return jnp.transpose(v.reshape(8, 32, 4, 8), (0, 2, 1, 3)).reshape(8, D)


def chunk_back(v):
    return jnp.transpose(v.reshape(8, 4, 32, 8), (0, 2, 1, 3)).reshape(8, D)


def swap(x):
    return lax.ppermute(x, "c", [(0, 1), (1, 0)])


def shards(
    hidden,
    lengths,
    teacher,
    norm_gain,
    final_gain,
    score_vector,
    query_weight,
    key_matrix,
    value_matrix,
    out_weight,
):
    at = jnp.stack([lax.axis_index("pb"), lax.axis_index("x")]).astype(jnp.int32)
    tokens = hidden.reshape(ROWS, D)
    lens = lengths[0]
    gain = norm_gain[None]
    fg = final_gain[None]
    sv = score_vector[None]
    cos_np, sin_np = rope_consts()
    cos, sin = jnp.asarray(cos_np), jnp.asarray(sin_np)
    (both_halves,) = call(
        pack_body,
        [],
        [key_matrix, value_matrix, query_weight, out_weight.T],
        [((8, 2, 4, 1536), BF16)],
        grant=62,
    )
    both_halves = both_halves.reshape(16, 4, 1536)
    column = lax.all_to_all(both_halves, ("z", "c"), 0, 0, tiled=True).reshape(64, 1536)
    normed, turned, nlast, xlast = call(
        prep_body,
        [lens],
        [tokens, gain],
        [((ROWS, D), BF16), ((D, ROWS), BF16), ((8, D), BF16), ((8, D), F32)],
        flops=10_000_000,
    )
    nlast = chunk_turn(nlast)
    wide = (PAIRS, HW)
    pack = jnp.concatenate(
        [
            xlast[0:PAIRS],
            nlast[0:PAIRS].astype(F32),
            jnp.broadcast_to(lens.astype(F32)[:, None], wide),
            jnp.broadcast_to(teacher[0][:, None], wide),
        ],
        axis=1,
    )
    column, normed, turned, pack = lax.optimization_barrier((column, normed, turned, pack))
    other = swap(normed)
    got = swap(pack)
    slab_b = everyone(column[:, WA:1536], "pb", 4).reshape(256, WB)
    ring_a = from_ring(column[:, 0:WA], "x")
    (slab_a,) = call(arrange_body, [at], ring_a, [((4, 256, WA), BF16)], [((8, 4, 8, WA), BF16)], grant=10)
    slab_a, slab_b, got = lax.optimization_barrier((slab_a, slab_b, got))
    packed = jnp.concatenate([pack, got], axis=0)
    xlast = packed[:, 0:1024]
    nlast = packed[:, 1024:2048].astype(BF16)
    lens_both = packed[:, 2048].astype(jnp.int32)
    teach = packed[:, 2048 + HW :]
    kvo = lax.all_to_all(slab_a, "pb", 0, 0, tiled=True).reshape(1024, WA)
    qo = from_ring(slab_b, "x")

    kproj, krot, vcast, qproj, qrot, attn, ctx, attended, oa = call(
        attend_body,
        [at, lens_both],
        [normed, other, nlast, cos, sin, kvo, *qo],
        [
            ((2 * ROWS, 256), F32),
            ((2 * ROWS, 256), BF16),
            ((2 * ROWS, 256), BF16),
            ((8, 512), F32),
            ((8, 512), BF16),
            ((64, SEQ), F32),
            ((8, 512), BF16),
            ((8, D), F32),
            ((D, 512), BF16),
        ],
        [((8, 512), F32), ((8, 512), F32), ((32, 4, 8, 512 - LOW), BF16), ((8 * BOTH, SEQ), F32)],
        flops=1_100_000_000,
    )
    ctx, turned_late = lax.optimization_barrier((ctx, turned))
    turned_other = swap(turned_late)
    unit, oscale, score, tot, line = call(
        score_body,
        [],
        [teach, attended, swap(attended), xlast, fg, sv],
        [((8, D), F32), ((8, HW), F32), ((8, HW), F32), ((32, 1, HW), F32), ((1, PAIRS), F32)],
        flops=1_000_000,
    )

    totals = lax.all_to_all(tot, ("z", "x"), 0, 0, tiled=True)

    gkv, gq, gr, last, send = call(
        unit_back_body,
        [at, lens_both],
        [krot, vcast, kproj, qproj, qrot, attn, unit, oscale, fg, sv, cos, sin, oa, *qo, kvo],
        [((2 * ROWS, 512), F32), ((8, 512), F32), ((8, D), F32), ((8, D), F32), ((ROWS, D), BF16)],
        [((8, 512), F32), ((8, 512), F32), ((8, 512), F32), ((8 * BOTH, SEQ), F32)],
        flops=200_000_000,
    )
    grturn = chunk_turn(gr)
    last = chunk_back(last)
    got = swap(send)

    pieces = ((4, 256, WA), BF16)
    chip_a, *rest = call(
        weight_body,
        [at],
        [totals, score, teach, gkv, gq, gr, grturn, turned, turned_other, nlast, ctx],
        [pieces]
        + [((256, WB), BF16)] * 4
        + [((8, HW), F32), ((ROWS * 2, 512), BF16), ((8, HW), F32), ((8, D), F32)],
        [((8, D), BF16), ((8, D), BF16), ((8, 512), BF16), ((4, 256, WB), BF16)],
        flops=1_100_000_000,
    )
    chip_b, (loss, skv, g, sr) = rest[0:4], rest[4:]
    got_a = lax.all_to_all(chip_a, "pb", 0, 0, tiled=True)
    got_b = along_ring(chip_b, "x")
    (grad_hidden,) = call(
        hidden_body,
        [lens_both],
        [tokens, gain, skv, g, last, swap(last), sr, kvo, got],
        [((ROWS, D), BF16)],
        flops=600_000_000,
    )
    got_a, got_b, grad_hidden = lax.optimization_barrier((got_a, got_b, grad_hidden))
    *mid_a, mid_b = call(
        middle_body,
        [at],
        [loss, got_a, *got_b],
        [((64, WA), BF16)] * 4 + [((4, 80, WB), BF16)],
        [((8, 4, 8, WA), F32)],
        grant=52,
    )
    done_a = along_ring(mid_a, "x")
    done_b = lax.all_to_all(mid_b, "pb", 0, 0, tiled=True)
    loss = jnp.sum(done_b[:, 64, 0:3].astype(F32), axis=1)
    loss = (loss[0] + loss[1]) + (loss[2] + loss[3])
    done_b = done_b[:, 0:64]

    def added(parts):
        total = parts[0].astype(F32)
        for part in parts[1:]:
            total = total + part.astype(F32)
        return total.astype(BF16)

    part = jnp.concatenate([added(done_a), added(done_b)], axis=1)
    rec = lax.all_to_all(part.reshape(16, 4, 1536), ("z", "c"), 0, 0, tiled=True)
    grad_query, grad_key, grad_value, grad_out = call(
        finish_body,
        [],
        [rec.reshape(8, 2, 4, 1536)],
        [((4, D), F32), ((4, 512), F32), ((4, 512), F32), ((4, D), F32)],
    )

    return (
        line,
        loss,
        grad_hidden.reshape(hidden.shape),
        grad_query,
        grad_key,
        grad_value,
        grad_out.T,
    )


def solution(mesh):
    torus = Mesh(mesh.devices.reshape(mesh.shape["pb"], 8, 4, 2), AXES)
    placed = (
        P("pb", NEG, None, None),
        P("pb", NEG),
        P("pb", NEG),
        P(),
        P(),
        P(),
        P(AXES, None),
        P(AXES, None),
        P(AXES, None),
        P(None, AXES),
    )
    return jax.shard_map(
        shards,
        mesh=torus,
        in_specs=placed,
        out_specs=(
            P("pb", NEG),
            P(),
            P("pb", NEG, None, None),
            P(AXES, None),
            P(AXES, None),
            P(AXES, None),
            P(None, AXES),
        ),
        check_vma=False,
    )
```

```python
import jax
import jax.numpy as jnp
import numpy as np
from jax import lax
from jax.experimental import pallas as pl
from jax.experimental.pallas import tpu as pltpu
from jax.sharding import Mesh
from jax.sharding import PartitionSpec as P

HW = 128
AXES = ("pb", "z", "x", "c")
NEG = ("z", "x", "c")
EPS = 1e-06
ROPE_BASE = 1000000.0
GRAD_SCALE = 512.0
PAIRS = 4
SEQ = 128
D = 1024
ROWS = PAIRS * SEQ
BOTH = 2 * PAIRS
LOW = 256
WA = 512 + LOW
WB = 1024 - LOW
F32 = jnp.float32
BF16 = jnp.bfloat16
SM = pl.BlockSpec(memory_space=pltpu.SMEM)
LAST = (((1,), (1,)), ((), ()))
FIRST = (((0,), (0,)), ((), ()))
SCALE = HW ** (-0.5)


def rope_consts():
    freqs = np.float32(ROPE_BASE) ** (-(np.arange(HW // 2, dtype=np.float32) * 2.0) / HW)
    angles = np.arange(SEQ, dtype=np.float32)[:, None] * freqs.astype(np.float32)[None, :]
    angles = np.concatenate([angles, angles], axis=1)
    sign = np.where(np.arange(HW) < HW // 2, -1.0, 1.0)
    return (
        np.cos(angles).astype(np.float32),
        (np.sin(angles) * sign[None, :]).astype(np.float32),
    )


def whole(shape):
    return pl.BlockSpec(shape, lambda i: (0,) * len(shape), pipeline_mode=pl.Buffered(1))


def call(body, scalars, arrays, outs, scratch=(), flops=0, grant=52):
    moved = sum(a.size * a.dtype.itemsize for a in arrays)
    moved += sum(int(np.prod(o)) * np.dtype(d).itemsize for o, d in outs)
    return pl.pallas_call(
        body,
        grid=(1,),
        out_shape=[jax.ShapeDtypeStruct(o, d) for o, d in outs],
        in_specs=[SM] * len(scalars) + [whole(a.shape) for a in arrays],
        out_specs=[whole(o) for o, _ in outs],
        scratch_shapes=[pltpu.VMEM(o, d) for o, d in scratch],
        compiler_params=pltpu.CompilerParams(vmem_limit_bytes=grant << 20),
        cost_estimate=pl.CostEstimate(flops=flops, bytes_accessed=moved, transcendentals=0),
    )(*scalars, *arrays)


def block_at(me, step, width):
    return pl.ds(pl.multiple_of(lax.rem(me + step + 4, 4) * width, width), width)


def dot(a, b, dims=(((1,), (0,)), ((), ()))):
    return lax.dot_general(a, b, dims, preferred_element_type=F32)


def half_turn(v):
    return pltpu.roll(v, HW // 2, 1)


def heads(v, n):
    return [v[:, i * HW : (i + 1) * HW] for i in range(n)]


def block_mask():
    row = lax.broadcasted_iota(jnp.int32, (8, 256), 0)
    lane = lax.broadcasted_iota(jnp.int32, (8, 256), 1)
    return (lane // HW) == (row // 2), (row % 2) == 0


def to_blocks(row, mask, even):
    h = heads(row, 4)
    e = jnp.broadcast_to(jnp.concatenate(h[0::2], axis=1), (8, 256))
    o = jnp.broadcast_to(jnp.concatenate(h[1::2], axis=1), (8, 256))
    return jnp.where(mask, jnp.where(even, e, o), 0.0)


def from_blocks(blocks, mask, even):
    e = jnp.sum(jnp.where(mask & even, blocks, 0.0), axis=0, keepdims=True)
    o = jnp.sum(jnp.where(mask & (~even), blocks, 0.0), axis=0, keepdims=True)
    return jnp.concatenate([e[:, 0:HW], o[:, 0:HW], e[:, HW:], o[:, HW:]], axis=1)


def query_tables(len_ref, cos_ref, sin_ref):
    return [
        jnp.concatenate([t[pl.ds(len_ref[p] - 1, 1), :] for p in range(BOTH)], axis=0)
        for t in (cos_ref, sin_ref)
    ]


def pack_body(k_ref, v_ref, q_ref, o_ref, out_ref):
    for h in range(2):
        wide, tall = slice(h * 256, h * 256 + 256), h * 512
        out_ref[0, h, :, 0:256] = k_ref[:, wide]
        out_ref[0, h, :, 256:512] = v_ref[:, wide]
        out_ref[0, h, :, 512:WA] = o_ref[:, tall : tall + LOW]
        out_ref[0, h, :, WA : WA + 512] = q_ref[:, tall : tall + 512]
        out_ref[0, h, :, WA + 512 : 1536] = o_ref[:, tall + LOW : tall + 512]
    for z in range(1, 8):
        out_ref[z] = out_ref[0]


def prep_body(len_ref, h_ref, gain_ref, normed_ref, turned_ref, nlast_ref, xlast_ref):
    row = lax.broadcasted_iota(jnp.int32, (8, SEQ), 0)
    lane = lax.broadcasted_iota(jnp.int32, (8, SEQ), 1)
    nl = jnp.zeros((8, D), F32)
    xl = jnp.zeros((8, D), F32)
    for p in range(PAIRS):
        raw = h_ref[p * SEQ : (p + 1) * SEQ, :]
        x = raw.astype(F32)
        inv = lax.rsqrt(jnp.mean(x * x, axis=-1, keepdims=True) + EPS)
        n = (x * inv * gain_ref[...]).astype(BF16)
        normed_ref[p * SEQ : (p + 1) * SEQ, :] = n
        turned_ref[:, p * SEQ : (p + 1) * SEQ] = n.T
        e = len_ref[p] - 1
        hot = jnp.where((row == p) & (lane == e), 1.0, 0.0).astype(BF16)
        nl = nl + dot(hot, n)
        xl = xl + dot(hot, raw)
    nlast_ref[...] = nl.astype(BF16)
    xlast_ref[...] = xl


def arrange_body(at_ref, *refs):
    a_refs, out_ref, slab_scr = refs[0:4], refs[4], refs[5]
    x = at_ref[1]
    for d in range(4):
        slab_scr[:, pl.ds(lax.rem(x - d + 4, 4), 1)] = a_refs[d][...].reshape(8, 1, 8, WA)
    slab = slab_scr[...].reshape(256, WA)
    for y in range(4):
        out_ref[y] = slab


def attend_body(
    at_ref, len_ref, normed_ref, other_ref, nlast_ref, cos_ref, sin_ref, kv_ref, *refs
):
    out_ref, o_ref, turn_scr, lg_scr = refs[11], refs[12], refs[15], refs[16]
    q_refs = refs[0:4]
    kproj_ref, krot_ref, vcast_ref, qproj_ref, qrot_ref, attn_ref, ctx_ref = refs[4:11]
    qr_scr, ctx_scr = refs[13:15]
    x = at_ref[1]
    mask, even = block_mask()
    lane = lax.broadcasted_iota(jnp.int32, (8 * BOTH, SEQ), 1)
    for side, rows_ref in enumerate((normed_ref, other_ref)):
        here = slice(side * ROWS, (side + 1) * ROWS)
        kv = dot(rows_ref[...], kv_ref[:, 0:512])
        kproj_ref[here, :] = kv[:, 0:256]
        vcast_ref[here, :] = kv[:, 256:512].astype(BF16)

    q = jnp.zeros((8, 512), F32)
    for d in range(4):
        q = q + dot(nlast_ref[:, block_at(x, -d, 256)], q_refs[d][:, 0:512])
    qproj_ref[...] = q
    cos_q, sin_q = query_tables(len_ref, cos_ref, sin_ref)
    for h in range(4):
        q = qproj_ref[:, h * HW : (h + 1) * HW]
        u = q * lax.rsqrt(jnp.mean(q * q, axis=-1, keepdims=True) + EPS)
        r = u * cos_q + half_turn(u) * sin_q
        qr_scr[:, h * HW : (h + 1) * HW] = r
        qrot_ref[:, h * HW : (h + 1) * HW] = r.astype(BF16)
    for p in range(BOTH):
        rows = slice(p * SEQ, (p + 1) * SEQ)
        for g in range(2):
            k = kproj_ref[rows, g * HW : (g + 1) * HW]
            u = k * lax.rsqrt(jnp.mean(k * k, axis=-1, keepdims=True) + EPS)
            r = u * cos_ref[...] + half_turn(u) * sin_ref[...]
            krot_ref[rows, g * HW : (g + 1) * HW] = r.astype(BF16)
    for p in range(BOTH):
        rows = slice(p * SEQ, (p + 1) * SEQ)
        qb = to_blocks(qr_scr[p : p + 1, :], mask, even).astype(BF16)
        lg_scr[p * 8 : (p + 1) * 8, :] = dot(qb, krot_ref[rows, :], LAST)
    last = jnp.concatenate(
        [jnp.full((8, SEQ), len_ref[p] - 1, jnp.int32) for p in range(BOTH)], axis=0
    )
    ex = jnp.where(lane <= last, jnp.exp(lg_scr[...] * SCALE), 0.0)
    w = ex / jnp.sum(ex, axis=-1, keepdims=True)
    attn_ref[...] = w
    probs = w.astype(BF16)
    for p in range(BOTH):
        c = dot(probs[p * 8 : (p + 1) * 8, :], vcast_ref[p * SEQ : (p + 1) * SEQ, :])
        ctx_scr[p : p + 1, :] = from_blocks(c, mask, even)
    ctx_ref[...] = ctx_scr[...].astype(BF16)
    for d in range(4):
        turn_scr[:, pl.ds(lax.rem(x - d + 4, 4), 1)] = q_refs[d][:, 512:WB].reshape(
            32, 1, 8, 512 - LOW
        )
    o_ref[:, 0:LOW] = kv_ref[:, 512:WA]
    o_ref[:, LOW:512] = turn_scr[...].reshape(1024, 512 - LOW)
    out_ref[...] = dot(ctx_ref[...], o_ref[...], LAST)


def score_body(teach_ref, mine_ref, theirs_ref, xlast_ref, fg_ref, sv_ref, *refs):
    unit_ref, oscale_ref, score_ref, tot_ref, line_ref = refs
    res = xlast_ref[...] + (mine_ref[...] + pltpu.roll(theirs_ref[...], PAIRS, 0))
    sc = lax.rsqrt(jnp.mean(res * res, axis=-1, keepdims=True) + EPS)
    unit = res * sc
    unit_ref[...] = unit
    oscale_ref[...] = jnp.broadcast_to(sc, (8, HW))
    s = jnp.sum(unit * fg_ref[...] * sv_ref[...], axis=-1, keepdims=True)
    s = jnp.broadcast_to(s, (8, HW))
    score_ref[...] = s
    row = lax.broadcasted_iota(jnp.int32, (8, HW), 0)
    lane = lax.broadcasted_iota(jnp.int32, (8, HW), 1)
    line_ref[...] = jnp.sum(jnp.where(row == lane, s, 0.0), axis=0, keepdims=True)[:, 0:PAIRS]
    scaled = teach_ref[...] / 2.0
    es = jnp.exp(s)
    et = jnp.exp(scaled)
    v = jnp.where(lane == 0, es, jnp.where(lane == 1, et, et * (scaled - s)))
    v = jnp.where(lane < 3, v + pltpu.roll(v, PAIRS, 0), 0.0)
    tot_ref[...] = jnp.broadcast_to(jnp.sum(v[0:PAIRS], axis=0, keepdims=True)[None], (32, 1, HW))


def unit_back_body(
    at_ref,
    len_ref,
    krot_ref,
    vcast_ref,
    kproj_ref,
    qproj_ref,
    qrot_ref,
    attn_ref,
    unit_ref,
    oscale_ref,
    fg_ref,
    sv_ref,
    cos_ref,
    sin_ref,
    *refs,
):
    o_ref, q_refs, kv_ref = refs[0], refs[1:5], refs[5]
    gkv_ref, gq_ref, gr_ref, last_ref, send_ref, gc_scr, gq_scr, qr_scr, gp_scr = refs[6:]
    mask, even = block_mask()
    unit = unit_ref[...]
    gu = sv_ref[...] * fg_ref[...]
    gr = oscale_ref[:, 0:1] * (gu - unit * jnp.mean(gu * unit, axis=-1, keepdims=True))
    gr_ref[...] = gr
    gc_scr[...] = dot(gr.astype(BF16), o_ref[...])
    qr_scr[...] = qrot_ref[...].astype(F32)
    blocks = []
    for p in range(BOTH):
        rows = slice(p * SEQ, (p + 1) * SEQ)
        gb = to_blocks(gc_scr[p : p + 1, :], mask, even).astype(BF16)
        blocks.append(gb)
        gp_scr[p * 8 : (p + 1) * 8, :] = dot(gb, vcast_ref[rows, :], LAST)
    w = attn_ref[...]
    gp = gp_scr[...]
    spread = jnp.sum(w * gp, axis=-1, keepdims=True)
    dls = (w * (gp - spread)).astype(BF16)
    probs = w.astype(BF16)
    for p in range(BOTH):
        rows = slice(p * SEQ, (p + 1) * SEQ)
        eight = slice(p * 8, (p + 1) * 8)
        qb = to_blocks(qr_scr[p : p + 1, :], mask, even).astype(BF16)
        gkv_ref[rows, 256:512] = dot(probs[eight, :], blocks[p], FIRST)
        dl = dls[eight, :]
        gq_scr[p : p + 1, :] = from_blocks(dot(dl, krot_ref[rows, :]) * SCALE, mask, even)
        gk = dot(dl, qb, FIRST) * SCALE
        for g in range(2):
            cols = slice(g * HW, (g + 1) * HW)
            k = kproj_ref[rows, cols]
            sc = lax.rsqrt(jnp.mean(k * k, axis=-1, keepdims=True) + EPS)
            u = k * sc
            r = gk[:, cols]
            t = r * cos_ref[...] + half_turn(r * sin_ref[...])
            gkv_ref[rows, cols] = sc * (t - u * jnp.mean(t * u, axis=-1, keepdims=True))
    cos_q, sin_q = query_tables(len_ref, cos_ref, sin_ref)
    for h in range(4):
        q = qproj_ref[:, h * HW : (h + 1) * HW]
        sc = lax.rsqrt(jnp.mean(q * q, axis=-1, keepdims=True) + EPS)
        u = q * sc
        r = gq_scr[:, h * HW : (h + 1) * HW]
        t = r * cos_q + half_turn(r * sin_q)
        gq_ref[:, h * HW : (h + 1) * HW] = sc * (
            t - u * jnp.mean(t * u, axis=-1, keepdims=True)
        )
    gqb = gq_ref[...].astype(BF16)
    for d in range(4):
        last_ref[:, block_at(at_ref[1], -d, 256)] = dot(gqb, q_refs[d][:, 0:512], LAST)

    gn = dot(gkv_ref[ROWS : 2 * ROWS, :].astype(BF16), kv_ref[:, 0:512], LAST)
    send_ref[...] = gn.astype(BF16)


def weight_body(
    at_ref,
    tot_ref,
    score_ref,
    teach_ref,
    gkv_ref,
    gq_ref,
    gr_ref,
    grturn_ref,
    turned_ref,
    turned_other_ref,
    nlast_ref,
    ctx_ref,
    *refs,
):
    out_a, outs_b, loss_ref, skv_ref, g_ref, sr_ref = refs[0], refs[1:5], *refs[5:9]
    srow_scr, sturn_scr, sq_scr, b_scr = refs[9:]
    x = at_ref[1]
    lane = lax.broadcasted_iota(jnp.int32, (1, HW), 1)

    def pick(v, i):
        return jnp.sum(jnp.where(lane == i, v, 0.0), axis=-1, keepdims=True)

    t = tot_ref[0]
    for i in range(1, 32):
        t = t + tot_ref[i]
    ts, tt, cr = pick(t, 0), pick(t, 1), pick(t, 2)
    loss_ref[...] = jnp.broadcast_to(cr / tt - jnp.log(tt) + jnp.log(ts), (8, HW))
    row = lax.broadcasted_iota(jnp.int32, (8, HW), 0)
    g = GRAD_SCALE * (jnp.exp(score_ref[...]) / ts - jnp.exp(teach_ref[...] / 2.0) / tt)
    gcol = g[:, 0:1]
    sr = gr_ref[...] * gcol
    sr_ref[...] = sr
    g_ref[...] = g
    sq_scr[...] = (gq_ref[...] * gcol).astype(BF16)
    srow_scr[...] = sr.astype(BF16)
    sturn_scr[...] = (grturn_ref[...] * gcol).astype(BF16)
    for p in range(BOTH):
        rows = slice(p * SEQ, (p + 1) * SEQ)
        skv_ref[rows, :] = (gkv_ref[rows, :] * gcol[p : p + 1, :]).astype(BF16)

    kv = dot(turned_ref[...], skv_ref[0:ROWS, :]) + dot(
        turned_other_ref[...], skv_ref[ROWS : 2 * ROWS, :]
    )
    out_a[:, :, 0:512] = kv.astype(BF16).reshape(4, 256, 512)
    o_low = dot(srow_scr[...], ctx_ref[:, 0:LOW], FIRST)
    out_a[:, :, 512:WA] = o_low.astype(BF16).reshape(4, 256, LOW)
    q = dot(nlast_ref[...], sq_scr[...], FIRST)
    b_scr[:, :, 0:512] = q.astype(BF16).reshape(4, 256, 512)
    o_high = dot(sturn_scr[...], ctx_ref[:, LOW:512], FIRST)
    b_scr[:, :, 512:WB] = o_high.astype(BF16).reshape(4, 256, 512 - LOW)
    for d in range(4):
        outs_b[d][...] = b_scr[lax.rem(x + d, 4)]


def middle_a_body(at_ref, got_a_ref, *refs):
    outs, a_scr = refs[0:4], refs[4]
    total = got_a_ref[0].astype(F32)
    for d in range(1, 4):
        total = total + got_a_ref[d].astype(F32)
    a_scr[...] = total.reshape(8, 4, 8, WA)
    for d in range(4):
        outs[d][...] = (
            a_scr[:, pl.ds(lax.rem(at_ref[1] + d, 4), 1)].reshape(64, WA).astype(BF16)
        )


def middle_b_body(loss_ref, *refs):
    b_refs, out_b = refs[0:4], refs[4]
    total = b_refs[0][...].astype(F32)
    for d in range(1, 4):
        total = total + b_refs[d][...].astype(F32)
    out_b[:, 0:64, :] = total.reshape(4, 64, WB).astype(BF16)
    rest = jnp.broadcast_to(loss_ref[0:1, 0:1], (16, WB))
    lane = lax.broadcasted_iota(jnp.int32, (16, WB), 1)
    parts = jnp.zeros((16, WB), F32)
    for i in range(3):
        part = rest.astype(BF16).astype(F32)
        parts = jnp.where(lane == i, part, parts)
        rest = rest - part
    for y in range(4):
        out_b[y, 64:80, :] = parts.astype(BF16)


def hidden_body(len_ref, h_ref, gain_ref, skv_ref, g_ref, last_ref, other_ref, sr_ref, kv_ref, got_ref, out_ref):
    pos = lax.broadcasted_iota(jnp.int32, (SEQ, 1), 0)

    @pl.loop(0, PAIRS)
    def _(p):
        rows = pl.ds(pl.multiple_of(p * SEQ, SEQ), SEQ)
        at = pos == len_ref[p] - 1
        last = last_ref[pl.ds(p, 1), :] + other_ref[pl.ds(PAIRS + p, 1), :]
        unit = got_ref[rows, :].astype(F32) + jnp.where(at, last, 0.0)
        gn = dot(skv_ref[rows, :], kv_ref[:, 0:512], LAST) + g_ref[pl.ds(p, 1), 0:1] * unit
        x = h_ref[rows, :].astype(F32)
        inv = lax.rsqrt(jnp.mean(x * x, axis=-1, keepdims=True) + EPS)
        s = gn * gain_ref[...]
        gi = inv * s - x * (inv * inv * inv * jnp.mean(s * x, axis=-1, keepdims=True))
        gi = gi + jnp.where(at, sr_ref[pl.ds(p, 1), :], 0.0)
        out_ref[rows, :] = gi.astype(BF16)


def finish_body(rec_ref, gq_ref, gk_ref, gv_ref, go_ref):
    for h in range(2):
        total = rec_ref[0, h].astype(F32)
        for z in range(1, 8):
            total = total + rec_ref[z, h].astype(F32)
        gk_ref[:, h * 256 : h * 256 + 256] = total[:, 0:256]
        gv_ref[:, h * 256 : h * 256 + 256] = total[:, 256:512]
        go_ref[:, h * 512 : h * 512 + LOW] = total[:, 512:WA]
        gq_ref[:, h * 512 : h * 512 + 512] = total[:, WA : WA + 512]
        go_ref[:, h * 512 + LOW : h * 512 + 512] = total[:, WA + 512 : 1536]


def everyone(x, axes, count):
    return lax.all_to_all(
        jnp.broadcast_to(x[None], (count, *x.shape)), axes, 0, 0, tiled=True
    )


def from_ring(x, axis):
    return [x] + [
        lax.ppermute(x, axis, [(i, (i + d) % 4) for i in range(4)]) for d in range(1, 4)
    ]


def along_ring(pieces, axis):
    return [pieces[0]] + [
        lax.ppermute(pieces[d], axis, [(i, (i + d) % 4) for i in range(4)]) for d in range(1, 4)
    ]


def chunk_turn(v):
    return jnp.transpose(v.reshape(8, 32, 4, 8), (0, 2, 1, 3)).reshape(8, D)


def chunk_back(v):
    return jnp.transpose(v.reshape(8, 4, 32, 8), (0, 2, 1, 3)).reshape(8, D)


def swap(x):
    return lax.ppermute(x, "c", [(0, 1), (1, 0)])


def shards(
    hidden,
    lengths,
    teacher,
    norm_gain,
    final_gain,
    score_vector,
    query_weight,
    key_matrix,
    value_matrix,
    out_weight,
):
    at = jnp.stack([lax.axis_index("pb"), lax.axis_index("x")]).astype(jnp.int32)
    tokens = hidden.reshape(ROWS, D)
    lens = lengths[0]
    gain = norm_gain[None]
    fg = final_gain[None]
    sv = score_vector[None]
    cos_np, sin_np = rope_consts()
    cos, sin = jnp.asarray(cos_np), jnp.asarray(sin_np)
    (both_halves,) = call(
        pack_body,
        [],
        [key_matrix, value_matrix, query_weight, out_weight.T],
        [((8, 2, 4, 1536), BF16)],
        grant=62,
    )
    both_halves = both_halves.reshape(16, 4, 1536)
    column = lax.all_to_all(both_halves, ("z", "c"), 0, 0, tiled=True).reshape(64, 1536)
    normed, turned, nlast, xlast = call(
        prep_body,
        [lens],
        [tokens, gain],
        [((ROWS, D), BF16), ((D, ROWS), BF16), ((8, D), BF16), ((8, D), F32)],
        flops=10_000_000,
    )
    nlast = chunk_turn(nlast)
    wide = (PAIRS, HW)
    pack = jnp.concatenate(
        [
            xlast[0:PAIRS],
            nlast[0:PAIRS].astype(F32),
            jnp.broadcast_to(lens.astype(F32)[:, None], wide),
            jnp.broadcast_to(teacher[0][:, None], wide),
        ],
        axis=1,
    )
    column, normed, turned, pack = lax.optimization_barrier((column, normed, turned, pack))
    other = swap(normed)
    got = swap(pack)
    slab_b = everyone(column[:, WA:1536], "pb", 4).reshape(256, WB)
    ring_a = from_ring(column[:, 0:WA], "x")
    (slab_a,) = call(arrange_body, [at], ring_a, [((4, 256, WA), BF16)], [((8, 4, 8, WA), BF16)], grant=10)
    slab_a, slab_b, got = lax.optimization_barrier((slab_a, slab_b, got))
    packed = jnp.concatenate([pack, got], axis=0)
    xlast = packed[:, 0:1024]
    nlast = packed[:, 1024:2048].astype(BF16)
    lens_both = packed[:, 2048].astype(jnp.int32)
    teach = packed[:, 2048 + HW :]
    kvo = lax.all_to_all(slab_a, "pb", 0, 0, tiled=True).reshape(1024, WA)
    qo = from_ring(slab_b, "x")

    kproj, krot, vcast, qproj, qrot, attn, ctx, attended, oa = call(
        attend_body,
        [at, lens_both],
        [normed, other, nlast, cos, sin, kvo, *qo],
        [
            ((2 * ROWS, 256), F32),
            ((2 * ROWS, 256), BF16),
            ((2 * ROWS, 256), BF16),
            ((8, 512), F32),
            ((8, 512), BF16),
            ((64, SEQ), F32),
            ((8, 512), BF16),
            ((8, D), F32),
            ((D, 512), BF16),
        ],
        [((8, 512), F32), ((8, 512), F32), ((32, 4, 8, 512 - LOW), BF16), ((8 * BOTH, SEQ), F32)],
        flops=1_100_000_000,
    )
    ctx, turned_late = lax.optimization_barrier((ctx, turned))
    turned_other = swap(turned_late)
    unit, oscale, score, tot, line = call(
        score_body,
        [],
        [teach, attended, swap(attended), xlast, fg, sv],
        [((8, D), F32), ((8, HW), F32), ((8, HW), F32), ((32, 1, HW), F32), ((1, PAIRS), F32)],
        flops=1_000_000,
    )

    totals = lax.all_to_all(tot, ("z", "x"), 0, 0, tiled=True)

    gkv, gq, gr, last, send = call(
        unit_back_body,
        [at, lens_both],
        [krot, vcast, kproj, qproj, qrot, attn, unit, oscale, fg, sv, cos, sin, oa, *qo, kvo],
        [((2 * ROWS, 512), F32), ((8, 512), F32), ((8, D), F32), ((8, D), F32), ((ROWS, D), BF16)],
        [((8, 512), F32), ((8, 512), F32), ((8, 512), F32), ((8 * BOTH, SEQ), F32)],
        flops=200_000_000,
    )
    grturn = chunk_turn(gr)
    last = chunk_back(last)
    got = swap(send)

    pieces = ((4, 256, WA), BF16)
    chip_a, *rest = call(
        weight_body,
        [at],
        [totals, score, teach, gkv, gq, gr, grturn, turned, turned_other, nlast, ctx],
        [pieces]
        + [((256, WB), BF16)] * 4
        + [((8, HW), F32), ((ROWS * 2, 512), BF16), ((8, HW), F32), ((8, D), F32)],
        [((8, D), BF16), ((8, D), BF16), ((8, 512), BF16), ((4, 256, WB), BF16)],
        flops=1_100_000_000,
    )
    chip_b, (loss, skv, g, sr) = rest[0:4], rest[4:]
    got_a = lax.all_to_all(chip_a, "pb", 0, 0, tiled=True)
    got_b = along_ring(chip_b, "x")
    (grad_hidden,) = call(
        hidden_body,
        [lens_both],
        [tokens, gain, skv, g, last, swap(last), sr, kvo, got],
        [((ROWS, D), BF16)],
        flops=600_000_000,
    )
    got_a, grad_hidden = lax.optimization_barrier((got_a, grad_hidden))
    mid_a = call(
        middle_a_body,
        [at],
        [got_a],
        [((64, WA), BF16)] * 4,
        [((8, 4, 8, WA), F32)],
        grant=62,
    )
    got_b, _ = lax.optimization_barrier((got_b, mid_a[0]))
    (mid_b,) = call(middle_b_body, [], [loss, *got_b], [((4, 80, WB), BF16)])
    done_a = along_ring(mid_a, "x")
    done_b = lax.all_to_all(mid_b, "pb", 0, 0, tiled=True)
    loss = jnp.sum(done_b[:, 64, 0:3].astype(F32), axis=1)
    loss = (loss[0] + loss[1]) + (loss[2] + loss[3])
    done_b = done_b[:, 0:64]

    def added(parts):
        total = parts[0].astype(F32)
        for part in parts[1:]:
            total = total + part.astype(F32)
        return total.astype(BF16)

    part = jnp.concatenate([added(done_a), added(done_b)], axis=1)
    rec = lax.all_to_all(part.reshape(16, 4, 1536), ("z", "c"), 0, 0, tiled=True)
    grad_query, grad_key, grad_value, grad_out = call(
        finish_body,
        [],
        [rec.reshape(8, 2, 4, 1536)],
        [((4, D), F32), ((4, 512), F32), ((4, 512), F32), ((4, D), F32)],
    )

    return (
        line,
        loss,
        grad_hidden.reshape(hidden.shape),
        grad_query,
        grad_key,
        grad_value,
        grad_out.T,
    )


def solution(mesh):
    torus = Mesh(mesh.devices.reshape(mesh.shape["pb"], 8, 4, 2), AXES)
    placed = (
        P("pb", NEG, None, None),
        P("pb", NEG),
        P("pb", NEG),
        P(),
        P(),
        P(),
        P(AXES, None),
        P(AXES, None),
        P(AXES, None),
        P(None, AXES),
    )
    return jax.shard_map(
        shards,
        mesh=torus,
        in_specs=placed,
        out_specs=(
            P("pb", NEG),
            P(),
            P("pb", NEG, None, None),
            P(AXES, None),
            P(AXES, None),
            P(AXES, None),
            P(None, AXES),
        ),
        check_vma=False,
    )
```
